32 devices in a mesh: outer: 4 (over z), dev: 8 (over y, x, core).
Axes of the slice: x: 2, y: 2, z: 4, core: 2. Of those that a mesh axis runs over, the one named last changes fastest.
Arguments:
- partials: bfloat16 [32, 8192, 128], P(('outer', 'dev')), may hold values from -6 to 6
- p_old: bfloat16 [8192, 1024], P('dev'), may hold values from -0.0625 to 0.0625
- p_new: bfloat16 [8192, 1024], P('dev'), may hold values from -0.0625 to 0.0625
- weight: float32 [8192, 128], P('dev'), may hold values from -4 to 4
- m_old: float32 [1024, 128], P('dev'), may hold values from -96 to 96
- v_old: float32 [1024, 128], P('dev'), may hold values from 32 to 1280
Outputs:
- new_weight: float32 [8192, 128], P('dev')
- m_new: float32 [1024, 128], P('dev')
- v_new: float32 [1024, 128], P('dev')
The draws below stay inside these ranges and needn't reach their ends.
All inputs are finite; a program needn't handle non-finite values.
Results may differ from the reference program's by a relative error of at most 0.0012.
Values may be sent and summed in bfloat16 or wider, within the bound.
A program may use at most 128 MiB of HBM per device.

```python
import math
import jax
import jax.numpy as jnp
from jax import lax

D = 8192
R = 1024
COLS = 128
DEVICES = 32


def levels(own_key, extent, shards, smallest, top_value):
    gain, own = 1.0, jax.random.fold_in(own_key, 6)
    for axis_at, shards_of in shards:
        heights = jnp.exp(jax.random.uniform(jax.random.fold_in(own, axis_at), (shards_of,), jnp.float32, smallest / len(shards), top_value / len(shards)))
        gain = gain * jnp.repeat(heights, extent[axis_at] // shards_of).reshape([-1 if axis == axis_at else 1 for axis in range(len(extent))])
    return gain


def centred(own_key, dims, deviation, limit, split=(), held_as=jnp.bfloat16):
    values = deviation * jax.random.normal(own_key, dims, jnp.float32)
    if split:
        values = values * levels(own_key, dims, split, -0.22, 0.18)
    return jnp.clip(values, -limit, limit).astype(held_as)


def setup_inputs(seed: int = 0) -> dict:
    streams_of = jax.random.split(jax.random.key(seed), 7)
    return {
        "partials": centred(streams_of[0], (DEVICES, D, COLS), 1.0, 6.0, ((0, 32),)),
        "p_old": centred(streams_of[1], (D, R), D ** -0.5, 0.0625, ((0, 8),)),
        "p_new": centred(streams_of[2], (D, R), D ** -0.5, 0.0625, ((0, 8),)),
        "weight": centred(streams_of[3], (D, COLS), 0.3, 4.0, ((0, 8),), jnp.float32),
        "m_old": centred(streams_of[4], (R, COLS), 16.0, 96.0, ((0, 8),), jnp.float32),
        "v_old": jnp.clip(jnp.exp(math.log(1280.0) - 3.6888795 * jax.random.uniform(streams_of[5], (R, COLS), jnp.float32) ** levels(streams_of[5], (R, COLS), ((0, 8),), -0.2, 0.2)), 32.0, 1280.0),
    }


beta_mean = 0.9
beta_square = 0.95
bias_mean = 0.9999734386011124
bias_square = 0.9940794707796659
adam_epsilon = 1e-08
step_scale = 0.5

def reference(partials, p_old, p_new, weight, m_old, v_old):

    def accumulate(total, piece):
        return (total + piece.astype(jnp.float32), None)
    grad, _ = lax.scan(accumulate, jnp.zeros((D, COLS), jnp.float32), partials)
    projected = jnp.dot(p_new.astype(jnp.float32).T, grad, precision=lax.Precision.HIGHEST)
    margin = jnp.dot(p_new.T, p_old, preferred_element_type=jnp.float32)
    m_rot = jnp.dot(margin, m_old, precision=lax.Precision.HIGHEST)
    v_rot = jnp.dot(margin * margin, v_old, precision=lax.Precision.HIGHEST)
    m_new = beta_mean * m_rot + (1.0 - beta_mean) * projected
    v_new = beta_square * v_rot + (1.0 - beta_square) * projected * projected
    direction = (m_new / bias_mean / (jnp.sqrt(v_new / bias_square) + adam_epsilon)).astype(jnp.bfloat16)
    update = jnp.dot(p_new, direction, preferred_element_type=jnp.float32)
    new_weight = weight - step_scale * update
    return (new_weight, m_new, v_new)
```

```python
import functools

import jax
import jax.numpy as jnp
from jax import lax
from jax.experimental import pallas as pl
from jax.experimental.pallas import tpu as pltpu
from jax.sharding import PartitionSpec as P

beta_mean = 0.9
beta_square = 0.95
bias_mean = 0.9999734386011124
bias_square = 0.9940794707796659
adam_epsilon = 1e-08
step_scale = 0.5

chunks = 2
early = 1
parts = 2
pieces = 2
vmem_limit = 67043328
finish_limit = 67043328

MESH = pl.DeviceIdType.MESH
F32 = jnp.float32
BF16 = jnp.bfloat16


def contract_rows(a, b):
    return lax.dot_general(a, b, (((0,), (0,)), ((), ())), preferred_element_type=F32)


def kernel(
    n_outer,
    n_dev,
    partials,
    p_old,
    p_new,
    weight,
    m_old,
    v_old,
    new_weight,
    m_new,
    v_new,
    grads,
    basis,
    basis_old,
    weights,
    moments,
    margin,
    margin_partner,
    margin_sum,
    margin_in,
    rotated,
    rotated_in,
    projected,
    projected_partner,
    projected_sum,
    projected_in,
    block,
    block_in,
    direction,
    load_sem,
    old_sem,
    grad_send,
    grad_recv,
    mom_send,
    mom_recv,
    fwd_send,
    fwd_recv,
    mp_send,
    mp_recv,
    ms_send,
    ms_recv,
    rot_send,
    rot_recv,
    pp_send,
    pp_recv,
    ps_send,
    ps_recv,
    blk_send,
    blk_recv,
    dir_send,
    dir_recv,
):
    z = lax.axis_index("outer")
    d = lax.axis_index("dev")
    n_chip = n_dev // 2
    q = d // 2
    c = d % 2
    partner = q * 2 + 1 - c
    rows, cols = weight.shape
    rank = p_new.shape[1]
    blk = rank // n_dev
    per = n_dev // n_outer

    def remote(src, dst, send, recv, where):
        return pltpu.make_async_remote_copy(
            src_ref=src, dst_ref=dst, send_sem=send, recv_sem=recv, device_id=where, device_id_type=MESH
        )

    barrier = pltpu.get_barrier_semaphore()
    for j in range(1, n_dev):
        pl.semaphore_signal(barrier, inc=1, device_id=(z, lax.rem(d + j, n_dev)), device_id_type=MESH)
    for j in range(1, n_outer):
        pl.semaphore_signal(barrier, inc=1, device_id=(lax.rem(z + j, n_outer), d), device_id_type=MESH)

    load_new = pltpu.make_async_copy(p_new, basis, load_sem.at[0])
    load_new.start()
    if p_old.shape[1] == per * blk:
        old_loads = [pltpu.make_async_copy(p_old, basis_old, old_sem.at[0])]
    else:
        old_loads = [
            pltpu.make_async_copy(
                p_old.at[:, pl.ds(pl.multiple_of((k * n_outer + z) * blk, blk), blk)],
                basis_old.at[:, k * blk : (k + 1) * blk],
                old_sem.at[k],
            )
            for k in range(per)
        ]
    for load in old_loads:
        load.start()
    load_weight = pltpu.make_async_copy(weight, weights, load_sem.at[2])
    load_weight.start()
    load_own = pltpu.make_async_copy(
        partials.at[pl.ds(pl.multiple_of(d * rows, rows), rows)], grads.at[0], load_sem.at[3]
    )
    load_own.start()

    pl.semaphore_wait(barrier, n_dev - 1 + n_outer - 1)

    def moment_copies(k, owner):
        copies = []
        for j in range(1, n_chip):
            to = (z, lax.rem(q + j, n_chip) * 2 + c)
            for i, src in enumerate((m_old, v_old)):
                copies.append(remote(src, moments.at[i, k], mom_send.at[i, k, j], mom_recv.at[i, k], to))
        return copies

    for k in range(per):
        owner = k * n_outer + z

        @pl.when(d == owner)
        def _():
            for copy in moment_copies(k, owner):
                copy.start()
            for i, src in enumerate((m_old, v_old)):
                pltpu.make_async_copy(src, moments.at[i, k], load_sem.at[4 + i]).start()

    tall = rows // chunks

    def send_gradients(chunk):
        copies = []
        for j in range(1, n_dev):
            to = lax.rem(d + j, n_dev)
            copy = remote(
                partials.at[pl.ds(pl.multiple_of(to * rows + chunk * tall, tall), tall)],
                grads.at[j, chunk * tall : (chunk + 1) * tall],
                grad_send.at[chunk, j],
                grad_recv.at[chunk, j],
                (z, to),
            )
            copy.start()
            copies.append(copy)
        return copies

    grad_copies = [send_gradients(chunk) for chunk in range(early)]

    load_new.wait()
    for load in old_loads:
        load.wait()
    width = min(rank, 256)
    for s in range(0, rank, width):
        part = contract_rows(basis[:, s : s + width], basis_old[...])
        margin[s // blk : (s + width) // blk] = part.reshape(width // blk, blk, part.shape[1])

    def scatter_start(val, prt, send, recv):
        copies = []
        for j in list(range(1, n_chip)) + [0]:
            k = lax.rem(q + j, n_chip)
            copy = remote(val.at[2 * k + 1 - c], prt.at[j], send.at[j], recv.at[j], (z, partner))
            copy.start()
            copies.append((j, k, copy))
        return copies

    def scatter_middle(pairs, val, prt, tot, arr, send, recv):
        copies = []
        for j, k, pair in pairs:
            pair.wait_recv()
            tot[j] = val[2 * k + c] + prt[j]
            if j:
                copy = remote(tot.at[j], arr.at[j], send.at[j], recv.at[j], (z, 2 * k + c))
                copy.start()
                copies.append((j, copy))
        return copies

    def scatter_end(copies, tot, arr):
        total = tot[0]
        for j, copy in copies:
            copy.wait_recv()
            total = total + arr[j]
        return total

    margin_pairs = scatter_start(margin, margin_partner, mp_send, mp_recv)

    for k in range(per):
        owner = k * n_outer + z
        mine = c == owner % 2

        @pl.when(d == owner)
        def _():
            for i, src in enumerate((m_old, v_old)):
                pltpu.make_async_copy(src, moments.at[i, k], load_sem.at[4 + i]).wait()

        @pl.when(jnp.logical_and(mine, d != owner))
        def _():
            for i, src in enumerate((m_old, v_old)):
                remote(src, moments.at[i, k], mom_send.at[i, k, 0], mom_recv.at[i, k], (z, d)).wait_recv()

        @pl.when(mine)
        def _():
            for i in range(2):
                remote(
                    moments.at[i, k], moments.at[i, k], fwd_send.at[i, k], fwd_recv.at[i, k], (z, partner)
                ).start()

    margin_copies = scatter_middle(
        margin_pairs, margin, margin_partner, margin_sum, margin_in, ms_send, ms_recv
    )

    for chunk in range(early, chunks):
        grad_copies.append(send_gradients(chunk))

    for k in range(per):
        mine = c == (k * n_outer + z) % 2

        @pl.when(jnp.logical_not(mine))
        def _():
            for i in range(2):
                remote(
                    moments.at[i, k], moments.at[i, k], fwd_send.at[i, k], fwd_recv.at[i, k], (z, partner)
                ).wait_recv()

    margin_rows = scatter_end(margin_copies, margin_sum, margin_in)
    old = moments[...].reshape(2, per * blk, cols)
    rotated[0] = jnp.dot(margin_rows, old[0], precision=lax.Precision.HIGHEST, preferred_element_type=F32)
    rotated[1] = jnp.dot(
        margin_rows * margin_rows, old[1], precision=lax.Precision.HIGHEST, preferred_element_type=F32
    )
    rot_copies = []
    for j in range(1, n_outer):
        copy = remote(
            rotated, rotated_in.at[j], rot_send.at[j], rot_recv.at[j], (lax.rem(z + j, n_outer), d)
        )
        copy.start()
        rot_copies.append(copy)

    load_own.wait()
    for chunk in range(chunks):
        for copy in grad_copies[chunk]:
            copy.wait_recv()
        part_rows = slice(chunk * tall, (chunk + 1) * tall)
        total = grads[0, part_rows].astype(F32)
        for j in range(1, n_dev):
            total = total + grads[j, part_rows].astype(F32)
        high = total.astype(BF16)
        low = (total - high.astype(F32)).astype(BF16)
        both = jnp.concatenate([high, low], axis=1)
        for s in range(0, rank, width):
            part = contract_rows(basis[part_rows, s : s + width], both)
            part = (part[:, :cols] + part[:, cols:]).reshape(width // blk, blk, cols)
            blocks = slice(s // blk, (s + width) // blk)
            projected[blocks] = part if chunk == 0 else projected[blocks] + part
    half = blk // parts
    views = [slice(h * half, (h + 1) * half) for h in range(parts)]
    pairs = [
        scatter_start(projected.at[:, v], projected_partner.at[:, v], pp_send.at[h], pp_recv.at[h])
        for h, v in enumerate(views)
    ]
    copies = [
        scatter_middle(
            pairs[h],
            projected.at[:, v],
            projected_partner.at[:, v],
            projected_sum.at[:, v],
            projected_in.at[:, v],
            ps_send.at[h],
            ps_recv.at[h],
        )
        for h, v in enumerate(views)
    ]
    blk_copies = []
    for h, v in enumerate(views):
        block[v] = scatter_end(copies[h], projected_sum.at[:, v], projected_in.at[:, v])
        for j in range(1, n_outer):
            copy = remote(
                block.at[v],
                block_in.at[j, v],
                blk_send.at[h, j],
                blk_recv.at[h, j],
                (lax.rem(z + j, n_outer), d),
            )
            copy.start()
            blk_copies.append(copy)
    for copy in rot_copies:
        copy.wait_recv()
    dir_copies = []
    for h, v in enumerate(views):
        for copy in blk_copies[h * (n_outer - 1) : (h + 1) * (n_outer - 1)]:
            copy.wait_recv()
        first = rotated[0, v]
        second = rotated[1, v]
        proj = block[v]
        for j in range(1, n_outer):
            first = first + rotated_in[j, 0, v]
            second = second + rotated_in[j, 1, v]
            proj = proj + block_in[j, v]
        mean = beta_mean * first + (1.0 - beta_mean) * proj
        square = beta_square * second + (1.0 - beta_square) * proj * proj
        m_new[v] = mean
        v_new[v] = square
        direction[d, v] = (mean / bias_mean / (jnp.sqrt(square / bias_square) + adam_epsilon)).astype(BF16)
        for j in range(1, n_dev):
            copy = remote(
                direction.at[d, v],
                direction.at[d, v],
                dir_send.at[h, j],
                dir_recv.at[h, j],
                (z, lax.rem(d + j, n_dev)),
            )
            copy.start()
            dir_copies.append(copy)
    load_weight.wait()
    for copy in dir_copies:
        copy.wait_recv()
    directions = direction[...].reshape(rank, cols)
    tall = min(rows, 256)
    for s in range(0, rows, tall):
        update = jnp.dot(basis[s : s + tall, :], directions, preferred_element_type=F32)
        new_weight[s : s + tall, :] = weights[s : s + tall, :] - step_scale * update

    for k in range(per):
        owner = k * n_outer + z
        mine = c == owner % 2

        @pl.when(d == owner)
        def _():
            for copy in moment_copies(k, owner):
                copy.wait_send()

        @pl.when(mine)
        def _():
            for i in range(2):
                remote(
                    moments.at[i, k], moments.at[i, k], fwd_send.at[i, k], fwd_recv.at[i, k], (z, partner)
                ).wait_send()

    for copy in sum(grad_copies, []) + rot_copies + blk_copies + dir_copies:
        copy.wait_send()
    for group in [margin_pairs] + pairs:
        for _, _, copy in group:
            copy.wait_send()
    for group in [margin_copies] + copies:
        for _, copy in group:
            copy.wait_send()

class Copies:
    def __init__(self, send, recv):
        self.send, self.recv, self.started = send, recv, []

    def start(self, src, dst, to):
        i = len(self.started)
        copy = pltpu.make_async_remote_copy(
            src_ref=src,
            dst_ref=dst,
            send_sem=self.send.at[i],
            recv_sem=self.recv.at[i],
            device_id=to,
            device_id_type=MESH,
        )
        copy.start()
        self.started.append(copy)
        return copy


def square_kernel(
    n_outer,
    n_dev,
    partials,
    p_old,
    p_new,
    weight,
    m_old,
    v_old,
    new_weight,
    m_new,
    v_new,
    own,
    pair,
    far_sum,
    relay_in,
    direct_out,
    direct_in,
    merged,
    merged_in,
    terms,
    basis,
    basis_old,
    weights,
    moments,
    margin,
    margin_partner,
    margin_sum,
    margin_in,
    rotated,
    rotated_in,
    projected,
    projected_partner,
    projected_sum,
    projected_in,
    block,
    block_in,
    direction,
    moments_new,
    load_sem,
    old_sem,
    own_sem,
    mom_send,
    mom_recv,
    fwd_send,
    fwd_recv,
    send_sem,
    recv_sem,
    line_sem,
):
    z = lax.axis_index("outer")
    d = lax.axis_index("dev")
    q = d // 2
    c = d % 2
    partner = q * 2 + 1 - c
    side = q + 1 - 2 * (q % 2)
    over = lax.rem(q + 2, 4)
    far = lax.rem(side + 2, 4)
    chips = (far, side, over, q)
    rows, cols = weight.shape
    rank = p_new.shape[1]
    blk = rank // n_dev
    sub = blk // n_outer
    fine = sub // pieces
    per = n_dev // n_outer
    half = rows // 2
    copies = Copies(send_sem, recv_sem)
    above = (2 * n_outer - 2 - z) // n_outer
    below = (z + n_outer - 1) // n_outer

    def signal_line(sem):
        @pl.when(z > 0)
        def _():
            pl.semaphore_signal(sem, inc=1, device_id=(z - 1, d), device_id_type=MESH)

        @pl.when(z < n_outer - 1)
        def _():
            pl.semaphore_signal(sem, inc=1, device_id=(z + 1, d), device_id_type=MESH)

    def pass_along(steps):
        for r in steps:
            pl.semaphore_wait(line_sem.at[r], above + below)
            if r + 1 < n_outer - 2:
                signal_line(line_sem.at[r + 1])

    barrier = pltpu.get_barrier_semaphore()
    for to in (partner, 2 * side + c, 2 * over + c):
        pl.semaphore_signal(barrier, inc=1, device_id=(z, to), device_id_type=MESH)
    signal_line(barrier)

    def rows_of(to):
        return partials.at[pl.ds(pl.multiple_of(to * rows, rows), rows)]

    own_loads = [
        pltpu.make_async_copy(rows_of(2 * k + c), own.at[i], own_sem.at[i]) for i, k in enumerate(chips)
    ]
    for load in own_loads[:3]:
        load.start()
    load_new = pltpu.make_async_copy(p_new, basis, load_sem.at[0])
    load_new.start()
    old_loads = [
        pltpu.make_async_copy(
            p_old.at[:, pl.ds(pl.multiple_of((k * n_outer + z) * blk, blk), blk)],
            basis_old.at[:, k * blk : (k + 1) * blk],
            old_sem.at[k],
        )
        for k in range(per)
    ]
    for load in old_loads:
        load.start()
    own_loads[3].start()
    load_weight = pltpu.make_async_copy(weight, weights, load_sem.at[1])
    load_weight.start()

    pl.semaphore_wait(barrier, 3 + above + below)

    pairs = [copies.start(rows_of(2 * k + 1 - c), pair.at[i], (z, partner)) for i, k in enumerate(chips)]
    if n_outer > 2:
        signal_line(line_sem.at[0])

    def chip_sum(i, at):
        return own[i, at].astype(F32) + pair[i, at].astype(F32)

    pairs[0].wait_recv()
    own_loads[0].wait()
    relays = []
    for h, chip in enumerate((side, over)):
        at = slice(h * half, (h + 1) * half)
        far_sum[at] = chip_sum(0, at).astype(BF16)
        relays.append(copies.start(far_sum.at[at], relay_in.at[h], (z, 2 * chip + c)))
    directs = []
    for h, chip in enumerate((side, over)):
        pairs[1 + h].wait_recv()
        own_loads[1 + h].wait()
        direct_out[h] = chip_sum(1 + h, slice(h * half, (h + 1) * half)).astype(BF16)
        directs.append(copies.start(direct_out.at[h], direct_in.at[h], (z, 2 * chip + c)))

    load_new.wait()
    for load in old_loads:
        load.wait()

    def chip_ranks(k):
        return pl.ds(pl.multiple_of(k * 2 * blk, 2 * blk), 2 * blk)

    margin_pairs = []
    for i, k in enumerate(chips):
        part = contract_rows(basis[:, chip_ranks(k)], basis_old[...])
        margin[i] = part.reshape(2, blk, per * blk)
        margin_pairs.append(copies.start(margin.at[i, 1 - c], margin_partner.at[i], (z, partner)))

    merges = []
    for h, (i, chip) in enumerate(((2, over), (1, side))):
        at = slice(h * half, (h + 1) * half)
        relays[h].wait_recv()
        merged[h] = chip_sum(i, at) + relay_in[h].astype(F32)
        merges.append(copies.start(merged.at[h], merged_in.at[h], (z, 2 * chip + c)))

    def moment_copy(i, k, j):
        return pltpu.make_async_remote_copy(
            src_ref=(m_old, v_old)[i],
            dst_ref=moments.at[i, k],
            send_sem=mom_send.at[i, k, j],
            recv_sem=mom_recv.at[i, k],
            device_id=(z, 2 * chips[j] + c),
            device_id_type=MESH,
        )

    def moment_load(i, k):
        return pltpu.make_async_copy((m_old, v_old)[i], moments.at[i, k], load_sem.at[2 + i])

    def moment_forward(i, k):
        return pltpu.make_async_remote_copy(
            src_ref=moments.at[i, k],
            dst_ref=moments.at[i, k],
            send_sem=fwd_send.at[i, k],
            recv_sem=fwd_recv.at[i, k],
            device_id=(z, partner),
            device_id_type=MESH,
        )

    for k in range(per):

        @pl.when(d == k * n_outer + z)
        def _():
            for j in range(3):
                for i in range(2):
                    moment_copy(i, k, j).start()
            for i in range(2):
                moment_load(i, k).start()

    margin_copies = []
    for i, k in enumerate(chips):
        margin_pairs[i].wait_recv()
        margin_sum[i] = margin[i, c] + margin_partner[i]
        if i < 3:
            margin_copies.append(copies.start(margin_sum.at[i], margin_in.at[i], (z, 2 * k + c)))

    pairs[3].wait_recv()
    own_loads[3].wait()
    for h in range(2):
        at = slice(h * half, (h + 1) * half)
        directs[h].wait_recv()
        merges[h].wait_recv()
        total = chip_sum(3, at) + direct_in[h].astype(F32) + merged_in[h]
        high = total.astype(BF16)
        terms[at, :cols] = high
        terms[at, cols:] = (total - high.astype(F32)).astype(BF16)

    projected_pairs = []
    for i, k in enumerate(chips):
        part = contract_rows(basis[:, chip_ranks(k)], terms[...])
        part = (part[:, :cols] + part[:, cols:]).reshape(2, n_outer, pieces, fine, cols)
        for h in range(pieces):
            projected[h, i] = part[:, :, h]
            projected_pairs.append(
                copies.start(projected.at[h, i, 1 - c], projected_partner.at[h, i], (z, partner))
            )
    projected_copies = []
    for h in range(pieces):
        for i, k in enumerate(chips):
            projected_pairs[i * pieces + h].wait_recv()
            projected_sum[h, i] = projected[h, i, c] + projected_partner[h, i]
            if i < 3:
                projected_copies.append(
                    copies.start(projected_sum.at[h, i], projected_in.at[h, i], (z, 2 * k + c))
                )

    for k in range(per):
        owner = k * n_outer + z
        mine = c == owner % 2

        @pl.when(d == owner)
        def _():
            for i in range(2):
                moment_load(i, k).wait()

        @pl.when(jnp.logical_and(mine, d != owner))
        def _():
            for i in range(2):
                moment_copy(i, k, 0).wait_recv()

        @pl.when(mine)
        def _():
            for i in range(2):
                moment_forward(i, k).start()

        @pl.when(jnp.logical_not(mine))
        def _():
            for i in range(2):
                moment_forward(i, k).wait_recv()

    for copy in margin_copies:
        copy.wait_recv()
    margin_rows = margin_sum[3] + margin_in[0] + margin_in[1] + margin_in[2]
    old = moments[...].reshape(2, per * blk, cols)
    for i, rows_in in enumerate((margin_rows, margin_rows * margin_rows)):
        turned = jnp.dot(rows_in, old[i], precision=lax.Precision.HIGHEST, preferred_element_type=F32)
        rotated[:, i] = turned.reshape(n_outer, sub, cols)
    pass_along(range(n_outer - 2))
    planes = [lax.rem(z + j, n_outer) for j in range(1, n_outer)]
    rot_copies = [
        copies.start(rotated.at[to], rotated_in.at[j], (to, d)) for j, to in enumerate(planes)
    ]

    block_copies = []
    for h in range(pieces):
        for copy in projected_copies[3 * h : 3 * h + 3]:
            copy.wait_recv()
        block[h] = projected_sum[h, 3] + projected_in[h, 0] + projected_in[h, 1] + projected_in[h, 2]
        for j, to in enumerate(planes):
            block_copies.append(copies.start(block.at[h, to], block_in.at[h, j], (to, d)))

    for copy in rot_copies:
        copy.wait_recv()
    first, second = rotated[z, 0], rotated[z, 1]
    for j in range(n_outer - 1):
        first = first + rotated_in[j, 0]
        second = second + rotated_in[j, 1]
    for h in range(pieces):
        at = slice(h * fine, (h + 1) * fine)
        proj = block[h, z]
        for j in range(n_outer - 1):
            block_copies[h * (n_outer - 1) + j].wait_recv()
            proj = proj + block_in[h, j]
        mean = beta_mean * first[at] + (1.0 - beta_mean) * proj
        square = beta_square * second[at] + (1.0 - beta_square) * proj * proj
        moments_new[z, 0, at] = mean
        moments_new[z, 1, at] = square
        direction[d, z, at] = (
            mean / bias_mean / (jnp.sqrt(square / bias_square) + adam_epsilon)
        ).astype(BF16)

    spread = []
    for i, k in enumerate(chips):
        group = []
        for to in planes + [z]:
            if i == 3 and to is z:
                continue
            group.append(copies.start(direction.at[d, z], direction.at[d, z], (to, 2 * k + c)))
        spread.append(group)
    moment_spread = [copies.start(moments_new.at[z], moments_new.at[z], (to, d)) for to in planes]
    forwards = []
    for i in (3, 1, 2, 0):
        for copy in spread[i]:
            copy.wait_recv()
        mine = direction.at[2 * chips[i] + c]
        forwards.append(copies.start(mine, mine, (z, partner)))
    load_weight.wait()
    for copy in forwards:
        copy.wait_recv()
    directions = direction[...].reshape(rank, cols)
    tall = min(rows, 256)
    for s in range(0, rows, tall):
        update = jnp.dot(basis[s : s + tall, :], directions, preferred_element_type=F32)
        new_weight[s : s + tall, :] = weights[s : s + tall, :] - step_scale * update
    for copy in moment_spread:
        copy.wait_recv()
    m_new[...] = moments_new[:, 0].reshape(blk, cols)
    v_new[...] = moments_new[:, 1].reshape(blk, cols)

    for k in range(per):
        owner = k * n_outer + z

        @pl.when(d == owner)
        def _():
            for j in range(3):
                for i in range(2):
                    moment_copy(i, k, j).wait_send()

        @pl.when(c == owner % 2)
        def _():
            for i in range(2):
                moment_forward(i, k).wait_send()

    for copy in copies.started:
        copy.wait_send()


def square_scratch(n_outer, n_dev, rows, cols, rank):
    blk = rank // n_dev
    sub = blk // n_outer
    fine = sub // pieces
    per = n_dev // n_outer
    span = per * blk
    dma = pltpu.SemaphoreType.DMA
    count = 34 + 15 * pieces + 6 * n_outer
    return [
        pltpu.VMEM((4, rows, cols), BF16),
        pltpu.VMEM((4, rows, cols), BF16),
        pltpu.VMEM((rows, cols), BF16),
        pltpu.VMEM((2, rows // 2, cols), BF16),
        pltpu.VMEM((2, rows // 2, cols), BF16),
        pltpu.VMEM((2, rows // 2, cols), BF16),
        pltpu.VMEM((2, rows // 2, cols), F32),
        pltpu.VMEM((2, rows // 2, cols), F32),
        pltpu.VMEM((rows, 2 * cols), BF16),
        pltpu.VMEM((rows, rank), BF16),
        pltpu.VMEM((rows, span), BF16),
        pltpu.VMEM((rows, cols), F32),
        pltpu.VMEM((2, per, blk, cols), F32),
        pltpu.VMEM((4, 2, blk, span), F32),
        pltpu.VMEM((4, blk, span), F32),
        pltpu.VMEM((4, blk, span), F32),
        pltpu.VMEM((3, blk, span), F32),
        pltpu.VMEM((n_outer, 2, sub, cols), F32),
        pltpu.VMEM((n_outer - 1, 2, sub, cols), F32),
        pltpu.VMEM((pieces, 4, 2, n_outer, fine, cols), F32),
        pltpu.VMEM((pieces, 4, n_outer, fine, cols), F32),
        pltpu.VMEM((pieces, 4, n_outer, fine, cols), F32),
        pltpu.VMEM((pieces, 3, n_outer, fine, cols), F32),
        pltpu.VMEM((pieces, n_outer, fine, cols), F32),
        pltpu.VMEM((pieces, n_outer - 1, fine, cols), F32),
        pltpu.VMEM((n_dev, n_outer, sub, cols), BF16),
        pltpu.VMEM((n_outer, 2, sub, cols), F32),
        dma((4,)),
        dma((per,)),
        dma((4,)),
        dma((2, per, 3)),
        dma((2, per)),
        dma((2, per)),
        dma((2, per)),
        dma((count,)),
        dma((count,)),
        pltpu.SemaphoreType.REGULAR((max(n_outer - 2, 1),)),
    ]


def plain_scratch(n_outer, n_dev, rows, cols, rank):
    blk = rank // n_dev
    per = n_dev // n_outer
    span = per * blk
    n_chip = n_dev // 2
    dma = pltpu.SemaphoreType.DMA
    return (
        [
            pltpu.VMEM((n_dev, rows, cols), BF16),
            pltpu.VMEM((rows, rank), BF16),
            pltpu.VMEM((rows, span), BF16),
            pltpu.VMEM((rows, cols), F32),
            pltpu.VMEM((2, per, blk, cols), F32),
            pltpu.VMEM((n_dev, blk, span), F32),
            pltpu.VMEM((n_chip, blk, span), F32),
            pltpu.VMEM((n_chip, blk, span), F32),
            pltpu.VMEM((n_chip, blk, span), F32),
            pltpu.VMEM((2, blk, cols), F32),
            pltpu.VMEM((n_outer, 2, blk, cols), F32),
            pltpu.VMEM((n_dev, blk, cols), F32),
            pltpu.VMEM((n_chip, blk, cols), F32),
            pltpu.VMEM((n_chip, blk, cols), F32),
            pltpu.VMEM((n_chip, blk, cols), F32),
            pltpu.VMEM((blk, cols), F32),
            pltpu.VMEM((n_outer, blk, cols), F32),
            pltpu.VMEM((n_dev, blk, cols), BF16),
            dma((6,)),
            dma((per,)),
            dma((chunks, n_dev)),
            dma((chunks, n_dev)),
            dma((2, per, n_chip)),
            dma((2, per)),
            dma((2, per)),
            dma((2, per)),
        ]
        + [dma((n_chip,))] * 4
        + [dma((n_outer,))] * 2
        + [dma((parts, n_chip))] * 4
        + [dma((parts, n_outer))] * 2
        + [dma((parts, n_dev))] * 2
    )


def hand_over(weight_in, m_in, v_in, weight_out, m_out, v_out):
    weight_out[...] = weight_in[...]
    m_out[...] = m_in[...]
    v_out[...] = v_in[...]


def on_device(n_outer, n_dev, partials, p_old, p_new, weight, m_old, v_old):
    rows, cols = weight.shape
    rank = p_new.shape[1]
    blk = rank // n_dev
    per = n_dev // n_outer
    span = per * blk
    n_chip = n_dev // 2
    squared = n_chip == 4 and n_dev % n_outer == 0 and n_outer > 1 and blk % (16 * pieces * n_outer) == 0
    if blk % 128 and not squared:
        z = lax.axis_index("outer")
        p_old = jnp.concatenate(
            [
                lax.dynamic_slice_in_dim(p_old, (k * n_outer + z) * blk, blk, axis=1)
                for k in range(per)
            ],
            axis=1,
        )
    anywhere = pl.BlockSpec(memory_space=pltpu.HBM)
    vmem = pl.BlockSpec(memory_space=pltpu.VMEM)
    if squared:
        body, scratch = square_kernel, square_scratch(n_outer, n_dev, rows, cols, rank)
    else:
        body, scratch = kernel, plain_scratch(n_outer, n_dev, rows, cols, rank)
    results = pl.pallas_call(
        functools.partial(body, n_outer, n_dev),
        out_shape=(
            jax.ShapeDtypeStruct((rows, cols), F32),
            jax.ShapeDtypeStruct((blk, cols), F32),
            jax.ShapeDtypeStruct((blk, cols), F32),
        ),
        in_specs=[anywhere] * 6,
        out_specs=(vmem, vmem, vmem),
        scratch_shapes=scratch,
        compiler_params=pltpu.CompilerParams(
            collective_id=0, has_side_effects=True, vmem_limit_bytes=vmem_limit
        ),
    )(partials[0], p_old, p_new, weight, m_old, v_old)
    return pl.pallas_call(
        hand_over,
        out_shape=tuple(jax.ShapeDtypeStruct(r.shape, r.dtype) for r in results),
        in_specs=[vmem] * 3,
        out_specs=(vmem,) * 3,
        compiler_params=pltpu.CompilerParams(vmem_limit_bytes=finish_limit),
    )(*results)


def solution(mesh):
    in_specs = (
        P(("outer", "dev"), None, None),
        P("dev", None),
        P("dev", None),
        P("dev", None),
        P("dev", None),
        P("dev", None),
    )
    out_specs = (P("dev", None), P("dev", None), P("dev", None))
    return jax.shard_map(
        functools.partial(on_device, mesh.shape["outer"], mesh.shape["dev"]),
        mesh=mesh,
        in_specs=in_specs,
        out_specs=out_specs,
        check_vma=False,
    )
```

```python
import functools

import jax
import jax.numpy as jnp
from jax import lax
from jax.experimental import pallas as pl
from jax.experimental.pallas import tpu as pltpu
from jax.sharding import PartitionSpec as P

beta_mean = 0.9
beta_square = 0.95
bias_mean = 0.9999734386011124
bias_square = 0.9940794707796659
adam_epsilon = 1e-08
step_scale = 0.5

chunks = 2
early = 1
parts = 2
pieces = 2
vmem_limit = 50331648
finish_limit = 4194304

MESH = pl.DeviceIdType.MESH
F32 = jnp.float32
BF16 = jnp.bfloat16


def contract_rows(a, b):
    return lax.dot_general(a, b, (((0,), (0,)), ((), ())), preferred_element_type=F32)


def kernel(
    n_outer,
    n_dev,
    partials,
    p_old,
    p_new,
    weight,
    m_old,
    v_old,
    new_weight,
    m_new,
    v_new,
    grads,
    basis,
    basis_old,
    weights,
    moments,
    margin,
    margin_partner,
    margin_sum,
    margin_in,
    rotated,
    rotated_in,
    projected,
    projected_partner,
    projected_sum,
    projected_in,
    block,
    block_in,
    direction,
    load_sem,
    old_sem,
    grad_send,
    grad_recv,
    mom_send,
    mom_recv,
    fwd_send,
    fwd_recv,
    mp_send,
    mp_recv,
    ms_send,
    ms_recv,
    rot_send,
    rot_recv,
    pp_send,
    pp_recv,
    ps_send,
    ps_recv,
    blk_send,
    blk_recv,
    dir_send,
    dir_recv,
):
    z = lax.axis_index("outer")
    d = lax.axis_index("dev")
    n_chip = n_dev // 2
    q = d // 2
    c = d % 2
    partner = q * 2 + 1 - c
    rows, cols = weight.shape
    rank = p_new.shape[1]
    blk = rank // n_dev
    per = n_dev // n_outer

    def remote(src, dst, send, recv, where):
        return pltpu.make_async_remote_copy(
            src_ref=src, dst_ref=dst, send_sem=send, recv_sem=recv, device_id=where, device_id_type=MESH
        )

    barrier = pltpu.get_barrier_semaphore()
    for j in range(1, n_dev):
        pl.semaphore_signal(barrier, inc=1, device_id=(z, lax.rem(d + j, n_dev)), device_id_type=MESH)
    for j in range(1, n_outer):
        pl.semaphore_signal(barrier, inc=1, device_id=(lax.rem(z + j, n_outer), d), device_id_type=MESH)

    load_new = pltpu.make_async_copy(p_new, basis, load_sem.at[0])
    load_new.start()
    if p_old.shape[1] == per * blk:
        old_loads = [pltpu.make_async_copy(p_old, basis_old, old_sem.at[0])]
    else:
        old_loads = [
            pltpu.make_async_copy(
                p_old.at[:, pl.ds(pl.multiple_of((k * n_outer + z) * blk, blk), blk)],
                basis_old.at[:, k * blk : (k + 1) * blk],
                old_sem.at[k],
            )
            for k in range(per)
        ]
    for load in old_loads:
        load.start()
    load_weight = pltpu.make_async_copy(weight, weights, load_sem.at[2])
    load_weight.start()
    load_own = pltpu.make_async_copy(
        partials.at[pl.ds(pl.multiple_of(d * rows, rows), rows)], grads.at[0], load_sem.at[3]
    )
    load_own.start()

    pl.semaphore_wait(barrier, n_dev - 1 + n_outer - 1)

    def moment_copies(k, owner):
        copies = []
        for j in range(1, n_chip):
            to = (z, lax.rem(q + j, n_chip) * 2 + c)
            for i, src in enumerate((m_old, v_old)):
                copies.append(remote(src, moments.at[i, k], mom_send.at[i, k, j], mom_recv.at[i, k], to))
        return copies

    for k in range(per):
        owner = k * n_outer + z

        @pl.when(d == owner)
        def _():
            for copy in moment_copies(k, owner):
                copy.start()
            for i, src in enumerate((m_old, v_old)):
                pltpu.make_async_copy(src, moments.at[i, k], load_sem.at[4 + i]).start()

    tall = rows // chunks

    def send_gradients(chunk):
        copies = []
        for j in range(1, n_dev):
            to = lax.rem(d + j, n_dev)
            copy = remote(
                partials.at[pl.ds(pl.multiple_of(to * rows + chunk * tall, tall), tall)],
                grads.at[j, chunk * tall : (chunk + 1) * tall],
                grad_send.at[chunk, j],
                grad_recv.at[chunk, j],
                (z, to),
            )
            copy.start()
            copies.append(copy)
        return copies

    grad_copies = [send_gradients(chunk) for chunk in range(early)]

    load_new.wait()
    for load in old_loads:
        load.wait()
    width = min(rank, 256)
    for s in range(0, rank, width):
        part = contract_rows(basis[:, s : s + width], basis_old[...])
        margin[s // blk : (s + width) // blk] = part.reshape(width // blk, blk, part.shape[1])

    def scatter_start(val, prt, send, recv):
        copies = []
        for j in list(range(1, n_chip)) + [0]:
            k = lax.rem(q + j, n_chip)
            copy = remote(val.at[2 * k + 1 - c], prt.at[j], send.at[j], recv.at[j], (z, partner))
            copy.start()
            copies.append((j, k, copy))
        return copies

    def scatter_middle(pairs, val, prt, tot, arr, send, recv):
        copies = []
        for j, k, pair in pairs:
            pair.wait_recv()
            tot[j] = val[2 * k + c] + prt[j]
            if j:
                copy = remote(tot.at[j], arr.at[j], send.at[j], recv.at[j], (z, 2 * k + c))
                copy.start()
                copies.append((j, copy))
        return copies

    def scatter_end(copies, tot, arr):
        total = tot[0]
        for j, copy in copies:
            copy.wait_recv()
            total = total + arr[j]
        return total

    margin_pairs = scatter_start(margin, margin_partner, mp_send, mp_recv)

    for k in range(per):
        owner = k * n_outer + z
        mine = c == owner % 2

        @pl.when(d == owner)
        def _():
            for i, src in enumerate((m_old, v_old)):
                pltpu.make_async_copy(src, moments.at[i, k], load_sem.at[4 + i]).wait()

        @pl.when(jnp.logical_and(mine, d != owner))
        def _():
            for i, src in enumerate((m_old, v_old)):
                remote(src, moments.at[i, k], mom_send.at[i, k, 0], mom_recv.at[i, k], (z, d)).wait_recv()

        @pl.when(mine)
        def _():
            for i in range(2):
                remote(
                    moments.at[i, k], moments.at[i, k], fwd_send.at[i, k], fwd_recv.at[i, k], (z, partner)
                ).start()

    margin_copies = scatter_middle(
        margin_pairs, margin, margin_partner, margin_sum, margin_in, ms_send, ms_recv
    )

    for chunk in range(early, chunks):
        grad_copies.append(send_gradients(chunk))

    for k in range(per):
        mine = c == (k * n_outer + z) % 2

        @pl.when(jnp.logical_not(mine))
        def _():
            for i in range(2):
                remote(
                    moments.at[i, k], moments.at[i, k], fwd_send.at[i, k], fwd_recv.at[i, k], (z, partner)
                ).wait_recv()

    margin_rows = scatter_end(margin_copies, margin_sum, margin_in)
    old = moments[...].reshape(2, per * blk, cols)
    rotated[0] = jnp.dot(margin_rows, old[0], precision=lax.Precision.HIGHEST, preferred_element_type=F32)
    rotated[1] = jnp.dot(
        margin_rows * margin_rows, old[1], precision=lax.Precision.HIGHEST, preferred_element_type=F32
    )
    rot_copies = []
    for j in range(1, n_outer):
        copy = remote(
            rotated, rotated_in.at[j], rot_send.at[j], rot_recv.at[j], (lax.rem(z + j, n_outer), d)
        )
        copy.start()
        rot_copies.append(copy)

    load_own.wait()
    for chunk in range(chunks):
        for copy in grad_copies[chunk]:
            copy.wait_recv()
        part_rows = slice(chunk * tall, (chunk + 1) * tall)
        total = grads[0, part_rows].astype(F32)
        for j in range(1, n_dev):
            total = total + grads[j, part_rows].astype(F32)
        high = total.astype(BF16)
        low = (total - high.astype(F32)).astype(BF16)
        both = jnp.concatenate([high, low], axis=1)
        for s in range(0, rank, width):
            part = contract_rows(basis[part_rows, s : s + width], both)
            part = (part[:, :cols] + part[:, cols:]).reshape(width // blk, blk, cols)
            blocks = slice(s // blk, (s + width) // blk)
            projected[blocks] = part if chunk == 0 else projected[blocks] + part
    half = blk // parts
    views = [slice(h * half, (h + 1) * half) for h in range(parts)]
    pairs = [
        scatter_start(projected.at[:, v], projected_partner.at[:, v], pp_send.at[h], pp_recv.at[h])
        for h, v in enumerate(views)
    ]
    copies = [
        scatter_middle(
            pairs[h],
            projected.at[:, v],
            projected_partner.at[:, v],
            projected_sum.at[:, v],
            projected_in.at[:, v],
            ps_send.at[h],
            ps_recv.at[h],
        )
        for h, v in enumerate(views)
    ]
    blk_copies = []
    for h, v in enumerate(views):
        block[v] = scatter_end(copies[h], projected_sum.at[:, v], projected_in.at[:, v])
        for j in range(1, n_outer):
            copy = remote(
                block.at[v],
                block_in.at[j, v],
                blk_send.at[h, j],
                blk_recv.at[h, j],
                (lax.rem(z + j, n_outer), d),
            )
            copy.start()
            blk_copies.append(copy)
    for copy in rot_copies:
        copy.wait_recv()
    dir_copies = []
    for h, v in enumerate(views):
        for copy in blk_copies[h * (n_outer - 1) : (h + 1) * (n_outer - 1)]:
            copy.wait_recv()
        first = rotated[0, v]
        second = rotated[1, v]
        proj = block[v]
        for j in range(1, n_outer):
            first = first + rotated_in[j, 0, v]
            second = second + rotated_in[j, 1, v]
            proj = proj + block_in[j, v]
        mean = beta_mean * first + (1.0 - beta_mean) * proj
        square = beta_square * second + (1.0 - beta_square) * proj * proj
        m_new[v] = mean
        v_new[v] = square
        direction[d, v] = (mean / bias_mean / (jnp.sqrt(square / bias_square) + adam_epsilon)).astype(BF16)
        for j in range(1, n_dev):
            copy = remote(
                direction.at[d, v],
                direction.at[d, v],
                dir_send.at[h, j],
                dir_recv.at[h, j],
                (z, lax.rem(d + j, n_dev)),
            )
            copy.start()
            dir_copies.append(copy)
    load_weight.wait()
    for copy in dir_copies:
        copy.wait_recv()
    directions = direction[...].reshape(rank, cols)
    tall = min(rows, 256)
    for s in range(0, rows, tall):
        update = jnp.dot(basis[s : s + tall, :], directions, preferred_element_type=F32)
        new_weight[s : s + tall, :] = weights[s : s + tall, :] - step_scale * update

    for k in range(per):
        owner = k * n_outer + z
        mine = c == owner % 2

        @pl.when(d == owner)
        def _():
            for copy in moment_copies(k, owner):
                copy.wait_send()

        @pl.when(mine)
        def _():
            for i in range(2):
                remote(
                    moments.at[i, k], moments.at[i, k], fwd_send.at[i, k], fwd_recv.at[i, k], (z, partner)
                ).wait_send()

    for copy in sum(grad_copies, []) + rot_copies + blk_copies + dir_copies:
        copy.wait_send()
    for group in [margin_pairs] + pairs:
        for _, _, copy in group:
            copy.wait_send()
    for group in [margin_copies] + copies:
        for _, copy in group:
            copy.wait_send()

class Copies:
    def __init__(self, send, recv):
        self.send, self.recv, self.started = send, recv, []

    def start(self, src, dst, to):
        i = len(self.started)
        copy = pltpu.make_async_remote_copy(
            src_ref=src,
            dst_ref=dst,
            send_sem=self.send.at[i],
            recv_sem=self.recv.at[i],
            device_id=to,
            device_id_type=MESH,
        )
        copy.start()
        self.started.append(copy)
        return copy


def square_kernel(
    n_outer,
    n_dev,
    partials,
    p_old,
    p_new,
    weight,
    m_old,
    v_old,
    new_weight,
    m_new,
    v_new,
    own,
    pair,
    far_sum,
    relay_in,
    direct_out,
    direct_in,
    merged,
    merged_in,
    terms,
    basis,
    basis_old,
    weights,
    moments,
    margin,
    margin_partner,
    margin_sum,
    margin_in,
    rotated,
    rotated_in,
    projected,
    projected_partner,
    projected_sum,
    projected_in,
    block,
    block_in,
    direction,
    moments_new,
    load_sem,
    old_sem,
    own_sem,
    mom_send,
    mom_recv,
    fwd_send,
    fwd_recv,
    send_sem,
    recv_sem,
    merge_send,
    merge_recv,
    line_sem,
):
    z = lax.axis_index("outer")
    d = lax.axis_index("dev")
    q = d // 2
    c = d % 2
    partner = q * 2 + 1 - c
    side = q + 1 - 2 * (q % 2)
    over = lax.rem(q + 2, 4)
    far = lax.rem(side + 2, 4)
    chips = (far, side, over, q)
    rows, cols = weight.shape
    rank = p_new.shape[1]
    blk = rank // n_dev
    sub = blk // n_outer
    fine = sub // pieces
    per = n_dev // n_outer
    half = rows // 2
    copies = Copies(send_sem, recv_sem)
    above = (2 * n_outer - 2 - z) // n_outer
    below = (z + n_outer - 1) // n_outer

    def signal_line(sem):
        @pl.when(z > 0)
        def _():
            pl.semaphore_signal(sem, inc=1, device_id=(z - 1, d), device_id_type=MESH)

        @pl.when(z < n_outer - 1)
        def _():
            pl.semaphore_signal(sem, inc=1, device_id=(z + 1, d), device_id_type=MESH)

    def pass_along(steps):
        for r in steps:
            pl.semaphore_wait(line_sem.at[r], above + below)
            if r + 1 < n_outer - 2:
                signal_line(line_sem.at[r + 1])

    barrier = pltpu.get_barrier_semaphore()
    for to in (partner, 2 * side + c, 2 * over + c):
        pl.semaphore_signal(barrier, inc=1, device_id=(z, to), device_id_type=MESH)
    signal_line(barrier)

    def rows_of(to):
        return partials.at[pl.ds(pl.multiple_of(to * rows, rows), rows)]

    own_loads = [
        pltpu.make_async_copy(rows_of(2 * k + c), own.at[i], own_sem.at[i]) for i, k in enumerate(chips)
    ]
    for load in own_loads[:3]:
        load.start()
    load_new = pltpu.make_async_copy(p_new, basis, load_sem.at[0])
    load_new.start()
    old_loads = [
        pltpu.make_async_copy(
            p_old.at[:, pl.ds(pl.multiple_of((k * n_outer + z) * blk, blk), blk)],
            basis_old.at[:, k * blk : (k + 1) * blk],
            old_sem.at[k],
        )
        for k in range(per)
    ]
    for load in old_loads:
        load.start()
    own_loads[3].start()
    load_weight = pltpu.make_async_copy(weight, weights, load_sem.at[1])
    load_weight.start()

    pl.semaphore_wait(barrier, 3 + above + below)

    def moment_copy(i, k, j):
        return pltpu.make_async_remote_copy(
            src_ref=(m_old, v_old)[i],
            dst_ref=moments.at[i, k],
            send_sem=mom_send.at[i, k, j],
            recv_sem=mom_recv.at[i, k],
            device_id=(z, 2 * (side, over)[j] + c),
            device_id_type=MESH,
        )

    def moment_relay(i, k):
        return pltpu.make_async_remote_copy(
            src_ref=moments.at[i, k],
            dst_ref=moments.at[i, k],
            send_sem=mom_send.at[i, k, 2],
            recv_sem=mom_recv.at[i, k],
            device_id=(z, 2 * (over, side)[i] + c),
            device_id_type=MESH,
        )

    def moments_from(k, chip):
        owner = k * n_outer + z
        return jnp.logical_and(c == owner % 2, owner // 2 == chip)

    def moment_load(i, k):
        return pltpu.make_async_copy((m_old, v_old)[i], moments.at[i, k], load_sem.at[2 + i])

    def moment_forward(i, k):
        return pltpu.make_async_remote_copy(
            src_ref=moments.at[i, k],
            dst_ref=moments.at[i, k],
            send_sem=fwd_send.at[i, k],
            recv_sem=fwd_recv.at[i, k],
            device_id=(z, partner),
            device_id_type=MESH,
        )

    for k in range(per):

        @pl.when(d == k * n_outer + z)
        def _():
            for j in range(2):
                for i in range(2):
                    moment_copy(i, k, j).start()
            for i in range(2):
                moment_load(i, k).start()

    pairs = [copies.start(rows_of(2 * k + 1 - c), pair.at[i], (z, partner)) for i, k in enumerate(chips)]
    if n_outer > 2:
        signal_line(line_sem.at[0])

    def chip_sum(i, at):
        return own[i, at].astype(F32) + pair[i, at].astype(F32)

    pairs[0].wait_recv()
    own_loads[0].wait()
    relays = []
    for h, chip in enumerate((side, over)):
        at = slice(h * half, (h + 1) * half)
        far_sum[at] = chip_sum(0, at).astype(BF16)
        relays.append(copies.start(far_sum.at[at], relay_in.at[h], (z, 2 * chip + c)))
    directs = []
    for h, chip in enumerate((side, over)):
        pairs[1 + h].wait_recv()
        own_loads[1 + h].wait()
        direct_out[h] = chip_sum(1 + h, slice(h * half, (h + 1) * half)).astype(BF16)
        directs.append(copies.start(direct_out.at[h], direct_in.at[h], (z, 2 * chip + c)))

    load_new.wait()
    for load in old_loads:
        load.wait()

    def chip_ranks(k):
        return pl.ds(pl.multiple_of(k * 2 * blk, 2 * blk), 2 * blk)

    margin_pairs = []
    for i, k in enumerate(chips):
        part = contract_rows(basis[:, chip_ranks(k)], basis_old[...])
        margin[i] = part.reshape(2, blk, per * blk)
        margin_pairs.append(copies.start(margin.at[i, 1 - c], margin_partner.at[i], (z, partner)))

    merges = []
    merging = Copies(merge_send, merge_recv)
    for h, (i, chip) in enumerate(((2, over), (1, side))):
        at = slice(h * half, (h + 1) * half)
        relays[h].wait_recv()
        merged[h] = chip_sum(i, at) + relay_in[h].astype(F32)
        merges.append(merging.start(merged.at[h], merged_in.at[h], (z, 2 * chip + c)))

    for k in range(per):
        for i, chip in enumerate((side, over)):

            @pl.when(moments_from(k, chip))
            def _():
                moment_copy(0, k, 0).wait_recv()
                moment_copy(1, k, 0).wait_recv()
                moment_relay(i, k).start()

    for copy in merges:
        copy.wait_send()
    margin_copies = []
    for i, k in enumerate(chips):
        margin_pairs[i].wait_recv()
        margin_sum[i] = margin[i, c] + margin_partner[i]
        if i < 3:
            margin_copies.append(copies.start(margin_sum.at[i], margin_in.at[i], (z, 2 * k + c)))

    pairs[3].wait_recv()
    own_loads[3].wait()
    for h in range(2):
        at = slice(h * half, (h + 1) * half)
        directs[h].wait_recv()
        merges[h].wait_recv()
        total = chip_sum(3, at) + direct_in[h].astype(F32) + merged_in[h]
        high = total.astype(BF16)
        terms[at, :cols] = high
        terms[at, cols:] = (total - high.astype(F32)).astype(BF16)

    projected_pairs = []
    for i, k in enumerate(chips):
        part = contract_rows(basis[:, chip_ranks(k)], terms[...])
        part = (part[:, :cols] + part[:, cols:]).reshape(2, n_outer, pieces, fine, cols)
        for h in range(pieces):
            projected[h, i] = part[:, :, h]
            projected_pairs.append(
                copies.start(projected.at[h, i, 1 - c], projected_partner.at[h, i], (z, partner))
            )
    projected_copies = []
    for h in range(pieces):
        for i, k in enumerate(chips):
            projected_pairs[i * pieces + h].wait_recv()
            projected_sum[h, i] = projected[h, i, c] + projected_partner[h, i]
            if i < 3:
                projected_copies.append(
                    copies.start(projected_sum.at[h, i], projected_in.at[h, i], (z, 2 * k + c))
                )

    for k in range(per):
        owner = k * n_outer + z
        mine = c == owner % 2

        @pl.when(d == owner)
        def _():
            for i in range(2):
                moment_load(i, k).wait()

        @pl.when(moments_from(k, far))
        def _():
            for i in range(2):
                moment_copy(i, k, 0).wait_recv()

        @pl.when(mine)
        def _():
            for i in range(2):
                moment_forward(i, k).start()

        @pl.when(jnp.logical_not(mine))
        def _():
            for i in range(2):
                moment_forward(i, k).wait_recv()

    for copy in margin_copies:
        copy.wait_recv()
    margin_rows = margin_sum[3] + margin_in[0] + margin_in[1] + margin_in[2]
    old = moments[...].reshape(2, per * blk, cols)
    for i, rows_in in enumerate((margin_rows, margin_rows * margin_rows)):
        turned = jnp.dot(rows_in, old[i], precision=lax.Precision.HIGHEST, preferred_element_type=F32)
        rotated[:, i] = turned.reshape(n_outer, sub, cols)
    pass_along(range(n_outer - 2))
    planes = [lax.rem(z + j, n_outer) for j in range(1, n_outer)]
    rot_copies = [
        copies.start(rotated.at[to], rotated_in.at[j], (to, d)) for j, to in enumerate(planes)
    ]

    block_copies = []
    for h in range(pieces):
        for copy in projected_copies[3 * h : 3 * h + 3]:
            copy.wait_recv()
        block[h] = projected_sum[h, 3] + projected_in[h, 0] + projected_in[h, 1] + projected_in[h, 2]
        for j, to in enumerate(planes):
            block_copies.append(copies.start(block.at[h, to], block_in.at[h, j], (to, d)))

    for copy in rot_copies:
        copy.wait_recv()
    first, second = rotated[z, 0], rotated[z, 1]
    for j in range(n_outer - 1):
        first = first + rotated_in[j, 0]
        second = second + rotated_in[j, 1]
    for h in range(pieces):
        at = slice(h * fine, (h + 1) * fine)
        proj = block[h, z]
        for j in range(n_outer - 1):
            block_copies[h * (n_outer - 1) + j].wait_recv()
            proj = proj + block_in[h, j]
        mean = beta_mean * first[at] + (1.0 - beta_mean) * proj
        square = beta_square * second[at] + (1.0 - beta_square) * proj * proj
        moments_new[z, 0, at] = mean
        moments_new[z, 1, at] = square
        direction[d, z, at] = (
            mean / bias_mean / (jnp.sqrt(square / bias_square) + adam_epsilon)
        ).astype(BF16)

    spread = []
    for i, k in enumerate(chips):
        group = []
        for to in planes + [z]:
            if i == 3 and to is z:
                continue
            group.append(copies.start(direction.at[d, z], direction.at[d, z], (to, 2 * k + c)))
        spread.append(group)
    moment_spread = [copies.start(moments_new.at[z], moments_new.at[z], (to, d)) for to in planes]
    forwards = []
    for i in (3, 1, 2, 0):
        for copy in spread[i]:
            copy.wait_recv()
        mine = direction.at[2 * chips[i] + c]
        forwards.append(copies.start(mine, mine, (z, partner)))
    load_weight.wait()
    for copy in forwards:
        copy.wait_recv()
    directions = direction[...].reshape(rank, cols)
    tall = min(rows, 256)
    for s in range(0, rows, tall):
        update = jnp.dot(basis[s : s + tall, :], directions, preferred_element_type=F32)
        new_weight[s : s + tall, :] = weights[s : s + tall, :] - step_scale * update
    for copy in moment_spread:
        copy.wait_recv()
    m_new[...] = moments_new[:, 0].reshape(blk, cols)
    v_new[...] = moments_new[:, 1].reshape(blk, cols)

    for k in range(per):
        owner = k * n_outer + z

        @pl.when(d == owner)
        def _():
            for j in range(2):
                for i in range(2):
                    moment_copy(i, k, j).wait_send()

        for i, chip in enumerate((side, over)):

            @pl.when(moments_from(k, chip))
            def _():
                moment_relay(i, k).wait_send()

        @pl.when(c == owner % 2)
        def _():
            for i in range(2):
                moment_forward(i, k).wait_send()

    for copy in copies.started:
        copy.wait_send()


def square_scratch(n_outer, n_dev, rows, cols, rank):
    blk = rank // n_dev
    sub = blk // n_outer
    fine = sub // pieces
    per = n_dev // n_outer
    span = per * blk
    dma = pltpu.SemaphoreType.DMA
    count = 34 + 15 * pieces + 6 * n_outer
    return [
        pltpu.VMEM((4, rows, cols), BF16),
        pltpu.VMEM((4, rows, cols), BF16),
        pltpu.VMEM((rows, cols), BF16),
        pltpu.VMEM((2, rows // 2, cols), BF16),
        pltpu.VMEM((2, rows // 2, cols), BF16),
        pltpu.VMEM((2, rows // 2, cols), BF16),
        pltpu.VMEM((2, rows // 2, cols), F32),
        pltpu.VMEM((2, rows // 2, cols), F32),
        pltpu.VMEM((rows, 2 * cols), BF16),
        pltpu.VMEM((rows, rank), BF16),
        pltpu.VMEM((rows, span), BF16),
        pltpu.VMEM((rows, cols), F32),
        pltpu.VMEM((2, per, blk, cols), F32),
        pltpu.VMEM((4, 2, blk, span), F32),
        pltpu.VMEM((4, blk, span), F32),
        pltpu.VMEM((4, blk, span), F32),
        pltpu.VMEM((3, blk, span), F32),
        pltpu.VMEM((n_outer, 2, sub, cols), F32),
        pltpu.VMEM((n_outer - 1, 2, sub, cols), F32),
        pltpu.VMEM((pieces, 4, 2, n_outer, fine, cols), F32),
        pltpu.VMEM((pieces, 4, n_outer, fine, cols), F32),
        pltpu.VMEM((pieces, 4, n_outer, fine, cols), F32),
        pltpu.VMEM((pieces, 3, n_outer, fine, cols), F32),
        pltpu.VMEM((pieces, n_outer, fine, cols), F32),
        pltpu.VMEM((pieces, n_outer - 1, fine, cols), F32),
        pltpu.VMEM((n_dev, n_outer, sub, cols), BF16),
        pltpu.VMEM((n_outer, 2, sub, cols), F32),
        dma((4,)),
        dma((per,)),
        dma((4,)),
        dma((2, per, 3)),
        dma((2, per)),
        dma((2, per)),
        dma((2, per)),
        dma((count,)),
        dma((count,)),
        dma((2,)),
        dma((2,)),
        pltpu.SemaphoreType.REGULAR((max(n_outer - 2, 1),)),
    ]


def plain_scratch(n_outer, n_dev, rows, cols, rank):
    blk = rank // n_dev
    per = n_dev // n_outer
    span = per * blk
    n_chip = n_dev // 2
    dma = pltpu.SemaphoreType.DMA
    return (
        [
            pltpu.VMEM((n_dev, rows, cols), BF16),
            pltpu.VMEM((rows, rank), BF16),
            pltpu.VMEM((rows, span), BF16),
            pltpu.VMEM((rows, cols), F32),
            pltpu.VMEM((2, per, blk, cols), F32),
            pltpu.VMEM((n_dev, blk, span), F32),
            pltpu.VMEM((n_chip, blk, span), F32),
            pltpu.VMEM((n_chip, blk, span), F32),
            pltpu.VMEM((n_chip, blk, span), F32),
            pltpu.VMEM((2, blk, cols), F32),
            pltpu.VMEM((n_outer, 2, blk, cols), F32),
            pltpu.VMEM((n_dev, blk, cols), F32),
            pltpu.VMEM((n_chip, blk, cols), F32),
            pltpu.VMEM((n_chip, blk, cols), F32),
            pltpu.VMEM((n_chip, blk, cols), F32),
            pltpu.VMEM((blk, cols), F32),
            pltpu.VMEM((n_outer, blk, cols), F32),
            pltpu.VMEM((n_dev, blk, cols), BF16),
            dma((6,)),
            dma((per,)),
            dma((chunks, n_dev)),
            dma((chunks, n_dev)),
            dma((2, per, n_chip)),
            dma((2, per)),
            dma((2, per)),
            dma((2, per)),
        ]
        + [dma((n_chip,))] * 4
        + [dma((n_outer,))] * 2
        + [dma((parts, n_chip))] * 4
        + [dma((parts, n_outer))] * 2
        + [dma((parts, n_dev))] * 2
    )


def hand_over(weight_in, m_in, v_in, weight_out, m_out, v_out):
    weight_out[...] = weight_in[...]
    m_out[...] = m_in[...]
    v_out[...] = v_in[...]


def on_device(n_outer, n_dev, partials, p_old, p_new, weight, m_old, v_old):
    rows, cols = weight.shape
    rank = p_new.shape[1]
    blk = rank // n_dev
    per = n_dev // n_outer
    span = per * blk
    n_chip = n_dev // 2
    squared = n_chip == 4 and n_dev % n_outer == 0 and n_outer > 1 and blk % (16 * pieces * n_outer) == 0
    if blk % 128 and not squared:
        z = lax.axis_index("outer")
        p_old = jnp.concatenate(
            [
                lax.dynamic_slice_in_dim(p_old, (k * n_outer + z) * blk, blk, axis=1)
                for k in range(per)
            ],
            axis=1,
        )
    anywhere = pl.BlockSpec(memory_space=pltpu.HBM)
    vmem = pl.BlockSpec(memory_space=pltpu.VMEM)
    if squared:
        body, scratch = square_kernel, square_scratch(n_outer, n_dev, rows, cols, rank)
    else:
        body, scratch = kernel, plain_scratch(n_outer, n_dev, rows, cols, rank)
    operands = (partials[0], p_old, p_new, weight, m_old, v_old)
    results = pl.pallas_call(
        functools.partial(body, n_outer, n_dev),
        out_shape=(
            jax.ShapeDtypeStruct((rows, cols), F32),
            jax.ShapeDtypeStruct((blk, cols), F32),
            jax.ShapeDtypeStruct((blk, cols), F32),
        ),
        in_specs=[anywhere] * 6,
        out_specs=(vmem, vmem, vmem),
        scratch_shapes=scratch,
        compiler_params=pltpu.CompilerParams(
            collective_id=0, has_side_effects=True, vmem_limit_bytes=vmem_limit
        ),
    )(*[pltpu.with_memory_space_constraint(a, pltpu.HBM) for a in operands])
    return pl.pallas_call(
        hand_over,
        out_shape=tuple(jax.ShapeDtypeStruct(r.shape, r.dtype) for r in results),
        in_specs=[vmem] * 3,
        out_specs=(vmem,) * 3,
        compiler_params=pltpu.CompilerParams(vmem_limit_bytes=finish_limit),
    )(*results)


def solution(mesh):
    in_specs = (
        P(("outer", "dev"), None, None),
        P("dev", None),
        P("dev", None),
        P("dev", None),
        P("dev", None),
        P("dev", None),
    )
    out_specs = (P("dev", None), P("dev", None), P("dev", None))
    return jax.shard_map(
        functools.partial(on_device, mesh.shape["outer"], mesh.shape["dev"]),
        mesh=mesh,
        in_specs=in_specs,
        out_specs=out_specs,
        check_vma=False,
    )
```

```python
import functools

import jax
import jax.numpy as jnp
from jax import lax
from jax.experimental import pallas as pl
from jax.experimental.pallas import tpu as pltpu
from jax.sharding import PartitionSpec as P

beta_mean = 0.9
beta_square = 0.95
bias_mean = 0.9999734386011124
bias_square = 0.9940794707796659
adam_epsilon = 1e-08
step_scale = 0.5

chunks = 2
early = 1
parts = 2
pieces = 2
shared_part = (3, 16)
vmem_limit = 50331648
finish_limit = 4194304

MESH = pl.DeviceIdType.MESH
F32 = jnp.float32
BF16 = jnp.bfloat16


def contract_rows(a, b):
    return lax.dot_general(a, b, (((0,), (0,)), ((), ())), preferred_element_type=F32)


def kernel(
    n_outer,
    n_dev,
    partials,
    p_old,
    p_new,
    weight,
    m_old,
    v_old,
    new_weight,
    m_new,
    v_new,
    grads,
    basis,
    basis_old,
    weights,
    moments,
    margin,
    margin_partner,
    margin_sum,
    margin_in,
    rotated,
    rotated_in,
    projected,
    projected_partner,
    projected_sum,
    projected_in,
    block,
    block_in,
    direction,
    load_sem,
    old_sem,
    grad_send,
    grad_recv,
    mom_send,
    mom_recv,
    fwd_send,
    fwd_recv,
    mp_send,
    mp_recv,
    ms_send,
    ms_recv,
    rot_send,
    rot_recv,
    pp_send,
    pp_recv,
    ps_send,
    ps_recv,
    blk_send,
    blk_recv,
    dir_send,
    dir_recv,
):
    z = lax.axis_index("outer")
    d = lax.axis_index("dev")
    n_chip = n_dev // 2
    q = d // 2
    c = d % 2
    partner = q * 2 + 1 - c
    rows, cols = weight.shape
    rank = p_new.shape[1]
    blk = rank // n_dev
    per = n_dev // n_outer

    def remote(src, dst, send, recv, where):
        return pltpu.make_async_remote_copy(
            src_ref=src, dst_ref=dst, send_sem=send, recv_sem=recv, device_id=where, device_id_type=MESH
        )

    barrier = pltpu.get_barrier_semaphore()
    for j in range(1, n_dev):
        pl.semaphore_signal(barrier, inc=1, device_id=(z, lax.rem(d + j, n_dev)), device_id_type=MESH)
    for j in range(1, n_outer):
        pl.semaphore_signal(barrier, inc=1, device_id=(lax.rem(z + j, n_outer), d), device_id_type=MESH)

    load_new = pltpu.make_async_copy(p_new, basis, load_sem.at[0])
    load_new.start()
    if p_old.shape[1] == per * blk:
        old_loads = [pltpu.make_async_copy(p_old, basis_old, old_sem.at[0])]
    else:
        old_loads = [
            pltpu.make_async_copy(
                p_old.at[:, pl.ds(pl.multiple_of((k * n_outer + z) * blk, blk), blk)],
                basis_old.at[:, k * blk : (k + 1) * blk],
                old_sem.at[k],
            )
            for k in range(per)
        ]
    for load in old_loads:
        load.start()
    load_weight = pltpu.make_async_copy(weight, weights, load_sem.at[2])
    load_weight.start()
    load_own = pltpu.make_async_copy(
        partials.at[pl.ds(pl.multiple_of(d * rows, rows), rows)], grads.at[0], load_sem.at[3]
    )
    load_own.start()

    pl.semaphore_wait(barrier, n_dev - 1 + n_outer - 1)

    def moment_copies(k, owner):
        copies = []
        for j in range(1, n_chip):
            to = (z, lax.rem(q + j, n_chip) * 2 + c)
            for i, src in enumerate((m_old, v_old)):
                copies.append(remote(src, moments.at[i, k], mom_send.at[i, k, j], mom_recv.at[i, k], to))
        return copies

    for k in range(per):
        owner = k * n_outer + z

        @pl.when(d == owner)
        def _():
            for copy in moment_copies(k, owner):
                copy.start()
            for i, src in enumerate((m_old, v_old)):
                pltpu.make_async_copy(src, moments.at[i, k], load_sem.at[4 + i]).start()

    tall = rows // chunks

    def send_gradients(chunk):
        copies = []
        for j in range(1, n_dev):
            to = lax.rem(d + j, n_dev)
            copy = remote(
                partials.at[pl.ds(pl.multiple_of(to * rows + chunk * tall, tall), tall)],
                grads.at[j, chunk * tall : (chunk + 1) * tall],
                grad_send.at[chunk, j],
                grad_recv.at[chunk, j],
                (z, to),
            )
            copy.start()
            copies.append(copy)
        return copies

    grad_copies = [send_gradients(chunk) for chunk in range(early)]

    load_new.wait()
    for load in old_loads:
        load.wait()
    width = min(rank, 256)
    for s in range(0, rank, width):
        part = contract_rows(basis[:, s : s + width], basis_old[...])
        margin[s // blk : (s + width) // blk] = part.reshape(width // blk, blk, part.shape[1])

    def scatter_start(val, prt, send, recv):
        copies = []
        for j in list(range(1, n_chip)) + [0]:
            k = lax.rem(q + j, n_chip)
            copy = remote(val.at[2 * k + 1 - c], prt.at[j], send.at[j], recv.at[j], (z, partner))
            copy.start()
            copies.append((j, k, copy))
        return copies

    def scatter_middle(pairs, val, prt, tot, arr, send, recv):
        copies = []
        for j, k, pair in pairs:
            pair.wait_recv()
            tot[j] = val[2 * k + c] + prt[j]
            if j:
                copy = remote(tot.at[j], arr.at[j], send.at[j], recv.at[j], (z, 2 * k + c))
                copy.start()
                copies.append((j, copy))
        return copies

    def scatter_end(copies, tot, arr):
        total = tot[0]
        for j, copy in copies:
            copy.wait_recv()
            total = total + arr[j]
        return total

    margin_pairs = scatter_start(margin, margin_partner, mp_send, mp_recv)

    for k in range(per):
        owner = k * n_outer + z
        mine = c == owner % 2

        @pl.when(d == owner)
        def _():
            for i, src in enumerate((m_old, v_old)):
                pltpu.make_async_copy(src, moments.at[i, k], load_sem.at[4 + i]).wait()

        @pl.when(jnp.logical_and(mine, d != owner))
        def _():
            for i, src in enumerate((m_old, v_old)):
                remote(src, moments.at[i, k], mom_send.at[i, k, 0], mom_recv.at[i, k], (z, d)).wait_recv()

        @pl.when(mine)
        def _():
            for i in range(2):
                remote(
                    moments.at[i, k], moments.at[i, k], fwd_send.at[i, k], fwd_recv.at[i, k], (z, partner)
                ).start()

    margin_copies = scatter_middle(
        margin_pairs, margin, margin_partner, margin_sum, margin_in, ms_send, ms_recv
    )

    for chunk in range(early, chunks):
        grad_copies.append(send_gradients(chunk))

    for k in range(per):
        mine = c == (k * n_outer + z) % 2

        @pl.when(jnp.logical_not(mine))
        def _():
            for i in range(2):
                remote(
                    moments.at[i, k], moments.at[i, k], fwd_send.at[i, k], fwd_recv.at[i, k], (z, partner)
                ).wait_recv()

    margin_rows = scatter_end(margin_copies, margin_sum, margin_in)
    old = moments[...].reshape(2, per * blk, cols)
    rotated[0] = jnp.dot(margin_rows, old[0], precision=lax.Precision.HIGHEST, preferred_element_type=F32)
    rotated[1] = jnp.dot(
        margin_rows * margin_rows, old[1], precision=lax.Precision.HIGHEST, preferred_element_type=F32
    )
    rot_copies = []
    for j in range(1, n_outer):
        copy = remote(
            rotated, rotated_in.at[j], rot_send.at[j], rot_recv.at[j], (lax.rem(z + j, n_outer), d)
        )
        copy.start()
        rot_copies.append(copy)

    load_own.wait()
    for chunk in range(chunks):
        for copy in grad_copies[chunk]:
            copy.wait_recv()
        part_rows = slice(chunk * tall, (chunk + 1) * tall)
        total = grads[0, part_rows].astype(F32)
        for j in range(1, n_dev):
            total = total + grads[j, part_rows].astype(F32)
        high = total.astype(BF16)
        low = (total - high.astype(F32)).astype(BF16)
        both = jnp.concatenate([high, low], axis=1)
        for s in range(0, rank, width):
            part = contract_rows(basis[part_rows, s : s + width], both)
            part = (part[:, :cols] + part[:, cols:]).reshape(width // blk, blk, cols)
            blocks = slice(s // blk, (s + width) // blk)
            projected[blocks] = part if chunk == 0 else projected[blocks] + part
    half = blk // parts
    views = [slice(h * half, (h + 1) * half) for h in range(parts)]
    pairs = [
        scatter_start(projected.at[:, v], projected_partner.at[:, v], pp_send.at[h], pp_recv.at[h])
        for h, v in enumerate(views)
    ]
    copies = [
        scatter_middle(
            pairs[h],
            projected.at[:, v],
            projected_partner.at[:, v],
            projected_sum.at[:, v],
            projected_in.at[:, v],
            ps_send.at[h],
            ps_recv.at[h],
        )
        for h, v in enumerate(views)
    ]
    blk_copies = []
    for h, v in enumerate(views):
        block[v] = scatter_end(copies[h], projected_sum.at[:, v], projected_in.at[:, v])
        for j in range(1, n_outer):
            copy = remote(
                block.at[v],
                block_in.at[j, v],
                blk_send.at[h, j],
                blk_recv.at[h, j],
                (lax.rem(z + j, n_outer), d),
            )
            copy.start()
            blk_copies.append(copy)
    for copy in rot_copies:
        copy.wait_recv()
    dir_copies = []
    for h, v in enumerate(views):
        for copy in blk_copies[h * (n_outer - 1) : (h + 1) * (n_outer - 1)]:
            copy.wait_recv()
        first = rotated[0, v]
        second = rotated[1, v]
        proj = block[v]
        for j in range(1, n_outer):
            first = first + rotated_in[j, 0, v]
            second = second + rotated_in[j, 1, v]
            proj = proj + block_in[j, v]
        mean = beta_mean * first + (1.0 - beta_mean) * proj
        square = beta_square * second + (1.0 - beta_square) * proj * proj
        m_new[v] = mean
        v_new[v] = square
        direction[d, v] = (mean / bias_mean / (jnp.sqrt(square / bias_square) + adam_epsilon)).astype(BF16)
        for j in range(1, n_dev):
            copy = remote(
                direction.at[d, v],
                direction.at[d, v],
                dir_send.at[h, j],
                dir_recv.at[h, j],
                (z, lax.rem(d + j, n_dev)),
            )
            copy.start()
            dir_copies.append(copy)
    load_weight.wait()
    for copy in dir_copies:
        copy.wait_recv()
    directions = direction[...].reshape(rank, cols)
    tall = min(rows, 256)
    for s in range(0, rows, tall):
        update = jnp.dot(basis[s : s + tall, :], directions, preferred_element_type=F32)
        new_weight[s : s + tall, :] = weights[s : s + tall, :] - step_scale * update

    for k in range(per):
        owner = k * n_outer + z
        mine = c == owner % 2

        @pl.when(d == owner)
        def _():
            for copy in moment_copies(k, owner):
                copy.wait_send()

        @pl.when(mine)
        def _():
            for i in range(2):
                remote(
                    moments.at[i, k], moments.at[i, k], fwd_send.at[i, k], fwd_recv.at[i, k], (z, partner)
                ).wait_send()

    for copy in sum(grad_copies, []) + rot_copies + blk_copies + dir_copies:
        copy.wait_send()
    for group in [margin_pairs] + pairs:
        for _, _, copy in group:
            copy.wait_send()
    for group in [margin_copies] + copies:
        for _, copy in group:
            copy.wait_send()

class Copies:
    def __init__(self, send, recv):
        self.send, self.recv, self.started = send, recv, []

    def start(self, src, dst, to):
        i = len(self.started)
        copy = pltpu.make_async_remote_copy(
            src_ref=src,
            dst_ref=dst,
            send_sem=self.send.at[i],
            recv_sem=self.recv.at[i],
            device_id=to,
            device_id_type=MESH,
        )
        copy.start()
        self.started.append(copy)
        return copy


def square_kernel(
    n_outer,
    n_dev,
    partials,
    p_old,
    p_new,
    weight,
    m_old,
    v_old,
    new_weight,
    m_new,
    v_new,
    own,
    pair,
    plane_own,
    plane_pair,
    far_sum,
    relay_in,
    direct_out,
    direct_in,
    merged,
    merged_in,
    terms,
    basis,
    basis_old,
    weights,
    moments,
    margin,
    margin_partner,
    margin_sum,
    margin_in,
    rotated,
    rotated_in,
    projected,
    projected_partner,
    projected_sum,
    projected_in,
    block,
    block_in,
    direction,
    moments_new,
    load_sem,
    old_sem,
    own_sem,
    mom_send,
    mom_recv,
    fwd_send,
    fwd_recv,
    send_sem,
    recv_sem,
    merge_send,
    merge_recv,
    line_sem,
):
    z = lax.axis_index("outer")
    d = lax.axis_index("dev")
    q = d // 2
    c = d % 2
    partner = q * 2 + 1 - c
    side = q + 1 - 2 * (q % 2)
    over = lax.rem(q + 2, 4)
    far = lax.rem(side + 2, 4)
    chips = (far, side, over, q)
    rows, cols = weight.shape
    rank = p_new.shape[1]
    blk = rank // n_dev
    sub = blk // n_outer
    fine = sub // pieces
    per = n_dev // n_outer
    few = shared_rows(rows)
    many = rows - 2 * few
    kept = few + many
    mate = z + 1 - 2 * (z % 2)
    kept_at = (z % 2) * kept
    given_at = (mate % 2) * kept
    copies = Copies(send_sem, recv_sem)
    above = (2 * n_outer - 2 - z) // n_outer
    below = (z + n_outer - 1) // n_outer

    def signal_line(sem):
        @pl.when(z > 0)
        def _():
            pl.semaphore_signal(sem, inc=1, device_id=(z - 1, d), device_id_type=MESH)

        @pl.when(z < n_outer - 1)
        def _():
            pl.semaphore_signal(sem, inc=1, device_id=(z + 1, d), device_id_type=MESH)

    def pass_along(steps):
        for r in steps:
            pl.semaphore_wait(line_sem.at[r], above + below)
            if r + 1 < n_outer - 2:
                signal_line(line_sem.at[r + 1])

    barrier = pltpu.get_barrier_semaphore()
    for to in (partner, 2 * side + c, 2 * over + c):
        pl.semaphore_signal(barrier, inc=1, device_id=(z, to), device_id_type=MESH)
    pl.semaphore_signal(barrier, inc=1, device_id=(mate, partner), device_id_type=MESH)
    signal_line(barrier)

    def rows_of(to, start, count):
        return partials.at[pl.ds(pl.multiple_of(to * rows + start, 16), count)]

    parts_of = ((kept_at, 0, few), (few, few, many))
    own_loads = [
        [
            pltpu.make_async_copy(rows_of(2 * k + c, start, count), own.at[i, at : at + count], own_sem.at[i, j])
            for j, (start, at, count) in enumerate(parts_of)
        ]
        for i, k in enumerate(chips)
    ]
    for i in range(3):
        for load in own_loads[i]:
            load.start()
    load_new = pltpu.make_async_copy(p_new, basis, load_sem.at[0])
    load_new.start()
    old_loads = [
        pltpu.make_async_copy(
            p_old.at[:, pl.ds(pl.multiple_of((k * n_outer + z) * blk, blk), blk)],
            basis_old.at[:, k * blk : (k + 1) * blk],
            old_sem.at[k],
        )
        for k in range(per)
    ]
    for load in old_loads:
        load.start()
    for load in own_loads[3]:
        load.start()
    load_weight = pltpu.make_async_copy(weight, weights, load_sem.at[1])
    load_weight.start()

    pl.semaphore_wait(barrier, 4 + above + below)

    def moment_copy(i, k, j):
        return pltpu.make_async_remote_copy(
            src_ref=(m_old, v_old)[i],
            dst_ref=moments.at[i, k],
            send_sem=mom_send.at[i, k, j],
            recv_sem=mom_recv.at[i, k],
            device_id=(z, 2 * (side, over)[j] + c),
            device_id_type=MESH,
        )

    def moment_relay(i, k):
        return pltpu.make_async_remote_copy(
            src_ref=moments.at[i, k],
            dst_ref=moments.at[i, k],
            send_sem=mom_send.at[i, k, 2],
            recv_sem=mom_recv.at[i, k],
            device_id=(z, 2 * (over, side)[i] + c),
            device_id_type=MESH,
        )

    def moments_from(k, chip):
        owner = k * n_outer + z
        return jnp.logical_and(c == owner % 2, owner // 2 == chip)

    def moment_load(i, k):
        return pltpu.make_async_copy((m_old, v_old)[i], moments.at[i, k], load_sem.at[2 + i])

    def moment_forward(i, k):
        return pltpu.make_async_remote_copy(
            src_ref=moments.at[i, k],
            dst_ref=moments.at[i, k],
            send_sem=fwd_send.at[i, k],
            recv_sem=fwd_recv.at[i, k],
            device_id=(z, partner),
            device_id_type=MESH,
        )

    for k in range(per):

        @pl.when(d == k * n_outer + z)
        def _():
            for j in range(2):
                for i in range(2):
                    moment_copy(i, k, j).start()
            for i in range(2):
                moment_load(i, k).start()

    pairs, crossed = [], []
    for i, k in enumerate(chips):
        pairs.append(
            [
                copies.start(rows_of(2 * k + 1 - c, start, count), pair.at[i, at : at + count], (z, partner))
                for start, at, count in parts_of
            ]
        )
        crossed.append(
            [
                copies.start(rows_of(2 * k + c, given_at, few), plane_own.at[i], (mate, d)),
                copies.start(rows_of(2 * k + 1 - c, given_at, few), plane_pair.at[i], (mate, partner)),
            ]
        )
    if n_outer > 2:
        signal_line(line_sem.at[0])

    def chip_sum(i, at):
        return own[i, at].astype(F32) + pair[i, at].astype(F32)

    def plane_sum(i, at):
        return chip_sum(i, at) + (plane_own[i, at].astype(F32) + plane_pair[i, at].astype(F32))

    def arrive(i, group):
        pairs[i][group].wait_recv()
        own_loads[i][group].wait()
        if group == 0:
            for copy in crossed[i]:
                copy.wait_recv()

    def rows_at(group, h):
        start, count = ((0, few // 2), (few, many // 2))[group]
        return slice(start + h * count, start + (h + 1) * count)

    sums = (plane_sum, chip_sum)
    merging = Copies(merge_send, merge_recv)
    relays, directs, merges = {}, {}, {}

    def send_far(group):
        arrive(0, group)
        for h, chip in enumerate((side, over)):
            at = rows_at(group, h)
            far_sum[at] = sums[group](0, at).astype(BF16)
            relays[group, h] = copies.start(far_sum.at[at], relay_in.at[at], (z, 2 * chip + c))

    def send_direct(group):
        for h, chip in enumerate((side, over)):
            arrive(1 + h, group)
            at = rows_at(group, h)
            direct_out[at] = sums[group](1 + h, at).astype(BF16)
            directs[group, h] = copies.start(direct_out.at[at], direct_in.at[at], (z, 2 * chip + c))

    def send_merged(group):
        for h, (i, chip) in enumerate(((2, over), (1, side))):
            at = rows_at(group, h)
            relays[group, h].wait_recv()
            merged[at] = sums[group](i, at) + relay_in[at].astype(F32)
            merges[group, h] = merging.start(merged.at[at], merged_in.at[at], (z, 2 * chip + c))

    send_far(1)
    send_direct(1)

    load_new.wait()
    for load in old_loads:
        load.wait()

    def chip_ranks(k):
        return pl.ds(pl.multiple_of(k * 2 * blk, 2 * blk), 2 * blk)

    margin_pairs = []
    for i, k in enumerate(chips):
        part = contract_rows(basis[:, chip_ranks(k)], basis_old[...])
        margin[i] = part.reshape(2, blk, per * blk)
        margin_pairs.append(copies.start(margin.at[i, 1 - c], margin_partner.at[i], (z, partner)))

    send_far(0)
    send_merged(1)
    for i in range(4):
        margin_pairs[i].wait_recv()
        margin_sum[i] = margin[i, c] + margin_partner[i]

    for k in range(per):
        for i, chip in enumerate((side, over)):

            @pl.when(moments_from(k, chip))
            def _():
                moment_copy(0, k, 0).wait_recv()
                moment_copy(1, k, 0).wait_recv()
                moment_relay(i, k).start()

    send_direct(0)
    send_merged(0)
    for copy in merging.started:
        copy.wait_send()
    margin_copies = [
        copies.start(margin_sum.at[i], margin_in.at[i], (z, 2 * k + c)) for i, k in enumerate(chips[:3])
    ]

    for group in (1, 0):
        arrive(3, group)
        for h in range(2):
            at = rows_at(group, h)
            directs[group, h].wait_recv()
            total = sums[group](3, at) + direct_in[at].astype(F32)
            merges[group, h].wait_recv()
            total = total + merged_in[at]
            high = total.astype(BF16)
            terms[at, :cols] = high
            terms[at, cols:] = (total - high.astype(F32)).astype(BF16)

    projected_pairs = []
    for i, k in enumerate(chips):
        ranks = chip_ranks(k)
        part = contract_rows(basis[few:kept, ranks], terms[few:])
        part = part + contract_rows(basis[pl.ds(pl.multiple_of(kept_at, 16), few), ranks], terms[:few])
        part = (part[:, :cols] + part[:, cols:]).reshape(2, n_outer, pieces, fine, cols)
        for h in range(pieces):
            projected[h, i] = part[:, :, h]
            projected_pairs.append(
                copies.start(projected.at[h, i, 1 - c], projected_partner.at[h, i], (z, partner))
            )
    projected_copies = []
    for h in range(pieces):
        for i, k in enumerate(chips):
            projected_pairs[i * pieces + h].wait_recv()
            projected_sum[h, i] = projected[h, i, c] + projected_partner[h, i]
            if i < 3:
                projected_copies.append(
                    copies.start(projected_sum.at[h, i], projected_in.at[h, i], (z, 2 * k + c))
                )

    for k in range(per):
        owner = k * n_outer + z
        mine = c == owner % 2

        @pl.when(d == owner)
        def _():
            for i in range(2):
                moment_load(i, k).wait()

        @pl.when(moments_from(k, far))
        def _():
            for i in range(2):
                moment_copy(i, k, 0).wait_recv()

        @pl.when(mine)
        def _():
            for i in range(2):
                moment_forward(i, k).start()

        @pl.when(jnp.logical_not(mine))
        def _():
            for i in range(2):
                moment_forward(i, k).wait_recv()

    for copy in margin_copies:
        copy.wait_recv()
    margin_rows = margin_sum[3] + margin_in[0] + margin_in[1] + margin_in[2]
    old = moments[...].reshape(2, per * blk, cols)
    for i, rows_in in enumerate((margin_rows, margin_rows * margin_rows)):
        turned = jnp.dot(rows_in, old[i], precision=lax.Precision.HIGHEST, preferred_element_type=F32)
        rotated[:, i] = turned.reshape(n_outer, sub, cols)
    pass_along(range(n_outer - 2))
    planes = [lax.rem(z + j, n_outer) for j in range(1, n_outer)]
    rot_copies = [
        copies.start(rotated.at[to], rotated_in.at[j], (to, d)) for j, to in enumerate(planes)
    ]

    block_copies = []
    for h in range(pieces):
        for copy in projected_copies[3 * h : 3 * h + 3]:
            copy.wait_recv()
        block[h] = projected_sum[h, 3] + projected_in[h, 0] + projected_in[h, 1] + projected_in[h, 2]
        for j, to in enumerate(planes):
            block_copies.append(copies.start(block.at[h, to], block_in.at[h, j], (to, d)))

    for copy in rot_copies:
        copy.wait_recv()
    first, second = rotated[z, 0], rotated[z, 1]
    for j in range(n_outer - 1):
        first = first + rotated_in[j, 0]
        second = second + rotated_in[j, 1]
    for h in range(pieces):
        at = slice(h * fine, (h + 1) * fine)
        proj = block[h, z]
        for j in range(n_outer - 1):
            block_copies[h * (n_outer - 1) + j].wait_recv()
            proj = proj + block_in[h, j]
        mean = beta_mean * first[at] + (1.0 - beta_mean) * proj
        square = beta_square * second[at] + (1.0 - beta_square) * proj * proj
        moments_new[z, 0, at] = mean
        moments_new[z, 1, at] = square
        direction[d, z, at] = (
            mean / bias_mean / (jnp.sqrt(square / bias_square) + adam_epsilon)
        ).astype(BF16)

    spread = []
    for i, k in enumerate(chips):
        group = []
        for to in planes + [z]:
            if i == 3 and to is z:
                continue
            group.append(copies.start(direction.at[d, z], direction.at[d, z], (to, 2 * k + c)))
        spread.append(group)
    moment_spread = [copies.start(moments_new.at[z], moments_new.at[z], (to, d)) for to in planes]
    forwards = []
    for i in (3, 1, 2, 0):
        for copy in spread[i]:
            copy.wait_recv()
        mine = direction.at[2 * chips[i] + c]
        forwards.append(copies.start(mine, mine, (z, partner)))
    load_weight.wait()
    for copy in forwards:
        copy.wait_recv()
    directions = direction[...].reshape(rank, cols)
    tall = min(rows, 256)
    for s in range(0, rows, tall):
        update = jnp.dot(basis[s : s + tall, :], directions, preferred_element_type=F32)
        new_weight[s : s + tall, :] = weights[s : s + tall, :] - step_scale * update
    for copy in moment_spread:
        copy.wait_recv()
    m_new[...] = moments_new[:, 0].reshape(blk, cols)
    v_new[...] = moments_new[:, 1].reshape(blk, cols)

    for k in range(per):
        owner = k * n_outer + z

        @pl.when(d == owner)
        def _():
            for j in range(2):
                for i in range(2):
                    moment_copy(i, k, j).wait_send()

        for i, chip in enumerate((side, over)):

            @pl.when(moments_from(k, chip))
            def _():
                moment_relay(i, k).wait_send()

        @pl.when(c == owner % 2)
        def _():
            for i in range(2):
                moment_forward(i, k).wait_send()

    for copy in copies.started:
        copy.wait_send()


def shared_rows(rows):
    top, bottom = shared_part
    return rows * top // bottom // 32 * 32


def square_scratch(n_outer, n_dev, rows, cols, rank):
    blk = rank // n_dev
    sub = blk // n_outer
    fine = sub // pieces
    per = n_dev // n_outer
    span = per * blk
    dma = pltpu.SemaphoreType.DMA
    few = shared_rows(rows)
    kept = rows - few
    count = 50 + 15 * pieces + 6 * n_outer
    return [
        pltpu.VMEM((4, kept, cols), BF16),
        pltpu.VMEM((4, kept, cols), BF16),
        pltpu.VMEM((4, few, cols), BF16),
        pltpu.VMEM((4, few, cols), BF16),
        pltpu.VMEM((kept, cols), BF16),
        pltpu.VMEM((kept, cols), BF16),
        pltpu.VMEM((kept, cols), BF16),
        pltpu.VMEM((kept, cols), BF16),
        pltpu.VMEM((kept, cols), F32),
        pltpu.VMEM((kept, cols), F32),
        pltpu.VMEM((kept, 2 * cols), BF16),
        pltpu.VMEM((rows, rank), BF16),
        pltpu.VMEM((rows, span), BF16),
        pltpu.VMEM((rows, cols), F32),
        pltpu.VMEM((2, per, blk, cols), F32),
        pltpu.VMEM((4, 2, blk, span), F32),
        pltpu.VMEM((4, blk, span), F32),
        pltpu.VMEM((4, blk, span), F32),
        pltpu.VMEM((3, blk, span), F32),
        pltpu.VMEM((n_outer, 2, sub, cols), F32),
        pltpu.VMEM((n_outer - 1, 2, sub, cols), F32),
        pltpu.VMEM((pieces, 4, 2, n_outer, fine, cols), F32),
        pltpu.VMEM((pieces, 4, n_outer, fine, cols), F32),
        pltpu.VMEM((pieces, 4, n_outer, fine, cols), F32),
        pltpu.VMEM((pieces, 3, n_outer, fine, cols), F32),
        pltpu.VMEM((pieces, n_outer, fine, cols), F32),
        pltpu.VMEM((pieces, n_outer - 1, fine, cols), F32),
        pltpu.VMEM((n_dev, n_outer, sub, cols), BF16),
        pltpu.VMEM((n_outer, 2, sub, cols), F32),
        dma((4,)),
        dma((per,)),
        dma((4, 2)),
        dma((2, per, 3)),
        dma((2, per)),
        dma((2, per)),
        dma((2, per)),
        dma((count,)),
        dma((count,)),
        dma((4,)),
        dma((4,)),
        pltpu.SemaphoreType.REGULAR((max(n_outer - 2, 1),)),
    ]


def plain_scratch(n_outer, n_dev, rows, cols, rank):
    blk = rank // n_dev
    per = n_dev // n_outer
    span = per * blk
    n_chip = n_dev // 2
    dma = pltpu.SemaphoreType.DMA
    return (
        [
            pltpu.VMEM((n_dev, rows, cols), BF16),
            pltpu.VMEM((rows, rank), BF16),
            pltpu.VMEM((rows, span), BF16),
            pltpu.VMEM((rows, cols), F32),
            pltpu.VMEM((2, per, blk, cols), F32),
            pltpu.VMEM((n_dev, blk, span), F32),
            pltpu.VMEM((n_chip, blk, span), F32),
            pltpu.VMEM((n_chip, blk, span), F32),
            pltpu.VMEM((n_chip, blk, span), F32),
            pltpu.VMEM((2, blk, cols), F32),
            pltpu.VMEM((n_outer, 2, blk, cols), F32),
            pltpu.VMEM((n_dev, blk, cols), F32),
            pltpu.VMEM((n_chip, blk, cols), F32),
            pltpu.VMEM((n_chip, blk, cols), F32),
            pltpu.VMEM((n_chip, blk, cols), F32),
            pltpu.VMEM((blk, cols), F32),
            pltpu.VMEM((n_outer, blk, cols), F32),
            pltpu.VMEM((n_dev, blk, cols), BF16),
            dma((6,)),
            dma((per,)),
            dma((chunks, n_dev)),
            dma((chunks, n_dev)),
            dma((2, per, n_chip)),
            dma((2, per)),
            dma((2, per)),
            dma((2, per)),
        ]
        + [dma((n_chip,))] * 4
        + [dma((n_outer,))] * 2
        + [dma((parts, n_chip))] * 4
        + [dma((parts, n_outer))] * 2
        + [dma((parts, n_dev))] * 2
    )


def hand_over(weight_in, m_in, v_in, weight_out, m_out, v_out):
    weight_out[...] = weight_in[...]
    m_out[...] = m_in[...]
    v_out[...] = v_in[...]


def on_device(n_outer, n_dev, partials, p_old, p_new, weight, m_old, v_old):
    rows, cols = weight.shape
    rank = p_new.shape[1]
    blk = rank // n_dev
    per = n_dev // n_outer
    span = per * blk
    n_chip = n_dev // 2
    squared = n_chip == 4 and n_dev % n_outer == 0 and n_outer % 2 == 0 and rows % 64 == 0 and blk % (16 * pieces * n_outer) == 0
    if blk % 128 and not squared:
        z = lax.axis_index("outer")
        p_old = jnp.concatenate(
            [
                lax.dynamic_slice_in_dim(p_old, (k * n_outer + z) * blk, blk, axis=1)
                for k in range(per)
            ],
            axis=1,
        )
    anywhere = pl.BlockSpec(memory_space=pltpu.HBM)
    vmem = pl.BlockSpec(memory_space=pltpu.VMEM)
    if squared:
        body, scratch = square_kernel, square_scratch(n_outer, n_dev, rows, cols, rank)
    else:
        body, scratch = kernel, plain_scratch(n_outer, n_dev, rows, cols, rank)
    operands = (partials[0], p_old, p_new, weight, m_old, v_old)
    results = pl.pallas_call(
        functools.partial(body, n_outer, n_dev),
        out_shape=(
            jax.ShapeDtypeStruct((rows, cols), F32),
            jax.ShapeDtypeStruct((blk, cols), F32),
            jax.ShapeDtypeStruct((blk, cols), F32),
        ),
        in_specs=[anywhere] * 6,
        out_specs=(vmem, vmem, vmem),
        scratch_shapes=scratch,
        compiler_params=pltpu.CompilerParams(
            collective_id=0, has_side_effects=True, vmem_limit_bytes=vmem_limit
        ),
    )(*[pltpu.with_memory_space_constraint(a, pltpu.HBM) for a in operands])
    return pl.pallas_call(
        hand_over,
        out_shape=tuple(jax.ShapeDtypeStruct(r.shape, r.dtype) for r in results),
        in_specs=[vmem] * 3,
        out_specs=(vmem,) * 3,
        compiler_params=pltpu.CompilerParams(vmem_limit_bytes=finish_limit),
    )(*results)


def solution(mesh):
    in_specs = (
        P(("outer", "dev"), None, None),
        P("dev", None),
        P("dev", None),
        P("dev", None),
        P("dev", None),
        P("dev", None),
    )
    out_specs = (P("dev", None), P("dev", None), P("dev", None))
    return jax.shard_map(
        functools.partial(on_device, mesh.shape["outer"], mesh.shape["dev"]),
        mesh=mesh,
        in_specs=in_specs,
        out_specs=out_specs,
        check_vma=False,
    )
```

```python
import functools

import jax
import jax.numpy as jnp
from jax import lax
from jax.experimental import pallas as pl
from jax.experimental.pallas import tpu as pltpu
from jax.sharding import PartitionSpec as P

beta_mean = 0.9
beta_square = 0.95
bias_mean = 0.9999734386011124
bias_square = 0.9940794707796659
adam_epsilon = 1e-08
step_scale = 0.5

chunks = 2
early = 1
parts = 2
pieces = 2
shared_part = (3, 16)
vmem_limit = 50331648
finish_limit = 4194304

MESH = pl.DeviceIdType.MESH
F32 = jnp.float32
BF16 = jnp.bfloat16


def contract_rows(a, b):
    return lax.dot_general(a, b, (((0,), (0,)), ((), ())), preferred_element_type=F32)


def kernel(
    n_outer,
    n_dev,
    partials,
    p_old,
    p_new,
    weight,
    m_old,
    v_old,
    new_weight,
    m_new,
    v_new,
    grads,
    basis,
    basis_old,
    weights,
    moments,
    margin,
    margin_partner,
    margin_sum,
    margin_in,
    rotated,
    rotated_in,
    projected,
    projected_partner,
    projected_sum,
    projected_in,
    block,
    block_in,
    direction,
    load_sem,
    old_sem,
    grad_send,
    grad_recv,
    mom_send,
    mom_recv,
    fwd_send,
    fwd_recv,
    mp_send,
    mp_recv,
    ms_send,
    ms_recv,
    rot_send,
    rot_recv,
    pp_send,
    pp_recv,
    ps_send,
    ps_recv,
    blk_send,
    blk_recv,
    dir_send,
    dir_recv,
):
    z = lax.axis_index("outer")
    d = lax.axis_index("dev")
    n_chip = n_dev // 2
    q = d // 2
    c = d % 2
    partner = q * 2 + 1 - c
    rows, cols = weight.shape
    rank = p_new.shape[1]
    blk = rank // n_dev
    per = n_dev // n_outer

    def remote(src, dst, send, recv, where):
        return pltpu.make_async_remote_copy(
            src_ref=src, dst_ref=dst, send_sem=send, recv_sem=recv, device_id=where, device_id_type=MESH
        )

    barrier = pltpu.get_barrier_semaphore()
    for j in range(1, n_dev):
        pl.semaphore_signal(barrier, inc=1, device_id=(z, lax.rem(d + j, n_dev)), device_id_type=MESH)
    for j in range(1, n_outer):
        pl.semaphore_signal(barrier, inc=1, device_id=(lax.rem(z + j, n_outer), d), device_id_type=MESH)

    load_new = pltpu.make_async_copy(p_new, basis, load_sem.at[0])
    load_new.start()
    if p_old.shape[1] == per * blk:
        old_loads = [pltpu.make_async_copy(p_old, basis_old, old_sem.at[0])]
    else:
        old_loads = [
            pltpu.make_async_copy(
                p_old.at[:, pl.ds(pl.multiple_of((k * n_outer + z) * blk, blk), blk)],
                basis_old.at[:, k * blk : (k + 1) * blk],
                old_sem.at[k],
            )
            for k in range(per)
        ]
    for load in old_loads:
        load.start()
    load_weight = pltpu.make_async_copy(weight, weights, load_sem.at[2])
    load_weight.start()
    load_own = pltpu.make_async_copy(
        partials.at[pl.ds(pl.multiple_of(d * rows, rows), rows)], grads.at[0], load_sem.at[3]
    )
    load_own.start()

    pl.semaphore_wait(barrier, n_dev - 1 + n_outer - 1)

    def moment_copies(k, owner):
        copies = []
        for j in range(1, n_chip):
            to = (z, lax.rem(q + j, n_chip) * 2 + c)
            for i, src in enumerate((m_old, v_old)):
                copies.append(remote(src, moments.at[i, k], mom_send.at[i, k, j], mom_recv.at[i, k], to))
        return copies

    for k in range(per):
        owner = k * n_outer + z

        @pl.when(d == owner)
        def _():
            for copy in moment_copies(k, owner):
                copy.start()
            for i, src in enumerate((m_old, v_old)):
                pltpu.make_async_copy(src, moments.at[i, k], load_sem.at[4 + i]).start()

    tall = rows // chunks

    def send_gradients(chunk):
        copies = []
        for j in range(1, n_dev):
            to = lax.rem(d + j, n_dev)
            copy = remote(
                partials.at[pl.ds(pl.multiple_of(to * rows + chunk * tall, tall), tall)],
                grads.at[j, chunk * tall : (chunk + 1) * tall],
                grad_send.at[chunk, j],
                grad_recv.at[chunk, j],
                (z, to),
            )
            copy.start()
            copies.append(copy)
        return copies

    grad_copies = [send_gradients(chunk) for chunk in range(early)]

    load_new.wait()
    for load in old_loads:
        load.wait()
    width = min(rank, 256)
    for s in range(0, rank, width):
        part = contract_rows(basis[:, s : s + width], basis_old[...])
        margin[s // blk : (s + width) // blk] = part.reshape(width // blk, blk, part.shape[1])

    def scatter_start(val, prt, send, recv):
        copies = []
        for j in list(range(1, n_chip)) + [0]:
            k = lax.rem(q + j, n_chip)
            copy = remote(val.at[2 * k + 1 - c], prt.at[j], send.at[j], recv.at[j], (z, partner))
            copy.start()
            copies.append((j, k, copy))
        return copies

    def scatter_middle(pairs, val, prt, tot, arr, send, recv):
        copies = []
        for j, k, pair in pairs:
            pair.wait_recv()
            tot[j] = val[2 * k + c] + prt[j]
            if j:
                copy = remote(tot.at[j], arr.at[j], send.at[j], recv.at[j], (z, 2 * k + c))
                copy.start()
                copies.append((j, copy))
        return copies

    def scatter_end(copies, tot, arr):
        total = tot[0]
        for j, copy in copies:
            copy.wait_recv()
            total = total + arr[j]
        return total

    margin_pairs = scatter_start(margin, margin_partner, mp_send, mp_recv)

    for k in range(per):
        owner = k * n_outer + z
        mine = c == owner % 2

        @pl.when(d == owner)
        def _():
            for i, src in enumerate((m_old, v_old)):
                pltpu.make_async_copy(src, moments.at[i, k], load_sem.at[4 + i]).wait()

        @pl.when(jnp.logical_and(mine, d != owner))
        def _():
            for i, src in enumerate((m_old, v_old)):
                remote(src, moments.at[i, k], mom_send.at[i, k, 0], mom_recv.at[i, k], (z, d)).wait_recv()

        @pl.when(mine)
        def _():
            for i in range(2):
                remote(
                    moments.at[i, k], moments.at[i, k], fwd_send.at[i, k], fwd_recv.at[i, k], (z, partner)
                ).start()

    margin_copies = scatter_middle(
        margin_pairs, margin, margin_partner, margin_sum, margin_in, ms_send, ms_recv
    )

    for chunk in range(early, chunks):
        grad_copies.append(send_gradients(chunk))

    for k in range(per):
        mine = c == (k * n_outer + z) % 2

        @pl.when(jnp.logical_not(mine))
        def _():
            for i in range(2):
                remote(
                    moments.at[i, k], moments.at[i, k], fwd_send.at[i, k], fwd_recv.at[i, k], (z, partner)
                ).wait_recv()

    margin_rows = scatter_end(margin_copies, margin_sum, margin_in)
    old = moments[...].reshape(2, per * blk, cols)
    rotated[0] = jnp.dot(margin_rows, old[0], precision=lax.Precision.HIGHEST, preferred_element_type=F32)
    rotated[1] = jnp.dot(
        margin_rows * margin_rows, old[1], precision=lax.Precision.HIGHEST, preferred_element_type=F32
    )
    rot_copies = []
    for j in range(1, n_outer):
        copy = remote(
            rotated, rotated_in.at[j], rot_send.at[j], rot_recv.at[j], (lax.rem(z + j, n_outer), d)
        )
        copy.start()
        rot_copies.append(copy)

    load_own.wait()
    for chunk in range(chunks):
        for copy in grad_copies[chunk]:
            copy.wait_recv()
        part_rows = slice(chunk * tall, (chunk + 1) * tall)
        total = grads[0, part_rows].astype(F32)
        for j in range(1, n_dev):
            total = total + grads[j, part_rows].astype(F32)
        high = total.astype(BF16)
        low = (total - high.astype(F32)).astype(BF16)
        both = jnp.concatenate([high, low], axis=1)
        for s in range(0, rank, width):
            part = contract_rows(basis[part_rows, s : s + width], both)
            part = (part[:, :cols] + part[:, cols:]).reshape(width // blk, blk, cols)
            blocks = slice(s // blk, (s + width) // blk)
            projected[blocks] = part if chunk == 0 else projected[blocks] + part
    half = blk // parts
    views = [slice(h * half, (h + 1) * half) for h in range(parts)]
    pairs = [
        scatter_start(projected.at[:, v], projected_partner.at[:, v], pp_send.at[h], pp_recv.at[h])
        for h, v in enumerate(views)
    ]
    copies = [
        scatter_middle(
            pairs[h],
            projected.at[:, v],
            projected_partner.at[:, v],
            projected_sum.at[:, v],
            projected_in.at[:, v],
            ps_send.at[h],
            ps_recv.at[h],
        )
        for h, v in enumerate(views)
    ]
    blk_copies = []
    for h, v in enumerate(views):
        block[v] = scatter_end(copies[h], projected_sum.at[:, v], projected_in.at[:, v])
        for j in range(1, n_outer):
            copy = remote(
                block.at[v],
                block_in.at[j, v],
                blk_send.at[h, j],
                blk_recv.at[h, j],
                (lax.rem(z + j, n_outer), d),
            )
            copy.start()
            blk_copies.append(copy)
    for copy in rot_copies:
        copy.wait_recv()
    dir_copies = []
    for h, v in enumerate(views):
        for copy in blk_copies[h * (n_outer - 1) : (h + 1) * (n_outer - 1)]:
            copy.wait_recv()
        first = rotated[0, v]
        second = rotated[1, v]
        proj = block[v]
        for j in range(1, n_outer):
            first = first + rotated_in[j, 0, v]
            second = second + rotated_in[j, 1, v]
            proj = proj + block_in[j, v]
        mean = beta_mean * first + (1.0 - beta_mean) * proj
        square = beta_square * second + (1.0 - beta_square) * proj * proj
        m_new[v] = mean
        v_new[v] = square
        direction[d, v] = (mean / bias_mean / (jnp.sqrt(square / bias_square) + adam_epsilon)).astype(BF16)
        for j in range(1, n_dev):
            copy = remote(
                direction.at[d, v],
                direction.at[d, v],
                dir_send.at[h, j],
                dir_recv.at[h, j],
                (z, lax.rem(d + j, n_dev)),
            )
            copy.start()
            dir_copies.append(copy)
    load_weight.wait()
    for copy in dir_copies:
        copy.wait_recv()
    directions = direction[...].reshape(rank, cols)
    tall = min(rows, 256)
    for s in range(0, rows, tall):
        update = jnp.dot(basis[s : s + tall, :], directions, preferred_element_type=F32)
        new_weight[s : s + tall, :] = weights[s : s + tall, :] - step_scale * update

    for k in range(per):
        owner = k * n_outer + z
        mine = c == owner % 2

        @pl.when(d == owner)
        def _():
            for copy in moment_copies(k, owner):
                copy.wait_send()

        @pl.when(mine)
        def _():
            for i in range(2):
                remote(
                    moments.at[i, k], moments.at[i, k], fwd_send.at[i, k], fwd_recv.at[i, k], (z, partner)
                ).wait_send()

    for copy in sum(grad_copies, []) + rot_copies + blk_copies + dir_copies:
        copy.wait_send()
    for group in [margin_pairs] + pairs:
        for _, _, copy in group:
            copy.wait_send()
    for group in [margin_copies] + copies:
        for _, copy in group:
            copy.wait_send()

class Copies:
    def __init__(self, send, recv):
        self.send, self.recv, self.started = send, recv, []

    def start(self, src, dst, to):
        i = len(self.started)
        copy = pltpu.make_async_remote_copy(
            src_ref=src,
            dst_ref=dst,
            send_sem=self.send.at[i],
            recv_sem=self.recv.at[i],
            device_id=to,
            device_id_type=MESH,
        )
        copy.start()
        self.started.append(copy)
        return copy


def square_kernel(
    n_outer,
    n_dev,
    partials,
    p_old,
    p_new,
    weight,
    m_old,
    v_old,
    new_weight,
    m_new,
    v_new,
    own,
    pair,
    plane_own,
    plane_pair,
    far_sum,
    relay_in,
    direct_out,
    direct_in,
    merged,
    merged_in,
    terms,
    basis,
    basis_old,
    weights,
    moments,
    margin,
    margin_partner,
    margin_sum,
    margin_in,
    margin_relay,
    rotated,
    rotated_in,
    projected,
    projected_partner,
    projected_sum,
    projected_in,
    block,
    block_in,
    direction,
    moments_new,
    load_sem,
    old_sem,
    own_sem,
    mom_send,
    mom_recv,
    fwd_send,
    fwd_recv,
    send_sem,
    recv_sem,
    merge_send,
    merge_recv,
    line_sem,
):
    z = lax.axis_index("outer")
    d = lax.axis_index("dev")
    q = d // 2
    c = d % 2
    partner = q * 2 + 1 - c
    side = q + 1 - 2 * (q % 2)
    over = lax.rem(q + 2, 4)
    far = lax.rem(side + 2, 4)
    chips = (far, side, over, q)
    rows, cols = weight.shape
    rank = p_new.shape[1]
    blk = rank // n_dev
    sub = blk // n_outer
    fine = sub // pieces
    few = shared_rows(rows)
    many = rows - 2 * few
    kept = few + many
    mate = z + 1 - 2 * (z % 2)
    odd = z % 2
    window = odd * few
    group_of = z // (n_outer // 2)
    turn = z % (n_outer // 2)
    few_at = odd * many
    many_at = few - window
    given_at = (1 - odd) * kept
    copies = Copies(send_sem, recv_sem)
    above = (2 * n_outer - 2 - z) // n_outer
    below = (z + n_outer - 1) // n_outer

    def signal_line(sem):
        @pl.when(z > 0)
        def _():
            pl.semaphore_signal(sem, inc=1, device_id=(z - 1, d), device_id_type=MESH)

        @pl.when(z < n_outer - 1)
        def _():
            pl.semaphore_signal(sem, inc=1, device_id=(z + 1, d), device_id_type=MESH)

    def pass_along(steps):
        for r in steps:
            pl.semaphore_wait(line_sem.at[r], above + below)
            if r + 1 < n_outer - 2:
                signal_line(line_sem.at[r + 1])

    barrier = pltpu.get_barrier_semaphore()
    for to in (partner, 2 * side + c, 2 * over + c):
        pl.semaphore_signal(barrier, inc=1, device_id=(z, to), device_id_type=MESH)
    pl.semaphore_signal(barrier, inc=1, device_id=(mate, partner), device_id_type=MESH)
    signal_line(barrier)

    def rows_of(to, start, count):
        return partials.at[pl.ds(pl.multiple_of(to * rows + start, 16), count)]

    own_loads = [
        pltpu.make_async_copy(rows_of(2 * k + c, window, kept), own.at[i], own_sem.at[i])
        for i, k in enumerate(chips)
    ]
    own_loads[0].start()
    pl.semaphore_wait(barrier, 4 + above + below)

    def moment_copy(i, j):
        return pltpu.make_async_remote_copy(
            src_ref=(m_old, v_old)[i],
            dst_ref=moments.at[i, q],
            send_sem=mom_send.at[i, j],
            recv_sem=mom_recv.at[i, j],
            device_id=(z, 2 * (side, over)[j] + c),
            device_id_type=MESH,
        )

    def moment_relay(i):
        came_from = (side, over)[i]
        return pltpu.make_async_remote_copy(
            src_ref=moments.at[i, came_from],
            dst_ref=moments.at[i, came_from],
            send_sem=mom_send.at[i, 2],
            recv_sem=mom_recv.at[i, 2],
            device_id=(z, 2 * (over, side)[i] + c),
            device_id_type=MESH,
        )

    def moment_load(i):
        return pltpu.make_async_copy((m_old, v_old)[i], moments.at[i, q], load_sem.at[2 + i])

    moment_forward = pltpu.make_async_remote_copy(
        src_ref=moments,
        dst_ref=moments,
        send_sem=fwd_send,
        recv_sem=fwd_recv,
        device_id=(z, partner),
        device_id_type=MESH,
    )

    def pair_start(i):
        own_rows = rows_of(2 * chips[i] + 1 - c, window, kept)
        return copies.start(own_rows, pair.at[i], (z, partner))

    def cross_start(i):
        return [
            copies.start(rows_of(2 * chips[i] + c, given_at, few), plane_own.at[i], (mate, d)),
            copies.start(rows_of(2 * chips[i] + 1 - c, given_at, few), plane_pair.at[i], (mate, partner)),
        ]

    pairs = [pair_start(0)]
    crossed = [cross_start(0)]
    for i in (1, 2):
        own_loads[i].start()
        pairs.append(pair_start(i))
    @pl.when(c == group_of)
    def _():
        for j in range(2):
            for i in range(2):
                moment_copy(i, j).start()
        for i in range(2):
            moment_load(i).start()

    arrived = set()

    def arrive(i, group):
        if i not in arrived:
            arrived.add(i)
            pairs[i].wait_recv()
            own_loads[i].wait()
        if group == 0:
            for copy in crossed[i]:
                copy.wait_recv()

    def rows_at(group, h):
        start, count = ((few_at, few // 2), (many_at, many // 2))[group]
        return pl.ds(pl.multiple_of(start + h * count, 16), count)

    def chip_sum(i, h):
        at = rows_at(1, h)
        return own[i, at].astype(F32) + pair[i, at].astype(F32)

    def plane_sum(i, h):
        at, near = rows_at(0, h), slice(h * few // 2, (h + 1) * few // 2)
        total = own[i, at].astype(F32) + pair[i, at].astype(F32)
        return total + (plane_own[i, near].astype(F32) + plane_pair[i, near].astype(F32))

    sums = (plane_sum, chip_sum)
    merging = Copies(merge_send, merge_recv)
    relays, directs, merges = {}, {}, {}

    def send_far(group):
        arrive(0, group)
        for h, chip in enumerate((side, over)):
            at = rows_at(group, h)
            far_sum[at] = sums[group](0, h).astype(BF16)
            relays[group, h] = copies.start(far_sum.at[at], relay_in.at[at], (z, 2 * chip + c))

    def send_direct(group):
        for h, chip in enumerate((side, over)):
            arrive(1 + h, group)
            at = rows_at(group, h)
            direct_out[at] = sums[group](1 + h, h).astype(BF16)
            directs[group, h] = copies.start(direct_out.at[at], direct_in.at[at], (z, 2 * chip + c))

    def send_merged(group):
        for h, (i, chip) in enumerate(((2, over), (1, side))):
            at = rows_at(group, h)
            relays[group, h].wait_recv()
            merged[at] = sums[group](i, h) + relay_in[at].astype(F32)
            merges[group, h] = merging.start(merged.at[at], merged_in.at[at], (z, 2 * chip + c))

    send_far(1)
    crossed += [cross_start(1), cross_start(2)]
    send_direct(1)
    load_new = pltpu.make_async_copy(p_new, basis, load_sem.at[0])
    load_new.start()
    old_loads = [
        pltpu.make_async_copy(
            p_old.at[:, pl.ds(pl.multiple_of((2 * k + group_of) * blk, blk), blk)],
            basis_old.at[:, k * blk : (k + 1) * blk],
            old_sem.at[k],
        )
        for k in range(4)
    ]
    for load in old_loads:
        load.start()
    own_loads[3].start()
    load_weight = pltpu.make_async_copy(weight, weights, load_sem.at[1])
    load_weight.start()
    pairs.append(pair_start(3))
    crossed.append(cross_start(3))
    if n_outer > 2:
        signal_line(line_sem.at[0])

    load_new.wait()
    for load in old_loads:
        load.wait()

    def chip_ranks(k):
        return pl.ds(pl.multiple_of(k * 2 * blk, 2 * blk), 2 * blk)

    for i, k in enumerate(chips):
        part = contract_rows(basis[:, chip_ranks(k)], basis_old[...])
        margin[:, i] = part.reshape(2, 2, n_outer // 2, sub, 4 * blk)
    margin_pair = copies.start(margin.at[1 - c, :, :, turn], margin_partner, (z, partner))

    send_far(0)
    send_merged(1)
    margin_pair.wait_recv()
    margin_sum[...] = margin[c, :, :, turn] + margin_partner[...]

    @pl.when(c == group_of)
    def _():
        for i in range(2):
            moment_copy(i, i).wait_recv()
            moment_relay(i).start()

    send_direct(0)
    send_merged(0)
    for copy in merging.started:
        copy.wait_send()
    margin_relays = [
        copies.start(margin_sum.at[0, h], margin_relay.at[h], (z, 2 * chip + c))
        for h, chip in enumerate((side, over))
    ]
    margin_copies = [
        copies.start(margin_sum.at[1 + h, h], margin_in.at[0, h], (z, 2 * chip + c))
        for h, chip in enumerate((side, over))
    ]

    for group in (1, 0):
        arrive(3, group)
        for h in range(2):
            at = rows_at(group, h)
            directs[group, h].wait_recv()
            total = sums[group](3, h) + direct_in[at].astype(F32)
            merges[group, h].wait_recv()
            total = total + merged_in[at]
            high = total.astype(BF16)
            terms[at, :cols] = high
            terms[at, cols:] = (total - high.astype(F32)).astype(BF16)

    for i, k in enumerate(chips):
        kept_rows = pl.ds(pl.multiple_of(window, 16), kept)
        part = contract_rows(basis[kept_rows, chip_ranks(k)], terms[...])
        part = (part[:, :cols] + part[:, cols:]).reshape(2, n_outer, pieces, fine, cols)
        for h in range(pieces):
            projected[h, :, i] = part[:, :, h]
    projected_pairs = [
        copies.start(projected.at[h, 1 - c], projected_partner.at[h], (z, partner)) for h in range(pieces)
    ]
    for h, (i, chip) in enumerate(((2, over), (1, side))):
        margin_relays[h].wait_recv()
        margin_sum[i, h] = margin_sum[i, h] + margin_relay[h]
        margin_copies.append(copies.start(margin_sum.at[i, h], margin_in.at[1, h], (z, 2 * chip + c)))

    projected_copies = []
    for h in range(pieces):
        projected_pairs[h].wait_recv()
        for i, k in enumerate(chips):
            projected_sum[h, i] = projected[h, c, i] + projected_partner[h, i]
            if i < 3:
                projected_copies.append(
                    copies.start(projected_sum.at[h, i], projected_in.at[h, i], (z, 2 * k + c))
                )

    @pl.when(c == group_of)
    def _():
        for i in range(2):
            moment_load(i).wait()
            moment_copy(i, 1 - i).wait_recv()
            moment_relay(i).wait_recv()
        moment_forward.start()

    @pl.when(c != group_of)
    def _():
        moment_forward.wait_recv()

    for copy in margin_copies:
        copy.wait_recv()
    margin_rows = margin_sum[3] + margin_in[0] + margin_in[1]
    margin_rows = margin_rows.reshape(2 * sub, 4 * blk)
    old = moments[...].reshape(2, 4 * blk, cols)
    for i, rows_in in enumerate((margin_rows, margin_rows * margin_rows)):
        turned = jnp.dot(rows_in, old[i], precision=lax.Precision.HIGHEST, preferred_element_type=F32)
        rotated[:, i] = turned.reshape(2, sub, cols)
    pass_along(range(n_outer - 2))
    planes = [lax.rem(z + j, n_outer) for j in range(1, n_outer)]
    across = lax.rem(z + n_outer // 2, n_outer)
    rot_copy = copies.start(rotated.at[1 - group_of], rotated_in, (across, d))

    block_copies = []
    for h in range(pieces):
        for copy in projected_copies[3 * h : 3 * h + 3]:
            copy.wait_recv()
        block[h] = projected_sum[h, 3] + projected_in[h, 0] + projected_in[h, 1] + projected_in[h, 2]
        for j, to in enumerate(planes):
            block_copies.append(copies.start(block.at[h, to], block_in.at[h, j], (to, d)))

    rot_copy.wait_recv()
    first = rotated[group_of, 0] + rotated_in[0]
    second = rotated[group_of, 1] + rotated_in[1]
    for h in range(pieces):
        at = slice(h * fine, (h + 1) * fine)
        proj = block[h, z]
        for j in range(n_outer - 1):
            block_copies[h * (n_outer - 1) + j].wait_recv()
            proj = proj + block_in[h, j]
        mean = beta_mean * first[at] + (1.0 - beta_mean) * proj
        square = beta_square * second[at] + (1.0 - beta_square) * proj * proj
        moments_new[z, 0, at] = mean
        moments_new[z, 1, at] = square
        direction[d, z, at] = (
            mean / bias_mean / (jnp.sqrt(square / bias_square) + adam_epsilon)
        ).astype(BF16)

    settled = len(copies.started)
    spread = []
    for i, k in enumerate(chips):
        group = []
        for to in planes + [z]:
            if i == 3 and to is z:
                continue
            group.append(copies.start(direction.at[d, z], direction.at[d, z], (to, 2 * k + c)))
        spread.append(group)
    moment_spread = [copies.start(moments_new.at[z], moments_new.at[z], (to, d)) for to in planes]
    for copy in copies.started[:settled]:
        copy.wait_send()

    @pl.when(c == group_of)
    def _():
        for i in range(2):
            for j in range(2):
                moment_copy(i, j).wait_send()
            moment_relay(i).wait_send()
        moment_forward.wait_send()

    forwards = []
    for i in (3, 1, 2, 0):
        for copy in spread[i]:
            copy.wait_recv()
        mine = direction.at[2 * chips[i] + c]
        forwards.append(copies.start(mine, mine, (z, partner)))
    load_weight.wait()
    for copy in sum(spread, moment_spread):
        copy.wait_send()
    for copy in forwards:
        copy.wait_recv()
    directions = direction[...].reshape(rank, cols)
    tall = min(rows, 256)
    for s in range(0, rows, tall):
        update = jnp.dot(basis[s : s + tall, :], directions, preferred_element_type=F32)
        new_weight[s : s + tall, :] = weights[s : s + tall, :] - step_scale * update
    for copy in moment_spread:
        copy.wait_recv()
    m_new[...] = moments_new[:, 0].reshape(blk, cols)
    v_new[...] = moments_new[:, 1].reshape(blk, cols)

    for copy in forwards:
        copy.wait_send()


def shared_rows(rows):
    top, bottom = shared_part
    return rows * top // bottom // 32 * 32


def square_scratch(n_outer, n_dev, rows, cols, rank):
    blk = rank // n_dev
    sub = blk // n_outer
    fine = sub // pieces
    span = 4 * blk
    dma = pltpu.SemaphoreType.DMA
    few = shared_rows(rows)
    kept = rows - few
    count = 50 + 15 * pieces + 6 * n_outer
    return [
        pltpu.VMEM((4, kept, cols), BF16),
        pltpu.VMEM((4, kept, cols), BF16),
        pltpu.VMEM((4, few, cols), BF16),
        pltpu.VMEM((4, few, cols), BF16),
        pltpu.VMEM((kept, cols), BF16),
        pltpu.VMEM((kept, cols), BF16),
        pltpu.VMEM((kept, cols), BF16),
        pltpu.VMEM((kept, cols), BF16),
        pltpu.VMEM((kept, cols), F32),
        pltpu.VMEM((kept, cols), F32),
        pltpu.VMEM((kept, 2 * cols), BF16),
        pltpu.VMEM((rows, rank), BF16),
        pltpu.VMEM((rows, span), BF16),
        pltpu.VMEM((rows, cols), F32),
        pltpu.VMEM((2, 4, blk, cols), F32),
        pltpu.VMEM((2, 4, 2, n_outer // 2, sub, span), F32),
        pltpu.VMEM((4, 2, sub, span), F32),
        pltpu.VMEM((4, 2, sub, span), F32),
        pltpu.VMEM((2, 2, sub, span), F32),
        pltpu.VMEM((2, sub, span), F32),
        pltpu.VMEM((2, 2, sub, cols), F32),
        pltpu.VMEM((2, sub, cols), F32),
        pltpu.VMEM((pieces, 2, 4, n_outer, fine, cols), F32),
        pltpu.VMEM((pieces, 4, n_outer, fine, cols), F32),
        pltpu.VMEM((pieces, 4, n_outer, fine, cols), F32),
        pltpu.VMEM((pieces, 3, n_outer, fine, cols), F32),
        pltpu.VMEM((pieces, n_outer, fine, cols), F32),
        pltpu.VMEM((pieces, n_outer - 1, fine, cols), F32),
        pltpu.VMEM((n_dev, n_outer, sub, cols), BF16),
        pltpu.VMEM((n_outer, 2, sub, cols), F32),
        dma((4,)),
        dma((4,)),
        dma((4,)),
        dma((2, 3)),
        dma((2, 3)),
        dma,
        dma,
        dma((count,)),
        dma((count,)),
        dma((4,)),
        dma((4,)),
        pltpu.SemaphoreType.REGULAR((max(n_outer - 2, 1),)),
    ]


def plain_scratch(n_outer, n_dev, rows, cols, rank):
    blk = rank // n_dev
    per = n_dev // n_outer
    span = per * blk
    n_chip = n_dev // 2
    dma = pltpu.SemaphoreType.DMA
    return (
        [
            pltpu.VMEM((n_dev, rows, cols), BF16),
            pltpu.VMEM((rows, rank), BF16),
            pltpu.VMEM((rows, span), BF16),
            pltpu.VMEM((rows, cols), F32),
            pltpu.VMEM((2, per, blk, cols), F32),
            pltpu.VMEM((n_dev, blk, span), F32),
            pltpu.VMEM((n_chip, blk, span), F32),
            pltpu.VMEM((n_chip, blk, span), F32),
            pltpu.VMEM((n_chip, blk, span), F32),
            pltpu.VMEM((2, blk, cols), F32),
            pltpu.VMEM((n_outer, 2, blk, cols), F32),
            pltpu.VMEM((n_dev, blk, cols), F32),
            pltpu.VMEM((n_chip, blk, cols), F32),
            pltpu.VMEM((n_chip, blk, cols), F32),
            pltpu.VMEM((n_chip, blk, cols), F32),
            pltpu.VMEM((blk, cols), F32),
            pltpu.VMEM((n_outer, blk, cols), F32),
            pltpu.VMEM((n_dev, blk, cols), BF16),
            dma((6,)),
            dma((per,)),
            dma((chunks, n_dev)),
            dma((chunks, n_dev)),
            dma((2, per, n_chip)),
            dma((2, per)),
            dma((2, per)),
            dma((2, per)),
        ]
        + [dma((n_chip,))] * 4
        + [dma((n_outer,))] * 2
        + [dma((parts, n_chip))] * 4
        + [dma((parts, n_outer))] * 2
        + [dma((parts, n_dev))] * 2
    )


def hand_over(weight_in, m_in, v_in, weight_out, m_out, v_out):
    weight_out[...] = weight_in[...]
    m_out[...] = m_in[...]
    v_out[...] = v_in[...]


def on_device(n_outer, n_dev, partials, p_old, p_new, weight, m_old, v_old):
    rows, cols = weight.shape
    rank = p_new.shape[1]
    blk = rank // n_dev
    per = n_dev // n_outer
    span = per * blk
    n_chip = n_dev // 2
    squared = n_chip == 4 and n_dev % n_outer == 0 and n_outer % 2 == 0 and rows % 64 == 0 and blk % 128 == 0 and blk % (16 * pieces * n_outer) == 0
    if blk % 128 and not squared:
        z = lax.axis_index("outer")
        p_old = jnp.concatenate(
            [
                lax.dynamic_slice_in_dim(p_old, (k * n_outer + z) * blk, blk, axis=1)
                for k in range(per)
            ],
            axis=1,
        )
    anywhere = pl.BlockSpec(memory_space=pltpu.HBM)
    vmem = pl.BlockSpec(memory_space=pltpu.VMEM)
    if squared:
        body, scratch = square_kernel, square_scratch(n_outer, n_dev, rows, cols, rank)
    else:
        body, scratch = kernel, plain_scratch(n_outer, n_dev, rows, cols, rank)
    operands = (partials[0], p_old, p_new, weight, m_old, v_old)
    results = pl.pallas_call(
        functools.partial(body, n_outer, n_dev),
        out_shape=(
            jax.ShapeDtypeStruct((rows, cols), F32),
            jax.ShapeDtypeStruct((blk, cols), F32),
            jax.ShapeDtypeStruct((blk, cols), F32),
        ),
        in_specs=[anywhere] * 6,
        out_specs=(vmem, vmem, vmem),
        scratch_shapes=scratch,
        compiler_params=pltpu.CompilerParams(
            collective_id=0, has_side_effects=True, vmem_limit_bytes=vmem_limit
        ),
    )(*[pltpu.with_memory_space_constraint(a, pltpu.HBM) for a in operands])
    return pl.pallas_call(
        hand_over,
        out_shape=tuple(jax.ShapeDtypeStruct(r.shape, r.dtype) for r in results),
        in_specs=[vmem] * 3,
        out_specs=(vmem,) * 3,
        compiler_params=pltpu.CompilerParams(vmem_limit_bytes=finish_limit),
    )(*results)


def solution(mesh):
    in_specs = (
        P(("outer", "dev"), None, None),
        P("dev", None),
        P("dev", None),
        P("dev", None),
        P("dev", None),
        P("dev", None),
    )
    out_specs = (P("dev", None), P("dev", None), P("dev", None))
    return jax.shard_map(
        functools.partial(on_device, mesh.shape["outer"], mesh.shape["dev"]),
        mesh=mesh,
        in_specs=in_specs,
        out_specs=out_specs,
        check_vma=False,
    )
```

```python
import functools

import jax
import jax.numpy as jnp
from jax import lax
from jax.experimental import pallas as pl
from jax.experimental.pallas import tpu as pltpu
from jax.sharding import PartitionSpec as P

beta_mean = 0.9
beta_square = 0.95
bias_mean = 0.9999734386011124
bias_square = 0.9940794707796659
adam_epsilon = 1e-08
step_scale = 0.5

chunks = 2
early = 1
parts = 2
pieces = 2
shared_part = (3, 16)
vmem_limit = 50331648
finish_limit = 4194304

MESH = pl.DeviceIdType.MESH
F32 = jnp.float32
BF16 = jnp.bfloat16


def contract_rows(a, b):
    return lax.dot_general(a, b, (((0,), (0,)), ((), ())), preferred_element_type=F32)


def kernel(
    n_outer,
    n_dev,
    partials,
    p_old,
    p_new,
    weight,
    m_old,
    v_old,
    new_weight,
    m_new,
    v_new,
    grads,
    basis,
    basis_old,
    weights,
    moments,
    margin,
    margin_partner,
    margin_sum,
    margin_in,
    rotated,
    rotated_in,
    projected,
    projected_partner,
    projected_sum,
    projected_in,
    block,
    block_in,
    direction,
    load_sem,
    old_sem,
    grad_send,
    grad_recv,
    mom_send,
    mom_recv,
    fwd_send,
    fwd_recv,
    mp_send,
    mp_recv,
    ms_send,
    ms_recv,
    rot_send,
    rot_recv,
    pp_send,
    pp_recv,
    ps_send,
    ps_recv,
    blk_send,
    blk_recv,
    dir_send,
    dir_recv,
):
    z = lax.axis_index("outer")
    d = lax.axis_index("dev")
    n_chip = n_dev // 2
    q = d // 2
    c = d % 2
    partner = q * 2 + 1 - c
    rows, cols = weight.shape
    rank = p_new.shape[1]
    blk = rank // n_dev
    per = n_dev // n_outer

    def remote(src, dst, send, recv, where):
        return pltpu.make_async_remote_copy(
            src_ref=src, dst_ref=dst, send_sem=send, recv_sem=recv, device_id=where, device_id_type=MESH
        )

    barrier = pltpu.get_barrier_semaphore()
    for j in range(1, n_dev):
        pl.semaphore_signal(barrier, inc=1, device_id=(z, lax.rem(d + j, n_dev)), device_id_type=MESH)
    for j in range(1, n_outer):
        pl.semaphore_signal(barrier, inc=1, device_id=(lax.rem(z + j, n_outer), d), device_id_type=MESH)

    load_new = pltpu.make_async_copy(p_new, basis, load_sem.at[0])
    load_new.start()
    if p_old.shape[1] == per * blk:
        old_loads = [pltpu.make_async_copy(p_old, basis_old, old_sem.at[0])]
    else:
        old_loads = [
            pltpu.make_async_copy(
                p_old.at[:, pl.ds(pl.multiple_of((k * n_outer + z) * blk, blk), blk)],
                basis_old.at[:, k * blk : (k + 1) * blk],
                old_sem.at[k],
            )
            for k in range(per)
        ]
    for load in old_loads:
        load.start()
    load_weight = pltpu.make_async_copy(weight, weights, load_sem.at[2])
    load_weight.start()
    load_own = pltpu.make_async_copy(
        partials.at[pl.ds(pl.multiple_of(d * rows, rows), rows)], grads.at[0], load_sem.at[3]
    )
    load_own.start()

    pl.semaphore_wait(barrier, n_dev - 1 + n_outer - 1)

    def moment_copies(k, owner):
        copies = []
        for j in range(1, n_chip):
            to = (z, lax.rem(q + j, n_chip) * 2 + c)
            for i, src in enumerate((m_old, v_old)):
                copies.append(remote(src, moments.at[i, k], mom_send.at[i, k, j], mom_recv.at[i, k], to))
        return copies

    for k in range(per):
        owner = k * n_outer + z

        @pl.when(d == owner)
        def _():
            for copy in moment_copies(k, owner):
                copy.start()
            for i, src in enumerate((m_old, v_old)):
                pltpu.make_async_copy(src, moments.at[i, k], load_sem.at[4 + i]).start()

    tall = rows // chunks

    def send_gradients(chunk):
        copies = []
        for j in range(1, n_dev):
            to = lax.rem(d + j, n_dev)
            copy = remote(
                partials.at[pl.ds(pl.multiple_of(to * rows + chunk * tall, tall), tall)],
                grads.at[j, chunk * tall : (chunk + 1) * tall],
                grad_send.at[chunk, j],
                grad_recv.at[chunk, j],
                (z, to),
            )
            copy.start()
            copies.append(copy)
        return copies

    grad_copies = [send_gradients(chunk) for chunk in range(early)]

    load_new.wait()
    for load in old_loads:
        load.wait()
    width = min(rank, 256)
    for s in range(0, rank, width):
        part = contract_rows(basis[:, s : s + width], basis_old[...])
        margin[s // blk : (s + width) // blk] = part.reshape(width // blk, blk, part.shape[1])

    def scatter_start(val, prt, send, recv):
        copies = []
        for j in list(range(1, n_chip)) + [0]:
            k = lax.rem(q + j, n_chip)
            copy = remote(val.at[2 * k + 1 - c], prt.at[j], send.at[j], recv.at[j], (z, partner))
            copy.start()
            copies.append((j, k, copy))
        return copies

    def scatter_middle(pairs, val, prt, tot, arr, send, recv):
        copies = []
        for j, k, pair in pairs:
            pair.wait_recv()
            tot[j] = val[2 * k + c] + prt[j]
            if j:
                copy = remote(tot.at[j], arr.at[j], send.at[j], recv.at[j], (z, 2 * k + c))
                copy.start()
                copies.append((j, copy))
        return copies

    def scatter_end(copies, tot, arr):
        total = tot[0]
        for j, copy in copies:
            copy.wait_recv()
            total = total + arr[j]
        return total

    margin_pairs = scatter_start(margin, margin_partner, mp_send, mp_recv)

    for k in range(per):
        owner = k * n_outer + z
        mine = c == owner % 2

        @pl.when(d == owner)
        def _():
            for i, src in enumerate((m_old, v_old)):
                pltpu.make_async_copy(src, moments.at[i, k], load_sem.at[4 + i]).wait()

        @pl.when(jnp.logical_and(mine, d != owner))
        def _():
            for i, src in enumerate((m_old, v_old)):
                remote(src, moments.at[i, k], mom_send.at[i, k, 0], mom_recv.at[i, k], (z, d)).wait_recv()

        @pl.when(mine)
        def _():
            for i in range(2):
                remote(
                    moments.at[i, k], moments.at[i, k], fwd_send.at[i, k], fwd_recv.at[i, k], (z, partner)
                ).start()

    margin_copies = scatter_middle(
        margin_pairs, margin, margin_partner, margin_sum, margin_in, ms_send, ms_recv
    )

    for chunk in range(early, chunks):
        grad_copies.append(send_gradients(chunk))

    for k in range(per):
        mine = c == (k * n_outer + z) % 2

        @pl.when(jnp.logical_not(mine))
        def _():
            for i in range(2):
                remote(
                    moments.at[i, k], moments.at[i, k], fwd_send.at[i, k], fwd_recv.at[i, k], (z, partner)
                ).wait_recv()

    margin_rows = scatter_end(margin_copies, margin_sum, margin_in)
    old = moments[...].reshape(2, per * blk, cols)
    rotated[0] = jnp.dot(margin_rows, old[0], precision=lax.Precision.HIGHEST, preferred_element_type=F32)
    rotated[1] = jnp.dot(
        margin_rows * margin_rows, old[1], precision=lax.Precision.HIGHEST, preferred_element_type=F32
    )
    rot_copies = []
    for j in range(1, n_outer):
        copy = remote(
            rotated, rotated_in.at[j], rot_send.at[j], rot_recv.at[j], (lax.rem(z + j, n_outer), d)
        )
        copy.start()
        rot_copies.append(copy)

    load_own.wait()
    for chunk in range(chunks):
        for copy in grad_copies[chunk]:
            copy.wait_recv()
        part_rows = slice(chunk * tall, (chunk + 1) * tall)
        total = grads[0, part_rows].astype(F32)
        for j in range(1, n_dev):
            total = total + grads[j, part_rows].astype(F32)
        high = total.astype(BF16)
        low = (total - high.astype(F32)).astype(BF16)
        both = jnp.concatenate([high, low], axis=1)
        for s in range(0, rank, width):
            part = contract_rows(basis[part_rows, s : s + width], both)
            part = (part[:, :cols] + part[:, cols:]).reshape(width // blk, blk, cols)
            blocks = slice(s // blk, (s + width) // blk)
            projected[blocks] = part if chunk == 0 else projected[blocks] + part
    half = blk // parts
    views = [slice(h * half, (h + 1) * half) for h in range(parts)]
    pairs = [
        scatter_start(projected.at[:, v], projected_partner.at[:, v], pp_send.at[h], pp_recv.at[h])
        for h, v in enumerate(views)
    ]
    copies = [
        scatter_middle(
            pairs[h],
            projected.at[:, v],
            projected_partner.at[:, v],
            projected_sum.at[:, v],
            projected_in.at[:, v],
            ps_send.at[h],
            ps_recv.at[h],
        )
        for h, v in enumerate(views)
    ]
    blk_copies = []
    for h, v in enumerate(views):
        block[v] = scatter_end(copies[h], projected_sum.at[:, v], projected_in.at[:, v])
        for j in range(1, n_outer):
            copy = remote(
                block.at[v],
                block_in.at[j, v],
                blk_send.at[h, j],
                blk_recv.at[h, j],
                (lax.rem(z + j, n_outer), d),
            )
            copy.start()
            blk_copies.append(copy)
    for copy in rot_copies:
        copy.wait_recv()
    dir_copies = []
    for h, v in enumerate(views):
        for copy in blk_copies[h * (n_outer - 1) : (h + 1) * (n_outer - 1)]:
            copy.wait_recv()
        first = rotated[0, v]
        second = rotated[1, v]
        proj = block[v]
        for j in range(1, n_outer):
            first = first + rotated_in[j, 0, v]
            second = second + rotated_in[j, 1, v]
            proj = proj + block_in[j, v]
        mean = beta_mean * first + (1.0 - beta_mean) * proj
        square = beta_square * second + (1.0 - beta_square) * proj * proj
        m_new[v] = mean
        v_new[v] = square
        direction[d, v] = (mean / bias_mean / (jnp.sqrt(square / bias_square) + adam_epsilon)).astype(BF16)
        for j in range(1, n_dev):
            copy = remote(
                direction.at[d, v],
                direction.at[d, v],
                dir_send.at[h, j],
                dir_recv.at[h, j],
                (z, lax.rem(d + j, n_dev)),
            )
            copy.start()
            dir_copies.append(copy)
    load_weight.wait()
    for copy in dir_copies:
        copy.wait_recv()
    directions = direction[...].reshape(rank, cols)
    tall = min(rows, 256)
    for s in range(0, rows, tall):
        update = jnp.dot(basis[s : s + tall, :], directions, preferred_element_type=F32)
        new_weight[s : s + tall, :] = weights[s : s + tall, :] - step_scale * update

    for k in range(per):
        owner = k * n_outer + z
        mine = c == owner % 2

        @pl.when(d == owner)
        def _():
            for copy in moment_copies(k, owner):
                copy.wait_send()

        @pl.when(mine)
        def _():
            for i in range(2):
                remote(
                    moments.at[i, k], moments.at[i, k], fwd_send.at[i, k], fwd_recv.at[i, k], (z, partner)
                ).wait_send()

    for copy in sum(grad_copies, []) + rot_copies + blk_copies + dir_copies:
        copy.wait_send()
    for group in [margin_pairs] + pairs:
        for _, _, copy in group:
            copy.wait_send()
    for group in [margin_copies] + copies:
        for _, copy in group:
            copy.wait_send()

class Copies:
    def __init__(self, send, recv):
        self.send, self.recv, self.started = send, recv, []

    def start(self, src, dst, to):
        i = len(self.started)
        copy = pltpu.make_async_remote_copy(
            src_ref=src,
            dst_ref=dst,
            send_sem=self.send.at[i],
            recv_sem=self.recv.at[i],
            device_id=to,
            device_id_type=MESH,
        )
        copy.start()
        self.started.append(copy)
        return copy


def square_kernel(
    n_outer,
    n_dev,
    partials,
    p_old,
    p_new,
    weight,
    m_old,
    v_old,
    new_weight,
    m_new,
    v_new,
    own,
    pair,
    plane_own,
    plane_pair,
    far_sum,
    relay_in,
    direct_out,
    direct_in,
    merged,
    merged_in,
    terms,
    basis,
    basis_old,
    weights,
    moments,
    margin,
    margin_partner,
    margin_sum,
    margin_in,
    margin_relay,
    rotated,
    rotated_in,
    projected,
    projected_partner,
    projected_sum,
    projected_in,
    block,
    block_in,
    column,
    column_in,
    chip_in,
    direction,
    moments_new,
    load_sem,
    old_sem,
    own_sem,
    mom_send,
    mom_recv,
    fwd_send,
    fwd_recv,
    send_sem,
    recv_sem,
    merge_send,
    merge_recv,
    line_sem,
):
    z = lax.axis_index("outer")
    d = lax.axis_index("dev")
    q = d // 2
    c = d % 2
    partner = q * 2 + 1 - c
    side = q + 1 - 2 * (q % 2)
    over = lax.rem(q + 2, 4)
    far = lax.rem(side + 2, 4)
    chips = (far, side, over, q)
    rows, cols = weight.shape
    rank = p_new.shape[1]
    blk = rank // n_dev
    sub = blk // n_outer
    fine = sub // pieces
    few = shared_rows(rows)
    many = rows - 2 * few
    kept = few + many
    mate = z + 1 - 2 * (z % 2)
    odd = z % 2
    window = odd * few
    group_of = z // (n_outer // 2)
    turn = z % (n_outer // 2)
    few_at = odd * many
    many_at = few - window
    given_at = (1 - odd) * kept
    copies = Copies(send_sem, recv_sem)
    above = (2 * n_outer - 2 - z) // n_outer
    below = (z + n_outer - 1) // n_outer

    def signal_line(sem):
        @pl.when(z > 0)
        def _():
            pl.semaphore_signal(sem, inc=1, device_id=(z - 1, d), device_id_type=MESH)

        @pl.when(z < n_outer - 1)
        def _():
            pl.semaphore_signal(sem, inc=1, device_id=(z + 1, d), device_id_type=MESH)

    def pass_along(steps):
        for r in steps:
            pl.semaphore_wait(line_sem.at[r], above + below)
            if r + 1 < n_outer - 2:
                signal_line(line_sem.at[r + 1])

    barrier = pltpu.get_barrier_semaphore()
    for to in (partner, 2 * side + c, 2 * over + c):
        pl.semaphore_signal(barrier, inc=1, device_id=(z, to), device_id_type=MESH)
    pl.semaphore_signal(barrier, inc=1, device_id=(mate, partner), device_id_type=MESH)
    signal_line(barrier)

    def rows_of(to, start, count):
        return partials.at[pl.ds(pl.multiple_of(to * rows + start, 16), count)]

    own_loads = [
        pltpu.make_async_copy(rows_of(2 * k + c, window, kept), own.at[i], own_sem.at[i])
        for i, k in enumerate(chips)
    ]
    own_loads[0].start()
    pl.semaphore_wait(barrier, 4 + above + below)

    def moment_copy(i, j):
        return pltpu.make_async_remote_copy(
            src_ref=(m_old, v_old)[i],
            dst_ref=moments.at[i, q],
            send_sem=mom_send.at[i, j],
            recv_sem=mom_recv.at[i, j],
            device_id=(z, 2 * (side, over)[j] + c),
            device_id_type=MESH,
        )

    def moment_relay(i):
        came_from = (side, over)[i]
        return pltpu.make_async_remote_copy(
            src_ref=moments.at[i, came_from],
            dst_ref=moments.at[i, came_from],
            send_sem=mom_send.at[i, 2],
            recv_sem=mom_recv.at[i, 2],
            device_id=(z, 2 * (over, side)[i] + c),
            device_id_type=MESH,
        )

    def moment_load(i):
        return pltpu.make_async_copy((m_old, v_old)[i], moments.at[i, q], load_sem.at[2 + i])

    moment_forward = pltpu.make_async_remote_copy(
        src_ref=moments,
        dst_ref=moments,
        send_sem=fwd_send,
        recv_sem=fwd_recv,
        device_id=(z, partner),
        device_id_type=MESH,
    )

    def pair_start(i):
        own_rows = rows_of(2 * chips[i] + 1 - c, window, kept)
        return copies.start(own_rows, pair.at[i], (z, partner))

    def cross_start(i):
        return [
            copies.start(rows_of(2 * chips[i] + c, given_at, few), plane_own.at[i], (mate, d)),
            copies.start(rows_of(2 * chips[i] + 1 - c, given_at, few), plane_pair.at[i], (mate, partner)),
        ]

    pairs = [pair_start(0)]
    crossed = [cross_start(0)]
    for i in (1, 2):
        own_loads[i].start()
        pairs.append(pair_start(i))
    @pl.when(c == group_of)
    def _():
        for j in range(2):
            for i in range(2):
                moment_copy(i, j).start()
        for i in range(2):
            moment_load(i).start()

    arrived = set()

    def arrive(i, group):
        if i not in arrived:
            arrived.add(i)
            pairs[i].wait_recv()
            own_loads[i].wait()
        if group == 0:
            for copy in crossed[i]:
                copy.wait_recv()

    def rows_at(group, h):
        start, count = ((few_at, few // 2), (many_at, many // 2))[group]
        return pl.ds(pl.multiple_of(start + h * count, 16), count)

    def chip_sum(i, h):
        at = rows_at(1, h)
        return own[i, at].astype(F32) + pair[i, at].astype(F32)

    def plane_sum(i, h):
        at, near = rows_at(0, h), slice(h * few // 2, (h + 1) * few // 2)
        total = own[i, at].astype(F32) + pair[i, at].astype(F32)
        return total + (plane_own[i, near].astype(F32) + plane_pair[i, near].astype(F32))

    sums = (plane_sum, chip_sum)
    merging = Copies(merge_send, merge_recv)
    relays, directs, merges = {}, {}, {}

    def send_far(group):
        arrive(0, group)
        for h, chip in enumerate((side, over)):
            at = rows_at(group, h)
            far_sum[at] = sums[group](0, h).astype(BF16)
            relays[group, h] = copies.start(far_sum.at[at], relay_in.at[at], (z, 2 * chip + c))

    def send_direct(group):
        for h, chip in enumerate((side, over)):
            arrive(1 + h, group)
            at = rows_at(group, h)
            direct_out[at] = sums[group](1 + h, h).astype(BF16)
            directs[group, h] = copies.start(direct_out.at[at], direct_in.at[at], (z, 2 * chip + c))

    def send_merged(group):
        for h, (i, chip) in enumerate(((2, over), (1, side))):
            at = rows_at(group, h)
            relays[group, h].wait_recv()
            merged[at] = sums[group](i, h) + relay_in[at].astype(F32)
            merges[group, h] = merging.start(merged.at[at], merged_in.at[at], (z, 2 * chip + c))

    send_far(1)
    crossed += [cross_start(1), cross_start(2)]
    send_direct(1)
    load_new = pltpu.make_async_copy(p_new, basis, load_sem.at[0])
    load_new.start()
    old_loads = [
        pltpu.make_async_copy(
            p_old.at[:, pl.ds(pl.multiple_of((2 * k + group_of) * blk, blk), blk)],
            basis_old.at[:, k * blk : (k + 1) * blk],
            old_sem.at[k],
        )
        for k in range(4)
    ]
    for load in old_loads:
        load.start()
    own_loads[3].start()
    load_weight = pltpu.make_async_copy(weight, weights, load_sem.at[1])
    load_weight.start()
    pairs.append(pair_start(3))
    crossed.append(cross_start(3))
    if n_outer > 2:
        signal_line(line_sem.at[0])

    load_new.wait()
    for load in old_loads:
        load.wait()

    def chip_ranks(k):
        return pl.ds(pl.multiple_of(k * 2 * blk, 2 * blk), 2 * blk)

    for i, k in enumerate(chips):
        part = contract_rows(basis[:, chip_ranks(k)], basis_old[...])
        margin[:, i] = part.reshape(2, 2, n_outer // 2, sub, 4 * blk)
    margin_pair = copies.start(margin.at[1 - c, :, :, turn], margin_partner, (z, partner))

    send_far(0)
    send_merged(1)
    margin_pair.wait_recv()
    margin_sum[...] = margin[c, :, :, turn] + margin_partner[...]

    @pl.when(c == group_of)
    def _():
        for i in range(2):
            moment_copy(i, i).wait_recv()
            moment_relay(i).start()

    send_direct(0)
    send_merged(0)
    for copy in merging.started:
        copy.wait_send()
    margin_relays = [
        copies.start(margin_sum.at[0, h], margin_relay.at[h], (z, 2 * chip + c))
        for h, chip in enumerate((side, over))
    ]
    margin_copies = [
        copies.start(margin_sum.at[1 + h, h], margin_in.at[0, h], (z, 2 * chip + c))
        for h, chip in enumerate((side, over))
    ]

    for group in (1, 0):
        arrive(3, group)
        for h in range(2):
            at = rows_at(group, h)
            directs[group, h].wait_recv()
            total = sums[group](3, h) + direct_in[at].astype(F32)
            merges[group, h].wait_recv()
            total = total + merged_in[at]
            high = total.astype(BF16)
            terms[at, :cols] = high
            terms[at, cols:] = (total - high.astype(F32)).astype(BF16)

    for i, k in enumerate(chips):
        kept_rows = pl.ds(pl.multiple_of(window, 16), kept)
        part = contract_rows(basis[kept_rows, chip_ranks(k)], terms[...])
        part = (part[:, :cols] + part[:, cols:]).reshape(2, n_outer, pieces, fine, cols)
        for h in range(pieces):
            projected[h, :, i] = part[:, :, h]
    projected_pairs = [
        copies.start(projected.at[h, 1 - c], projected_partner.at[h], (z, partner)) for h in range(pieces)
    ]
    for h, (i, chip) in enumerate(((2, over), (1, side))):
        margin_relays[h].wait_recv()
        margin_sum[i, h] = margin_sum[i, h] + margin_relay[h]
        margin_copies.append(copies.start(margin_sum.at[i, h], margin_in.at[1, h], (z, 2 * chip + c)))

    planes = [lax.rem(z + j, n_outer) for j in range(1, n_outer)]
    pass_along(range(n_outer - 2))
    projected_pairs[0].wait_recv()
    projected_copies = []
    for i, k in enumerate(chips):
        projected_sum[0, i] = projected[0, c, i] + projected_partner[0, i]
        if i < 3:
            projected_copies.append(
                copies.start(projected_sum.at[0, i], projected_in.at[i], (z, 2 * k + c))
            )
    projected_pairs[1].wait_recv()
    projected_sum[1] = projected[1, c] + projected_partner[1]
    column_copies = [
        copies.start(projected_sum.at[1, :, to], column_in.at[j], (to, d)) for j, to in enumerate(planes)
    ]

    @pl.when(c == group_of)
    def _():
        for i in range(2):
            moment_load(i).wait()
            moment_copy(i, 1 - i).wait_recv()
            moment_relay(i).wait_recv()
        moment_forward.start()

    @pl.when(c != group_of)
    def _():
        moment_forward.wait_recv()

    for copy in margin_copies:
        copy.wait_recv()
    margin_rows = margin_sum[3] + margin_in[0] + margin_in[1]
    margin_rows = margin_rows.reshape(2 * sub, 4 * blk)
    old = moments[...].reshape(2, 4 * blk, cols)
    for i, rows_in in enumerate((margin_rows, margin_rows * margin_rows)):
        turned = jnp.dot(rows_in, old[i], precision=lax.Precision.HIGHEST, preferred_element_type=F32)
        rotated[:, i] = turned.reshape(2, sub, cols)
    across = lax.rem(z + n_outer // 2, n_outer)
    rot_copy = copies.start(rotated.at[1 - group_of], rotated_in, (across, d))

    for copy in projected_copies:
        copy.wait_recv()
    block[...] = projected_sum[0, 3] + projected_in[0] + projected_in[1] + projected_in[2]
    block_copies = [copies.start(block.at[to], block_in.at[j], (to, d)) for j, to in enumerate(planes)]
    for copy in column_copies:
        copy.wait_recv()
    for i in range(4):
        total = projected_sum[1, i, z]
        for j in range(n_outer - 1):
            total = total + column_in[j, i]
        column[i] = total
    chip_copies = [
        copies.start(column.at[i], chip_in.at[i], (z, 2 * k + c)) for i, k in enumerate(chips[:3])
    ]

    rot_copy.wait_recv()
    first = rotated[group_of, 0] + rotated_in[0]
    second = rotated[group_of, 1] + rotated_in[1]
    for h in range(pieces):
        at = slice(h * fine, (h + 1) * fine)
        if h == 0:
            proj = block[z]
            for j, copy in enumerate(block_copies):
                copy.wait_recv()
                proj = proj + block_in[j]
        else:
            proj = column[3]
            for i, copy in enumerate(chip_copies):
                copy.wait_recv()
                proj = proj + chip_in[i]
        mean = beta_mean * first[at] + (1.0 - beta_mean) * proj
        square = beta_square * second[at] + (1.0 - beta_square) * proj * proj
        moments_new[z, 0, at] = mean
        moments_new[z, 1, at] = square
        direction[d, z, at] = (
            mean / bias_mean / (jnp.sqrt(square / bias_square) + adam_epsilon)
        ).astype(BF16)

    settled = len(copies.started)
    spread = []
    for i, k in enumerate(chips):
        group = []
        for to in planes + [z]:
            if i == 3 and to is z:
                continue
            group.append(copies.start(direction.at[d, z], direction.at[d, z], (to, 2 * k + c)))
        spread.append(group)
    moment_spread = [copies.start(moments_new.at[z], moments_new.at[z], (to, d)) for to in planes]
    for copy in copies.started[:settled]:
        copy.wait_send()

    @pl.when(c == group_of)
    def _():
        for i in range(2):
            for j in range(2):
                moment_copy(i, j).wait_send()
            moment_relay(i).wait_send()
        moment_forward.wait_send()

    forwards = []
    for i in (3, 1, 2, 0):
        for copy in spread[i]:
            copy.wait_recv()
        mine = direction.at[2 * chips[i] + c]
        forwards.append(copies.start(mine, mine, (z, partner)))
    load_weight.wait()
    for copy in sum(spread, moment_spread):
        copy.wait_send()
    for copy in forwards:
        copy.wait_recv()
    directions = direction[...].reshape(rank, cols)
    tall = min(rows, 256)
    for s in range(0, rows, tall):
        update = jnp.dot(basis[s : s + tall, :], directions, preferred_element_type=F32)
        new_weight[s : s + tall, :] = weights[s : s + tall, :] - step_scale * update
    for copy in moment_spread:
        copy.wait_recv()
    m_new[...] = moments_new[:, 0].reshape(blk, cols)
    v_new[...] = moments_new[:, 1].reshape(blk, cols)

    for copy in forwards:
        copy.wait_send()


def shared_rows(rows):
    top, bottom = shared_part
    return rows * top // bottom // 32 * 32


def square_scratch(n_outer, n_dev, rows, cols, rank):
    blk = rank // n_dev
    sub = blk // n_outer
    fine = sub // pieces
    span = 4 * blk
    dma = pltpu.SemaphoreType.DMA
    few = shared_rows(rows)
    kept = rows - few
    count = 50 + 15 * pieces + 6 * n_outer
    return [
        pltpu.VMEM((4, kept, cols), BF16),
        pltpu.VMEM((4, kept, cols), BF16),
        pltpu.VMEM((4, few, cols), BF16),
        pltpu.VMEM((4, few, cols), BF16),
        pltpu.VMEM((kept, cols), BF16),
        pltpu.VMEM((kept, cols), BF16),
        pltpu.VMEM((kept, cols), BF16),
        pltpu.VMEM((kept, cols), BF16),
        pltpu.VMEM((kept, cols), F32),
        pltpu.VMEM((kept, cols), F32),
        pltpu.VMEM((kept, 2 * cols), BF16),
        pltpu.VMEM((rows, rank), BF16),
        pltpu.VMEM((rows, span), BF16),
        pltpu.VMEM((rows, cols), F32),
        pltpu.VMEM((2, 4, blk, cols), F32),
        pltpu.VMEM((2, 4, 2, n_outer // 2, sub, span), F32),
        pltpu.VMEM((4, 2, sub, span), F32),
        pltpu.VMEM((4, 2, sub, span), F32),
        pltpu.VMEM((2, 2, sub, span), F32),
        pltpu.VMEM((2, sub, span), F32),
        pltpu.VMEM((2, 2, sub, cols), F32),
        pltpu.VMEM((2, sub, cols), F32),
        pltpu.VMEM((pieces, 2, 4, n_outer, fine, cols), F32),
        pltpu.VMEM((pieces, 4, n_outer, fine, cols), F32),
        pltpu.VMEM((pieces, 4, n_outer, fine, cols), F32),
        pltpu.VMEM((3, n_outer, fine, cols), F32),
        pltpu.VMEM((n_outer, fine, cols), F32),
        pltpu.VMEM((n_outer - 1, fine, cols), F32),
        pltpu.VMEM((4, fine, cols), F32),
        pltpu.VMEM((n_outer - 1, 4, fine, cols), F32),
        pltpu.VMEM((3, fine, cols), F32),
        pltpu.VMEM((n_dev, n_outer, sub, cols), BF16),
        pltpu.VMEM((n_outer, 2, sub, cols), F32),
        dma((4,)),
        dma((4,)),
        dma((4,)),
        dma((2, 3)),
        dma((2, 3)),
        dma,
        dma,
        dma((count,)),
        dma((count,)),
        dma((4,)),
        dma((4,)),
        pltpu.SemaphoreType.REGULAR((max(n_outer - 2, 1),)),
    ]


def plain_scratch(n_outer, n_dev, rows, cols, rank):
    blk = rank // n_dev
    per = n_dev // n_outer
    span = per * blk
    n_chip = n_dev // 2
    dma = pltpu.SemaphoreType.DMA
    return (
        [
            pltpu.VMEM((n_dev, rows, cols), BF16),
            pltpu.VMEM((rows, rank), BF16),
            pltpu.VMEM((rows, span), BF16),
            pltpu.VMEM((rows, cols), F32),
            pltpu.VMEM((2, per, blk, cols), F32),
            pltpu.VMEM((n_dev, blk, span), F32),
            pltpu.VMEM((n_chip, blk, span), F32),
            pltpu.VMEM((n_chip, blk, span), F32),
            pltpu.VMEM((n_chip, blk, span), F32),
            pltpu.VMEM((2, blk, cols), F32),
            pltpu.VMEM((n_outer, 2, blk, cols), F32),
            pltpu.VMEM((n_dev, blk, cols), F32),
            pltpu.VMEM((n_chip, blk, cols), F32),
            pltpu.VMEM((n_chip, blk, cols), F32),
            pltpu.VMEM((n_chip, blk, cols), F32),
            pltpu.VMEM((blk, cols), F32),
            pltpu.VMEM((n_outer, blk, cols), F32),
            pltpu.VMEM((n_dev, blk, cols), BF16),
            dma((6,)),
            dma((per,)),
            dma((chunks, n_dev)),
            dma((chunks, n_dev)),
            dma((2, per, n_chip)),
            dma((2, per)),
            dma((2, per)),
            dma((2, per)),
        ]
        + [dma((n_chip,))] * 4
        + [dma((n_outer,))] * 2
        + [dma((parts, n_chip))] * 4
        + [dma((parts, n_outer))] * 2
        + [dma((parts, n_dev))] * 2
    )


def hand_over(weight_in, m_in, v_in, weight_out, m_out, v_out):
    weight_out[...] = weight_in[...]
    m_out[...] = m_in[...]
    v_out[...] = v_in[...]


def on_device(n_outer, n_dev, partials, p_old, p_new, weight, m_old, v_old):
    rows, cols = weight.shape
    rank = p_new.shape[1]
    blk = rank // n_dev
    per = n_dev // n_outer
    span = per * blk
    n_chip = n_dev // 2
    squared = n_chip == 4 and n_dev % n_outer == 0 and n_outer % 2 == 0 and rows % 64 == 0 and blk % 128 == 0 and pieces == 2 and blk % (16 * pieces * n_outer) == 0
    if blk % 128 and not squared:
        z = lax.axis_index("outer")
        p_old = jnp.concatenate(
            [
                lax.dynamic_slice_in_dim(p_old, (k * n_outer + z) * blk, blk, axis=1)
                for k in range(per)
            ],
            axis=1,
        )
    anywhere = pl.BlockSpec(memory_space=pltpu.HBM)
    vmem = pl.BlockSpec(memory_space=pltpu.VMEM)
    if squared:
        body, scratch = square_kernel, square_scratch(n_outer, n_dev, rows, cols, rank)
    else:
        body, scratch = kernel, plain_scratch(n_outer, n_dev, rows, cols, rank)
    operands = (partials[0], p_old, p_new, weight, m_old, v_old)
    results = pl.pallas_call(
        functools.partial(body, n_outer, n_dev),
        out_shape=(
            jax.ShapeDtypeStruct((rows, cols), F32),
            jax.ShapeDtypeStruct((blk, cols), F32),
            jax.ShapeDtypeStruct((blk, cols), F32),
        ),
        in_specs=[anywhere] * 6,
        out_specs=(vmem, vmem, vmem),
        scratch_shapes=scratch,
        compiler_params=pltpu.CompilerParams(
            collective_id=0, has_side_effects=True, vmem_limit_bytes=vmem_limit
        ),
    )(*[pltpu.with_memory_space_constraint(a, pltpu.HBM) for a in operands])
    return pl.pallas_call(
        hand_over,
        out_shape=tuple(jax.ShapeDtypeStruct(r.shape, r.dtype) for r in results),
        in_specs=[vmem] * 3,
        out_specs=(vmem,) * 3,
        compiler_params=pltpu.CompilerParams(vmem_limit_bytes=finish_limit),
    )(*results)


def solution(mesh):
    in_specs = (
        P(("outer", "dev"), None, None),
        P("dev", None),
        P("dev", None),
        P("dev", None),
        P("dev", None),
        P("dev", None),
    )
    out_specs = (P("dev", None), P("dev", None), P("dev", None))
    return jax.shard_map(
        functools.partial(on_device, mesh.shape["outer"], mesh.shape["dev"]),
        mesh=mesh,
        in_specs=in_specs,
        out_specs=out_specs,
        check_vma=False,
    )
```

```python
import functools

import jax
import jax.numpy as jnp
from jax import lax
from jax.experimental import pallas as pl
from jax.experimental.pallas import tpu as pltpu
from jax.sharding import PartitionSpec as P

beta_mean = 0.9
beta_square = 0.95
bias_mean = 0.9999734386011124
bias_square = 0.9940794707796659
adam_epsilon = 1e-08
step_scale = 0.5

chunks = 2
early = 1
parts = 2
pieces = 2
shared_part = (7, 32)
vmem_limit = 50331648
finish_limit = 4194304

MESH = pl.DeviceIdType.MESH
F32 = jnp.float32
BF16 = jnp.bfloat16


def contract_rows(a, b):
    return lax.dot_general(a, b, (((0,), (0,)), ((), ())), preferred_element_type=F32)


def kernel(
    n_outer,
    n_dev,
    partials,
    p_old,
    p_new,
    weight,
    m_old,
    v_old,
    new_weight,
    m_new,
    v_new,
    grads,
    basis,
    basis_old,
    weights,
    moments,
    margin,
    margin_partner,
    margin_sum,
    margin_in,
    rotated,
    rotated_in,
    projected,
    projected_partner,
    projected_sum,
    projected_in,
    block,
    block_in,
    direction,
    load_sem,
    old_sem,
    grad_send,
    grad_recv,
    mom_send,
    mom_recv,
    fwd_send,
    fwd_recv,
    mp_send,
    mp_recv,
    ms_send,
    ms_recv,
    rot_send,
    rot_recv,
    pp_send,
    pp_recv,
    ps_send,
    ps_recv,
    blk_send,
    blk_recv,
    dir_send,
    dir_recv,
):
    z = lax.axis_index("outer")
    d = lax.axis_index("dev")
    n_chip = n_dev // 2
    q = d // 2
    c = d % 2
    partner = q * 2 + 1 - c
    rows, cols = weight.shape
    rank = p_new.shape[1]
    blk = rank // n_dev
    per = n_dev // n_outer

    def remote(src, dst, send, recv, where):
        return pltpu.make_async_remote_copy(
            src_ref=src, dst_ref=dst, send_sem=send, recv_sem=recv, device_id=where, device_id_type=MESH
        )

    barrier = pltpu.get_barrier_semaphore()
    for j in range(1, n_dev):
        pl.semaphore_signal(barrier, inc=1, device_id=(z, lax.rem(d + j, n_dev)), device_id_type=MESH)
    for j in range(1, n_outer):
        pl.semaphore_signal(barrier, inc=1, device_id=(lax.rem(z + j, n_outer), d), device_id_type=MESH)

    load_new = pltpu.make_async_copy(p_new, basis, load_sem.at[0])
    load_new.start()
    if p_old.shape[1] == per * blk:
        old_loads = [pltpu.make_async_copy(p_old, basis_old, old_sem.at[0])]
    else:
        old_loads = [
            pltpu.make_async_copy(
                p_old.at[:, pl.ds(pl.multiple_of((k * n_outer + z) * blk, blk), blk)],
                basis_old.at[:, k * blk : (k + 1) * blk],
                old_sem.at[k],
            )
            for k in range(per)
        ]
    for load in old_loads:
        load.start()
    load_weight = pltpu.make_async_copy(weight, weights, load_sem.at[2])
    load_weight.start()
    load_own = pltpu.make_async_copy(
        partials.at[pl.ds(pl.multiple_of(d * rows, rows), rows)], grads.at[0], load_sem.at[3]
    )
    load_own.start()

    pl.semaphore_wait(barrier, n_dev - 1 + n_outer - 1)

    def moment_copies(k, owner):
        copies = []
        for j in range(1, n_chip):
            to = (z, lax.rem(q + j, n_chip) * 2 + c)
            for i, src in enumerate((m_old, v_old)):
                copies.append(remote(src, moments.at[i, k], mom_send.at[i, k, j], mom_recv.at[i, k], to))
        return copies

    for k in range(per):
        owner = k * n_outer + z

        @pl.when(d == owner)
        def _():
            for copy in moment_copies(k, owner):
                copy.start()
            for i, src in enumerate((m_old, v_old)):
                pltpu.make_async_copy(src, moments.at[i, k], load_sem.at[4 + i]).start()

    tall = rows // chunks

    def send_gradients(chunk):
        copies = []
        for j in range(1, n_dev):
            to = lax.rem(d + j, n_dev)
            copy = remote(
                partials.at[pl.ds(pl.multiple_of(to * rows + chunk * tall, tall), tall)],
                grads.at[j, chunk * tall : (chunk + 1) * tall],
                grad_send.at[chunk, j],
                grad_recv.at[chunk, j],
                (z, to),
            )
            copy.start()
            copies.append(copy)
        return copies

    grad_copies = [send_gradients(chunk) for chunk in range(early)]

    load_new.wait()
    for load in old_loads:
        load.wait()
    width = min(rank, 256)
    for s in range(0, rank, width):
        part = contract_rows(basis[:, s : s + width], basis_old[...])
        margin[s // blk : (s + width) // blk] = part.reshape(width // blk, blk, part.shape[1])

    def scatter_start(val, prt, send, recv):
        copies = []
        for j in list(range(1, n_chip)) + [0]:
            k = lax.rem(q + j, n_chip)
            copy = remote(val.at[2 * k + 1 - c], prt.at[j], send.at[j], recv.at[j], (z, partner))
            copy.start()
            copies.append((j, k, copy))
        return copies

    def scatter_middle(pairs, val, prt, tot, arr, send, recv):
        copies = []
        for j, k, pair in pairs:
            pair.wait_recv()
            tot[j] = val[2 * k + c] + prt[j]
            if j:
                copy = remote(tot.at[j], arr.at[j], send.at[j], recv.at[j], (z, 2 * k + c))
                copy.start()
                copies.append((j, copy))
        return copies

    def scatter_end(copies, tot, arr):
        total = tot[0]
        for j, copy in copies:
            copy.wait_recv()
            total = total + arr[j]
        return total

    margin_pairs = scatter_start(margin, margin_partner, mp_send, mp_recv)

    for k in range(per):
        owner = k * n_outer + z
        mine = c == owner % 2

        @pl.when(d == owner)
        def _():
            for i, src in enumerate((m_old, v_old)):
                pltpu.make_async_copy(src, moments.at[i, k], load_sem.at[4 + i]).wait()

        @pl.when(jnp.logical_and(mine, d != owner))
        def _():
            for i, src in enumerate((m_old, v_old)):
                remote(src, moments.at[i, k], mom_send.at[i, k, 0], mom_recv.at[i, k], (z, d)).wait_recv()

        @pl.when(mine)
        def _():
            for i in range(2):
                remote(
                    moments.at[i, k], moments.at[i, k], fwd_send.at[i, k], fwd_recv.at[i, k], (z, partner)
                ).start()

    margin_copies = scatter_middle(
        margin_pairs, margin, margin_partner, margin_sum, margin_in, ms_send, ms_recv
    )

    for chunk in range(early, chunks):
        grad_copies.append(send_gradients(chunk))

    for k in range(per):
        mine = c == (k * n_outer + z) % 2

        @pl.when(jnp.logical_not(mine))
        def _():
            for i in range(2):
                remote(
                    moments.at[i, k], moments.at[i, k], fwd_send.at[i, k], fwd_recv.at[i, k], (z, partner)
                ).wait_recv()

    margin_rows = scatter_end(margin_copies, margin_sum, margin_in)
    old = moments[...].reshape(2, per * blk, cols)
    rotated[0] = jnp.dot(margin_rows, old[0], precision=lax.Precision.HIGHEST, preferred_element_type=F32)
    rotated[1] = jnp.dot(
        margin_rows * margin_rows, old[1], precision=lax.Precision.HIGHEST, preferred_element_type=F32
    )
    rot_copies = []
    for j in range(1, n_outer):
        copy = remote(
            rotated, rotated_in.at[j], rot_send.at[j], rot_recv.at[j], (lax.rem(z + j, n_outer), d)
        )
        copy.start()
        rot_copies.append(copy)

    load_own.wait()
    for chunk in range(chunks):
        for copy in grad_copies[chunk]:
            copy.wait_recv()
        part_rows = slice(chunk * tall, (chunk + 1) * tall)
        total = grads[0, part_rows].astype(F32)
        for j in range(1, n_dev):
            total = total + grads[j, part_rows].astype(F32)
        high = total.astype(BF16)
        low = (total - high.astype(F32)).astype(BF16)
        both = jnp.concatenate([high, low], axis=1)
        for s in range(0, rank, width):
            part = contract_rows(basis[part_rows, s : s + width], both)
            part = (part[:, :cols] + part[:, cols:]).reshape(width // blk, blk, cols)
            blocks = slice(s // blk, (s + width) // blk)
            projected[blocks] = part if chunk == 0 else projected[blocks] + part
    half = blk // parts
    views = [slice(h * half, (h + 1) * half) for h in range(parts)]
    pairs = [
        scatter_start(projected.at[:, v], projected_partner.at[:, v], pp_send.at[h], pp_recv.at[h])
        for h, v in enumerate(views)
    ]
    copies = [
        scatter_middle(
            pairs[h],
            projected.at[:, v],
            projected_partner.at[:, v],
            projected_sum.at[:, v],
            projected_in.at[:, v],
            ps_send.at[h],
            ps_recv.at[h],
        )
        for h, v in enumerate(views)
    ]
    blk_copies = []
    for h, v in enumerate(views):
        block[v] = scatter_end(copies[h], projected_sum.at[:, v], projected_in.at[:, v])
        for j in range(1, n_outer):
            copy = remote(
                block.at[v],
                block_in.at[j, v],
                blk_send.at[h, j],
                blk_recv.at[h, j],
                (lax.rem(z + j, n_outer), d),
            )
            copy.start()
            blk_copies.append(copy)
    for copy in rot_copies:
        copy.wait_recv()
    dir_copies = []
    for h, v in enumerate(views):
        for copy in blk_copies[h * (n_outer - 1) : (h + 1) * (n_outer - 1)]:
            copy.wait_recv()
        first = rotated[0, v]
        second = rotated[1, v]
        proj = block[v]
        for j in range(1, n_outer):
            first = first + rotated_in[j, 0, v]
            second = second + rotated_in[j, 1, v]
            proj = proj + block_in[j, v]
        mean = beta_mean * first + (1.0 - beta_mean) * proj
        square = beta_square * second + (1.0 - beta_square) * proj * proj
        m_new[v] = mean
        v_new[v] = square
        direction[d, v] = (mean / bias_mean / (jnp.sqrt(square / bias_square) + adam_epsilon)).astype(BF16)
        for j in range(1, n_dev):
            copy = remote(
                direction.at[d, v],
                direction.at[d, v],
                dir_send.at[h, j],
                dir_recv.at[h, j],
                (z, lax.rem(d + j, n_dev)),
            )
            copy.start()
            dir_copies.append(copy)
    load_weight.wait()
    for copy in dir_copies:
        copy.wait_recv()
    directions = direction[...].reshape(rank, cols)
    tall = min(rows, 256)
    for s in range(0, rows, tall):
        update = jnp.dot(basis[s : s + tall, :], directions, preferred_element_type=F32)
        new_weight[s : s + tall, :] = weights[s : s + tall, :] - step_scale * update

    for k in range(per):
        owner = k * n_outer + z
        mine = c == owner % 2

        @pl.when(d == owner)
        def _():
            for copy in moment_copies(k, owner):
                copy.wait_send()

        @pl.when(mine)
        def _():
            for i in range(2):
                remote(
                    moments.at[i, k], moments.at[i, k], fwd_send.at[i, k], fwd_recv.at[i, k], (z, partner)
                ).wait_send()

    for copy in sum(grad_copies, []) + rot_copies + blk_copies + dir_copies:
        copy.wait_send()
    for group in [margin_pairs] + pairs:
        for _, _, copy in group:
            copy.wait_send()
    for group in [margin_copies] + copies:
        for _, copy in group:
            copy.wait_send()

class Copies:
    def __init__(self, send, recv):
        self.send, self.recv, self.started = send, recv, []

    def start(self, src, dst, to):
        i = len(self.started)
        copy = pltpu.make_async_remote_copy(
            src_ref=src,
            dst_ref=dst,
            send_sem=self.send.at[i],
            recv_sem=self.recv.at[i],
            device_id=to,
            device_id_type=MESH,
        )
        copy.start()
        self.started.append(copy)
        return copy


def square_kernel(
    n_outer,
    n_dev,
    partials,
    p_old,
    p_new,
    weight,
    m_old,
    v_old,
    new_weight,
    m_new,
    v_new,
    own,
    pair,
    plane_own,
    plane_pair,
    far_sum,
    relay_in,
    direct_out,
    direct_in,
    merged,
    merged_in,
    terms,
    basis,
    basis_old,
    weights,
    moments,
    margin,
    margin_partner,
    margin_sum,
    margin_in,
    margin_relay,
    rotated,
    rotated_in,
    projected,
    projected_partner,
    projected_sum,
    projected_in,
    block,
    block_in,
    column,
    column_in,
    chip_in,
    direction,
    moments_new,
    load_sem,
    old_sem,
    own_sem,
    mom_send,
    mom_recv,
    fwd_send,
    fwd_recv,
    send_sem,
    recv_sem,
    merge_send,
    merge_recv,
    line_sem,
):
    z = lax.axis_index("outer")
    d = lax.axis_index("dev")
    q = d // 2
    c = d % 2
    partner = q * 2 + 1 - c
    side = q + 1 - 2 * (q % 2)
    over = lax.rem(q + 2, 4)
    far = lax.rem(side + 2, 4)
    chips = (far, side, over, q)
    rows, cols = weight.shape
    rank = p_new.shape[1]
    blk = rank // n_dev
    sub = blk // n_outer
    fine = sub // pieces
    few = shared_rows(rows)
    many = rows - 2 * few
    kept = few + many
    mate = z + 1 - 2 * (z % 2)
    odd = z % 2
    window = odd * few
    group_of = odd
    turn = z // 2
    few_at = odd * many
    many_at = few - window
    given_at = (1 - odd) * kept
    copies = Copies(send_sem, recv_sem)
    above = (2 * n_outer - 2 - z) // n_outer
    below = (z + n_outer - 1) // n_outer

    def signal_line(sem):
        @pl.when(z > 0)
        def _():
            pl.semaphore_signal(sem, inc=1, device_id=(z - 1, d), device_id_type=MESH)

        @pl.when(z < n_outer - 1)
        def _():
            pl.semaphore_signal(sem, inc=1, device_id=(z + 1, d), device_id_type=MESH)

    def pass_along(steps):
        for r in steps:
            pl.semaphore_wait(line_sem.at[r], above + below)
            if r + 1 < n_outer - 2:
                signal_line(line_sem.at[r + 1])

    barrier = pltpu.get_barrier_semaphore()
    for to in (partner, 2 * side + c, 2 * over + c):
        pl.semaphore_signal(barrier, inc=1, device_id=(z, to), device_id_type=MESH)
    pl.semaphore_signal(barrier, inc=1, device_id=(mate, partner), device_id_type=MESH)
    signal_line(barrier)

    def rows_of(to, start, count):
        return partials.at[pl.ds(pl.multiple_of(to * rows + start, 16), count)]

    own_loads = [
        pltpu.make_async_copy(rows_of(2 * k + c, window, kept), own.at[i], own_sem.at[i])
        for i, k in enumerate(chips)
    ]
    own_loads[0].start()
    pl.semaphore_wait(barrier, 4 + above + below)

    def moment_copy(i, j):
        return pltpu.make_async_remote_copy(
            src_ref=(m_old, v_old)[i],
            dst_ref=moments.at[i, q],
            send_sem=mom_send.at[i, j],
            recv_sem=mom_recv.at[i, j],
            device_id=(z, 2 * (side, over)[j] + c),
            device_id_type=MESH,
        )

    def moment_relay(i):
        came_from = (side, over)[i]
        return pltpu.make_async_remote_copy(
            src_ref=moments.at[i, came_from],
            dst_ref=moments.at[i, came_from],
            send_sem=mom_send.at[i, 2],
            recv_sem=mom_recv.at[i, 2],
            device_id=(z, 2 * (over, side)[i] + c),
            device_id_type=MESH,
        )

    def moment_load(i):
        return pltpu.make_async_copy((m_old, v_old)[i], moments.at[i, q], load_sem.at[2 + i])

    moment_forward = pltpu.make_async_remote_copy(
        src_ref=moments,
        dst_ref=moments,
        send_sem=fwd_send,
        recv_sem=fwd_recv,
        device_id=(z, partner),
        device_id_type=MESH,
    )

    def pair_start(i):
        own_rows = rows_of(2 * chips[i] + 1 - c, window, kept)
        return copies.start(own_rows, pair.at[i], (z, partner))

    def cross_start(i):
        return [
            copies.start(rows_of(2 * chips[i] + c, given_at, few), plane_own.at[i], (mate, d)),
            copies.start(rows_of(2 * chips[i] + 1 - c, given_at, few), plane_pair.at[i], (mate, partner)),
        ]

    pairs = [pair_start(0)]
    crossed = [cross_start(0)]
    for i in (1, 2):
        own_loads[i].start()
        pairs.append(pair_start(i))
    @pl.when(c == group_of)
    def _():
        for j in range(2):
            for i in range(2):
                moment_copy(i, j).start()
        for i in range(2):
            moment_load(i).start()

    arrived = set()

    def arrive(i, group):
        if i not in arrived:
            arrived.add(i)
            pairs[i].wait_recv()
            own_loads[i].wait()
        if group == 0:
            for copy in crossed[i]:
                copy.wait_recv()

    def rows_at(group, h):
        start, count = ((few_at, few // 2), (many_at, many // 2))[group]
        return pl.ds(pl.multiple_of(start + h * count, 16), count)

    def chip_sum(i, h):
        at = rows_at(1, h)
        return own[i, at].astype(F32) + pair[i, at].astype(F32)

    def plane_sum(i, h):
        at, near = rows_at(0, h), slice(h * few // 2, (h + 1) * few // 2)
        total = own[i, at].astype(F32) + pair[i, at].astype(F32)
        return total + (plane_own[i, near].astype(F32) + plane_pair[i, near].astype(F32))

    sums = (plane_sum, chip_sum)
    merging = Copies(merge_send, merge_recv)
    relays, directs, merges = {}, {}, {}

    def send_far(group):
        arrive(0, group)
        for h, chip in enumerate((side, over)):
            at = rows_at(group, h)
            far_sum[at] = sums[group](0, h).astype(BF16)
            relays[group, h] = copies.start(far_sum.at[at], relay_in.at[at], (z, 2 * chip + c))

    def send_direct(group):
        for h, chip in enumerate((side, over)):
            arrive(1 + h, group)
            at = rows_at(group, h)
            direct_out[at] = sums[group](1 + h, h).astype(BF16)
            directs[group, h] = copies.start(direct_out.at[at], direct_in.at[at], (z, 2 * chip + c))

    def send_merged(group):
        for h, (i, chip) in enumerate(((2, over), (1, side))):
            at = rows_at(group, h)
            relays[group, h].wait_recv()
            merged[at] = sums[group](i, h) + relay_in[at].astype(F32)
            merges[group, h] = merging.start(merged.at[at], merged_in.at[at], (z, 2 * chip + c))

    send_far(1)
    crossed += [cross_start(1), cross_start(2)]
    send_direct(1)
    load_new = pltpu.make_async_copy(p_new, basis, load_sem.at[0])
    load_new.start()
    old_loads = [
        pltpu.make_async_copy(
            p_old.at[:, pl.ds(pl.multiple_of((2 * k + group_of) * blk, blk), blk)],
            basis_old.at[:, k * blk : (k + 1) * blk],
            old_sem.at[k],
        )
        for k in range(4)
    ]
    for load in old_loads:
        load.start()
    own_loads[3].start()
    load_weight = pltpu.make_async_copy(weight, weights, load_sem.at[1])
    load_weight.start()
    pairs.append(pair_start(3))
    crossed.append(cross_start(3))
    if n_outer > 2:
        signal_line(line_sem.at[0])

    load_new.wait()
    for load in old_loads:
        load.wait()

    def chip_ranks(k):
        return pl.ds(pl.multiple_of(k * 2 * blk, 2 * blk), 2 * blk)

    for i, k in enumerate(chips):
        part = contract_rows(basis[:, chip_ranks(k)], basis_old[...])
        margin[:, i] = part.reshape(2, n_outer // 2, 2, sub, 4 * blk)
    margin_pair = copies.start(margin.at[1 - c, :, turn], margin_partner, (z, partner))

    send_far(0)
    send_merged(1)
    margin_pair.wait_recv()
    margin_sum[...] = margin[c, :, turn] + margin_partner[...]

    @pl.when(c == group_of)
    def _():
        for i in range(2):
            moment_copy(i, i).wait_recv()
            moment_relay(i).start()

    send_direct(0)
    send_merged(0)
    for copy in merging.started:
        copy.wait_send()
    margin_relays = [
        copies.start(margin_sum.at[0, h], margin_relay.at[h], (z, 2 * chip + c))
        for h, chip in enumerate((side, over))
    ]
    margin_copies = [
        copies.start(margin_sum.at[1 + h, h], margin_in.at[0, h], (z, 2 * chip + c))
        for h, chip in enumerate((side, over))
    ]

    for group in (1, 0):
        arrive(3, group)
        for h in range(2):
            at = rows_at(group, h)
            directs[group, h].wait_recv()
            total = sums[group](3, h) + direct_in[at].astype(F32)
            merges[group, h].wait_recv()
            total = total + merged_in[at]
            high = total.astype(BF16)
            terms[at, :cols] = high
            terms[at, cols:] = (total - high.astype(F32)).astype(BF16)

    for i, k in enumerate(chips):
        kept_rows = pl.ds(pl.multiple_of(window, 16), kept)
        part = contract_rows(basis[kept_rows, chip_ranks(k)], terms[...])
        part = (part[:, :cols] + part[:, cols:]).reshape(2, n_outer, pieces, fine, cols)
        for h in range(pieces):
            projected[h, :, i] = part[:, :, h]
    projected_pairs = [
        copies.start(projected.at[h, 1 - c], projected_partner.at[h], (z, partner)) for h in range(pieces)
    ]
    for h, (i, chip) in enumerate(((2, over), (1, side))):
        margin_relays[h].wait_recv()
        margin_sum[i, h] = margin_sum[i, h] + margin_relay[h]
        margin_copies.append(copies.start(margin_sum.at[i, h], margin_in.at[1, h], (z, 2 * chip + c)))

    planes = [lax.rem(z + j, n_outer) for j in range(1, n_outer)]
    pass_along(range(n_outer - 2))
    projected_pairs[0].wait_recv()
    projected_copies = []
    for i, k in enumerate(chips):
        projected_sum[0, i] = projected[0, c, i] + projected_partner[0, i]
        if i < 3:
            projected_copies.append(
                copies.start(projected_sum.at[0, i], projected_in.at[i], (z, 2 * k + c))
            )
    projected_pairs[1].wait_recv()
    projected_sum[1] = projected[1, c] + projected_partner[1]
    column_copies = [
        copies.start(projected_sum.at[1, :, to], column_in.at[j], (to, d)) for j, to in enumerate(planes)
    ]

    @pl.when(c == group_of)
    def _():
        for i in range(2):
            moment_load(i).wait()
            moment_copy(i, 1 - i).wait_recv()
            moment_relay(i).wait_recv()
        moment_forward.start()

    @pl.when(c != group_of)
    def _():
        moment_forward.wait_recv()

    for copy in projected_copies:
        copy.wait_recv()
    block[...] = projected_sum[0, 3] + projected_in[0] + projected_in[1] + projected_in[2]
    block_copies = [copies.start(block.at[to], block_in.at[j], (to, d)) for j, to in enumerate(planes)]
    for copy in margin_copies:
        copy.wait_recv()
    margin_rows = margin_sum[3] + margin_in[0] + margin_in[1]
    margin_rows = margin_rows.reshape(2 * sub, 4 * blk)
    old = moments[...].reshape(2, 4 * blk, cols)
    for i, rows_in in enumerate((margin_rows, margin_rows * margin_rows)):
        turned = jnp.dot(rows_in, old[i], precision=lax.Precision.HIGHEST, preferred_element_type=F32)
        rotated[:, i] = turned.reshape(2, sub, cols)
    rot_copy = copies.start(rotated.at[1 - group_of], rotated_in, (mate, d))

    for copy in column_copies:
        copy.wait_recv()
    for i in range(4):
        total = projected_sum[1, i, z]
        for j in range(n_outer - 1):
            total = total + column_in[j, i]
        column[i] = total
    chip_copies = [
        copies.start(column.at[i], chip_in.at[i], (z, 2 * k + c)) for i, k in enumerate(chips[:3])
    ]

    rot_copy.wait_recv()
    first = rotated[group_of, 0] + rotated_in[0]
    second = rotated[group_of, 1] + rotated_in[1]
    for h in range(pieces):
        at = slice(h * fine, (h + 1) * fine)
        if h == 0:
            proj = block[z]
            for j, copy in enumerate(block_copies):
                copy.wait_recv()
                proj = proj + block_in[j]
        else:
            proj = column[3]
            for i, copy in enumerate(chip_copies):
                copy.wait_recv()
                proj = proj + chip_in[i]
        mean = beta_mean * first[at] + (1.0 - beta_mean) * proj
        square = beta_square * second[at] + (1.0 - beta_square) * proj * proj
        moments_new[z, 0, at] = mean
        moments_new[z, 1, at] = square
        direction[d, z, at] = (
            mean / bias_mean / (jnp.sqrt(square / bias_square) + adam_epsilon)
        ).astype(BF16)

    settled = len(copies.started)
    spread = []
    for i, k in enumerate(chips):
        group = []
        for to in planes + [z]:
            if i == 3 and to is z:
                continue
            group.append(copies.start(direction.at[d, z], direction.at[d, z], (to, 2 * k + c)))
        spread.append(group)
    moment_spread = [copies.start(moments_new.at[z], moments_new.at[z], (to, d)) for to in planes]
    for copy in copies.started[:settled]:
        copy.wait_send()

    @pl.when(c == group_of)
    def _():
        for i in range(2):
            for j in range(2):
                moment_copy(i, j).wait_send()
            moment_relay(i).wait_send()
        moment_forward.wait_send()

    forwards = []
    for i in (3, 1, 2, 0):
        for copy in spread[i]:
            copy.wait_recv()
        mine = direction.at[2 * chips[i] + c]
        forwards.append(copies.start(mine, mine, (z, partner)))
    load_weight.wait()
    for copy in sum(spread, moment_spread):
        copy.wait_send()
    for copy in forwards:
        copy.wait_recv()
    directions = direction[...].reshape(rank, cols)
    tall = min(rows, 256)
    for s in range(0, rows, tall):
        update = jnp.dot(basis[s : s + tall, :], directions, preferred_element_type=F32)
        new_weight[s : s + tall, :] = weights[s : s + tall, :] - step_scale * update
    for copy in moment_spread:
        copy.wait_recv()
    m_new[...] = moments_new[:, 0].reshape(blk, cols)
    v_new[...] = moments_new[:, 1].reshape(blk, cols)

    for copy in forwards:
        copy.wait_send()


def shared_rows(rows):
    top, bottom = shared_part
    return rows * top // bottom // 32 * 32


def square_scratch(n_outer, n_dev, rows, cols, rank):
    blk = rank // n_dev
    sub = blk // n_outer
    fine = sub // pieces
    span = 4 * blk
    dma = pltpu.SemaphoreType.DMA
    few = shared_rows(rows)
    kept = rows - few
    count = 50 + 15 * pieces + 6 * n_outer
    return [
        pltpu.VMEM((4, kept, cols), BF16),
        pltpu.VMEM((4, kept, cols), BF16),
        pltpu.VMEM((4, few, cols), BF16),
        pltpu.VMEM((4, few, cols), BF16),
        pltpu.VMEM((kept, cols), BF16),
        pltpu.VMEM((kept, cols), BF16),
        pltpu.VMEM((kept, cols), BF16),
        pltpu.VMEM((kept, cols), BF16),
        pltpu.VMEM((kept, cols), F32),
        pltpu.VMEM((kept, cols), F32),
        pltpu.VMEM((kept, 2 * cols), BF16),
        pltpu.VMEM((rows, rank), BF16),
        pltpu.VMEM((rows, span), BF16),
        pltpu.VMEM((rows, cols), F32),
        pltpu.VMEM((2, 4, blk, cols), F32),
        pltpu.VMEM((2, 4, n_outer // 2, 2, sub, span), F32),
        pltpu.VMEM((4, 2, sub, span), F32),
        pltpu.VMEM((4, 2, sub, span), F32),
        pltpu.VMEM((2, 2, sub, span), F32),
        pltpu.VMEM((2, sub, span), F32),
        pltpu.VMEM((2, 2, sub, cols), F32),
        pltpu.VMEM((2, sub, cols), F32),
        pltpu.VMEM((pieces, 2, 4, n_outer, fine, cols), F32),
        pltpu.VMEM((pieces, 4, n_outer, fine, cols), F32),
        pltpu.VMEM((pieces, 4, n_outer, fine, cols), F32),
        pltpu.VMEM((3, n_outer, fine, cols), F32),
        pltpu.VMEM((n_outer, fine, cols), F32),
        pltpu.VMEM((n_outer - 1, fine, cols), F32),
        pltpu.VMEM((4, fine, cols), F32),
        pltpu.VMEM((n_outer - 1, 4, fine, cols), F32),
        pltpu.VMEM((3, fine, cols), F32),
        pltpu.VMEM((n_dev, n_outer, sub, cols), BF16),
        pltpu.VMEM((n_outer, 2, sub, cols), F32),
        dma((4,)),
        dma((4,)),
        dma((4,)),
        dma((2, 3)),
        dma((2, 3)),
        dma,
        dma,
        dma((count,)),
        dma((count,)),
        dma((4,)),
        dma((4,)),
        pltpu.SemaphoreType.REGULAR((max(n_outer - 2, 1),)),
    ]


def plain_scratch(n_outer, n_dev, rows, cols, rank):
    blk = rank // n_dev
    per = n_dev // n_outer
    span = per * blk
    n_chip = n_dev // 2
    dma = pltpu.SemaphoreType.DMA
    return (
        [
            pltpu.VMEM((n_dev, rows, cols), BF16),
            pltpu.VMEM((rows, rank), BF16),
            pltpu.VMEM((rows, span), BF16),
            pltpu.VMEM((rows, cols), F32),
            pltpu.VMEM((2, per, blk, cols), F32),
            pltpu.VMEM((n_dev, blk, span), F32),
            pltpu.VMEM((n_chip, blk, span), F32),
            pltpu.VMEM((n_chip, blk, span), F32),
            pltpu.VMEM((n_chip, blk, span), F32),
            pltpu.VMEM((2, blk, cols), F32),
            pltpu.VMEM((n_outer, 2, blk, cols), F32),
            pltpu.VMEM((n_dev, blk, cols), F32),
            pltpu.VMEM((n_chip, blk, cols), F32),
            pltpu.VMEM((n_chip, blk, cols), F32),
            pltpu.VMEM((n_chip, blk, cols), F32),
            pltpu.VMEM((blk, cols), F32),
            pltpu.VMEM((n_outer, blk, cols), F32),
            pltpu.VMEM((n_dev, blk, cols), BF16),
            dma((6,)),
            dma((per,)),
            dma((chunks, n_dev)),
            dma((chunks, n_dev)),
            dma((2, per, n_chip)),
            dma((2, per)),
            dma((2, per)),
            dma((2, per)),
        ]
        + [dma((n_chip,))] * 4
        + [dma((n_outer,))] * 2
        + [dma((parts, n_chip))] * 4
        + [dma((parts, n_outer))] * 2
        + [dma((parts, n_dev))] * 2
    )


def hand_over(weight_in, m_in, v_in, weight_out, m_out, v_out):
    weight_out[...] = weight_in[...]
    m_out[...] = m_in[...]
    v_out[...] = v_in[...]


def on_device(n_outer, n_dev, partials, p_old, p_new, weight, m_old, v_old):
    rows, cols = weight.shape
    rank = p_new.shape[1]
    blk = rank // n_dev
    per = n_dev // n_outer
    span = per * blk
    n_chip = n_dev // 2
    squared = n_chip == 4 and n_dev % n_outer == 0 and n_outer % 2 == 0 and rows % 64 == 0 and blk % 128 == 0 and pieces == 2 and blk % (16 * pieces * n_outer) == 0
    if blk % 128 and not squared:
        z = lax.axis_index("outer")
        p_old = jnp.concatenate(
            [
                lax.dynamic_slice_in_dim(p_old, (k * n_outer + z) * blk, blk, axis=1)
                for k in range(per)
            ],
            axis=1,
        )
    anywhere = pl.BlockSpec(memory_space=pltpu.HBM)
    vmem = pl.BlockSpec(memory_space=pltpu.VMEM)
    if squared:
        body, scratch = square_kernel, square_scratch(n_outer, n_dev, rows, cols, rank)
    else:
        body, scratch = kernel, plain_scratch(n_outer, n_dev, rows, cols, rank)
    operands = (partials[0], p_old, p_new, weight, m_old, v_old)
    results = pl.pallas_call(
        functools.partial(body, n_outer, n_dev),
        out_shape=(
            jax.ShapeDtypeStruct((rows, cols), F32),
            jax.ShapeDtypeStruct((blk, cols), F32),
            jax.ShapeDtypeStruct((blk, cols), F32),
        ),
        in_specs=[anywhere] * 6,
        out_specs=(vmem, vmem, vmem),
        scratch_shapes=scratch,
        compiler_params=pltpu.CompilerParams(
            collective_id=0, has_side_effects=True, vmem_limit_bytes=vmem_limit
        ),
    )(*[pltpu.with_memory_space_constraint(a, pltpu.HBM) for a in operands])
    return pl.pallas_call(
        hand_over,
        out_shape=tuple(jax.ShapeDtypeStruct(r.shape, r.dtype) for r in results),
        in_specs=[vmem] * 3,
        out_specs=(vmem,) * 3,
        compiler_params=pltpu.CompilerParams(vmem_limit_bytes=finish_limit),
    )(*results)


def solution(mesh):
    in_specs = (
        P(("outer", "dev"), None, None),
        P("dev", None),
        P("dev", None),
        P("dev", None),
        P("dev", None),
        P("dev", None),
    )
    out_specs = (P("dev", None), P("dev", None), P("dev", None))
    return jax.shard_map(
        functools.partial(on_device, mesh.shape["outer"], mesh.shape["dev"]),
        mesh=mesh,
        in_specs=in_specs,
        out_specs=out_specs,
        check_vma=False,
    )
```

```python
import functools

import jax
import jax.numpy as jnp
from jax import lax
from jax.experimental import pallas as pl
from jax.experimental.pallas import tpu as pltpu
from jax.sharding import PartitionSpec as P

beta_mean = 0.9
beta_square = 0.95
bias_mean = 0.9999734386011124
bias_square = 0.9940794707796659
adam_epsilon = 1e-08
step_scale = 0.5

chunks = 2
early = 1
parts = 2
pieces = 2
shared_part = (7, 32)
vmem_limit = 50331648
finish_limit = 4194304

MESH = pl.DeviceIdType.MESH
F32 = jnp.float32
BF16 = jnp.bfloat16


def contract_rows(a, b):
    return lax.dot_general(a, b, (((0,), (0,)), ((), ())), preferred_element_type=F32)


def kernel(
    n_outer,
    n_dev,
    partials,
    p_old,
    p_new,
    weight,
    m_old,
    v_old,
    new_weight,
    m_new,
    v_new,
    grads,
    basis,
    basis_old,
    weights,
    moments,
    margin,
    margin_partner,
    margin_sum,
    margin_in,
    rotated,
    rotated_in,
    projected,
    projected_partner,
    projected_sum,
    projected_in,
    block,
    block_in,
    direction,
    load_sem,
    old_sem,
    grad_send,
    grad_recv,
    mom_send,
    mom_recv,
    fwd_send,
    fwd_recv,
    mp_send,
    mp_recv,
    ms_send,
    ms_recv,
    rot_send,
    rot_recv,
    pp_send,
    pp_recv,
    ps_send,
    ps_recv,
    blk_send,
    blk_recv,
    dir_send,
    dir_recv,
):
    z = lax.axis_index("outer")
    d = lax.axis_index("dev")
    n_chip = n_dev // 2
    q = d // 2
    c = d % 2
    partner = q * 2 + 1 - c
    rows, cols = weight.shape
    rank = p_new.shape[1]
    blk = rank // n_dev
    per = n_dev // n_outer

    def remote(src, dst, send, recv, where):
        return pltpu.make_async_remote_copy(
            src_ref=src, dst_ref=dst, send_sem=send, recv_sem=recv, device_id=where, device_id_type=MESH
        )

    barrier = pltpu.get_barrier_semaphore()
    for j in range(1, n_dev):
        pl.semaphore_signal(barrier, inc=1, device_id=(z, lax.rem(d + j, n_dev)), device_id_type=MESH)
    for j in range(1, n_outer):
        pl.semaphore_signal(barrier, inc=1, device_id=(lax.rem(z + j, n_outer), d), device_id_type=MESH)

    load_new = pltpu.make_async_copy(p_new, basis, load_sem.at[0])
    load_new.start()
    if p_old.shape[1] == per * blk:
        old_loads = [pltpu.make_async_copy(p_old, basis_old, old_sem.at[0])]
    else:
        old_loads = [
            pltpu.make_async_copy(
                p_old.at[:, pl.ds(pl.multiple_of((k * n_outer + z) * blk, blk), blk)],
                basis_old.at[:, k * blk : (k + 1) * blk],
                old_sem.at[k],
            )
            for k in range(per)
        ]
    for load in old_loads:
        load.start()
    load_weight = pltpu.make_async_copy(weight, weights, load_sem.at[2])
    load_weight.start()
    load_own = pltpu.make_async_copy(
        partials.at[pl.ds(pl.multiple_of(d * rows, rows), rows)], grads.at[0], load_sem.at[3]
    )
    load_own.start()

    pl.semaphore_wait(barrier, n_dev - 1 + n_outer - 1)

    def moment_copies(k, owner):
        copies = []
        for j in range(1, n_chip):
            to = (z, lax.rem(q + j, n_chip) * 2 + c)
            for i, src in enumerate((m_old, v_old)):
                copies.append(remote(src, moments.at[i, k], mom_send.at[i, k, j], mom_recv.at[i, k], to))
        return copies

    for k in range(per):
        owner = k * n_outer + z

        @pl.when(d == owner)
        def _():
            for copy in moment_copies(k, owner):
                copy.start()
            for i, src in enumerate((m_old, v_old)):
                pltpu.make_async_copy(src, moments.at[i, k], load_sem.at[4 + i]).start()

    tall = rows // chunks

    def send_gradients(chunk):
        copies = []
        for j in range(1, n_dev):
            to = lax.rem(d + j, n_dev)
            copy = remote(
                partials.at[pl.ds(pl.multiple_of(to * rows + chunk * tall, tall), tall)],
                grads.at[j, chunk * tall : (chunk + 1) * tall],
                grad_send.at[chunk, j],
                grad_recv.at[chunk, j],
                (z, to),
            )
            copy.start()
            copies.append(copy)
        return copies

    grad_copies = [send_gradients(chunk) for chunk in range(early)]

    load_new.wait()
    for load in old_loads:
        load.wait()
    width = min(rank, 256)
    for s in range(0, rank, width):
        part = contract_rows(basis[:, s : s + width], basis_old[...])
        margin[s // blk : (s + width) // blk] = part.reshape(width // blk, blk, part.shape[1])

    def scatter_start(val, prt, send, recv):
        copies = []
        for j in list(range(1, n_chip)) + [0]:
            k = lax.rem(q + j, n_chip)
            copy = remote(val.at[2 * k + 1 - c], prt.at[j], send.at[j], recv.at[j], (z, partner))
            copy.start()
            copies.append((j, k, copy))
        return copies

    def scatter_middle(pairs, val, prt, tot, arr, send, recv):
        copies = []
        for j, k, pair in pairs:
            pair.wait_recv()
            tot[j] = val[2 * k + c] + prt[j]
            if j:
                copy = remote(tot.at[j], arr.at[j], send.at[j], recv.at[j], (z, 2 * k + c))
                copy.start()
                copies.append((j, copy))
        return copies

    def scatter_end(copies, tot, arr):
        total = tot[0]
        for j, copy in copies:
            copy.wait_recv()
            total = total + arr[j]
        return total

    margin_pairs = scatter_start(margin, margin_partner, mp_send, mp_recv)

    for k in range(per):
        owner = k * n_outer + z
        mine = c == owner % 2

        @pl.when(d == owner)
        def _():
            for i, src in enumerate((m_old, v_old)):
                pltpu.make_async_copy(src, moments.at[i, k], load_sem.at[4 + i]).wait()

        @pl.when(jnp.logical_and(mine, d != owner))
        def _():
            for i, src in enumerate((m_old, v_old)):
                remote(src, moments.at[i, k], mom_send.at[i, k, 0], mom_recv.at[i, k], (z, d)).wait_recv()

        @pl.when(mine)
        def _():
            for i in range(2):
                remote(
                    moments.at[i, k], moments.at[i, k], fwd_send.at[i, k], fwd_recv.at[i, k], (z, partner)
                ).start()

    margin_copies = scatter_middle(
        margin_pairs, margin, margin_partner, margin_sum, margin_in, ms_send, ms_recv
    )

    for chunk in range(early, chunks):
        grad_copies.append(send_gradients(chunk))

    for k in range(per):
        mine = c == (k * n_outer + z) % 2

        @pl.when(jnp.logical_not(mine))
        def _():
            for i in range(2):
                remote(
                    moments.at[i, k], moments.at[i, k], fwd_send.at[i, k], fwd_recv.at[i, k], (z, partner)
                ).wait_recv()

    margin_rows = scatter_end(margin_copies, margin_sum, margin_in)
    old = moments[...].reshape(2, per * blk, cols)
    rotated[0] = jnp.dot(margin_rows, old[0], precision=lax.Precision.HIGHEST, preferred_element_type=F32)
    rotated[1] = jnp.dot(
        margin_rows * margin_rows, old[1], precision=lax.Precision.HIGHEST, preferred_element_type=F32
    )
    rot_copies = []
    for j in range(1, n_outer):
        copy = remote(
            rotated, rotated_in.at[j], rot_send.at[j], rot_recv.at[j], (lax.rem(z + j, n_outer), d)
        )
        copy.start()
        rot_copies.append(copy)

    load_own.wait()
    for chunk in range(chunks):
        for copy in grad_copies[chunk]:
            copy.wait_recv()
        part_rows = slice(chunk * tall, (chunk + 1) * tall)
        total = grads[0, part_rows].astype(F32)
        for j in range(1, n_dev):
            total = total + grads[j, part_rows].astype(F32)
        high = total.astype(BF16)
        low = (total - high.astype(F32)).astype(BF16)
        both = jnp.concatenate([high, low], axis=1)
        for s in range(0, rank, width):
            part = contract_rows(basis[part_rows, s : s + width], both)
            part = (part[:, :cols] + part[:, cols:]).reshape(width // blk, blk, cols)
            blocks = slice(s // blk, (s + width) // blk)
            projected[blocks] = part if chunk == 0 else projected[blocks] + part
    half = blk // parts
    views = [slice(h * half, (h + 1) * half) for h in range(parts)]
    pairs = [
        scatter_start(projected.at[:, v], projected_partner.at[:, v], pp_send.at[h], pp_recv.at[h])
        for h, v in enumerate(views)
    ]
    copies = [
        scatter_middle(
            pairs[h],
            projected.at[:, v],
            projected_partner.at[:, v],
            projected_sum.at[:, v],
            projected_in.at[:, v],
            ps_send.at[h],
            ps_recv.at[h],
        )
        for h, v in enumerate(views)
    ]
    blk_copies = []
    for h, v in enumerate(views):
        block[v] = scatter_end(copies[h], projected_sum.at[:, v], projected_in.at[:, v])
        for j in range(1, n_outer):
            copy = remote(
                block.at[v],
                block_in.at[j, v],
                blk_send.at[h, j],
                blk_recv.at[h, j],
                (lax.rem(z + j, n_outer), d),
            )
            copy.start()
            blk_copies.append(copy)
    for copy in rot_copies:
        copy.wait_recv()
    dir_copies = []
    for h, v in enumerate(views):
        for copy in blk_copies[h * (n_outer - 1) : (h + 1) * (n_outer - 1)]:
            copy.wait_recv()
        first = rotated[0, v]
        second = rotated[1, v]
        proj = block[v]
        for j in range(1, n_outer):
            first = first + rotated_in[j, 0, v]
            second = second + rotated_in[j, 1, v]
            proj = proj + block_in[j, v]
        mean = beta_mean * first + (1.0 - beta_mean) * proj
        square = beta_square * second + (1.0 - beta_square) * proj * proj
        m_new[v] = mean
        v_new[v] = square
        direction[d, v] = (mean / bias_mean / (jnp.sqrt(square / bias_square) + adam_epsilon)).astype(BF16)
        for j in range(1, n_dev):
            copy = remote(
                direction.at[d, v],
                direction.at[d, v],
                dir_send.at[h, j],
                dir_recv.at[h, j],
                (z, lax.rem(d + j, n_dev)),
            )
            copy.start()
            dir_copies.append(copy)
    load_weight.wait()
    for copy in dir_copies:
        copy.wait_recv()
    directions = direction[...].reshape(rank, cols)
    tall = min(rows, 256)
    for s in range(0, rows, tall):
        update = jnp.dot(basis[s : s + tall, :], directions, preferred_element_type=F32)
        new_weight[s : s + tall, :] = weights[s : s + tall, :] - step_scale * update

    for k in range(per):
        owner = k * n_outer + z
        mine = c == owner % 2

        @pl.when(d == owner)
        def _():
            for copy in moment_copies(k, owner):
                copy.wait_send()

        @pl.when(mine)
        def _():
            for i in range(2):
                remote(
                    moments.at[i, k], moments.at[i, k], fwd_send.at[i, k], fwd_recv.at[i, k], (z, partner)
                ).wait_send()

    for copy in sum(grad_copies, []) + rot_copies + blk_copies + dir_copies:
        copy.wait_send()
    for group in [margin_pairs] + pairs:
        for _, _, copy in group:
            copy.wait_send()
    for group in [margin_copies] + copies:
        for _, copy in group:
            copy.wait_send()

class Copies:
    def __init__(self, send, recv):
        self.send, self.recv, self.started = send, recv, []

    def start(self, src, dst, to):
        i = len(self.started)
        copy = pltpu.make_async_remote_copy(
            src_ref=src,
            dst_ref=dst,
            send_sem=self.send.at[i],
            recv_sem=self.recv.at[i],
            device_id=to,
            device_id_type=MESH,
        )
        copy.start()
        self.started.append(copy)
        return copy


def square_kernel(
    n_outer,
    n_dev,
    partials,
    p_old,
    p_new,
    weight,
    m_old,
    v_old,
    new_weight,
    m_new,
    v_new,
    own,
    pair,
    plane_own,
    plane_pair,
    far_sum,
    relay_in,
    direct_out,
    direct_in,
    merged,
    merged_in,
    terms,
    basis,
    basis_old,
    weights,
    moments,
    margin,
    margin_partner,
    margin_sum,
    margin_in,
    margin_relay,
    rotated,
    rotated_in,
    projected,
    projected_partner,
    projected_sum,
    projected_in,
    block,
    block_in,
    column,
    column_in,
    chip_in,
    direction,
    moments_new,
    load_sem,
    old_sem,
    own_sem,
    mom_send,
    mom_recv,
    fwd_send,
    fwd_recv,
    send_sem,
    recv_sem,
    merge_send,
    merge_recv,
    line_sem,
):
    z = lax.axis_index("outer")
    d = lax.axis_index("dev")
    q = d // 2
    c = d % 2
    partner = q * 2 + 1 - c
    side = q + 1 - 2 * (q % 2)
    over = lax.rem(q + 2, 4)
    far = lax.rem(side + 2, 4)
    chips = (far, side, over, q)
    rows, cols = weight.shape
    rank = p_new.shape[1]
    blk = rank // n_dev
    sub = blk // n_outer
    fine = sub // pieces
    few = shared_rows(rows)
    many = rows - 2 * few
    kept = few + many
    mate = z + 1 - 2 * (z % 2)
    odd = z % 2
    window = odd * few
    group_of = odd
    turn = z // 2
    few_at = odd * many
    many_at = few - window
    given_at = (1 - odd) * kept
    copies = Copies(send_sem, recv_sem)
    above = (2 * n_outer - 2 - z) // n_outer
    below = (z + n_outer - 1) // n_outer

    def signal_line(sem):
        @pl.when(z > 0)
        def _():
            pl.semaphore_signal(sem, inc=1, device_id=(z - 1, d), device_id_type=MESH)

        @pl.when(z < n_outer - 1)
        def _():
            pl.semaphore_signal(sem, inc=1, device_id=(z + 1, d), device_id_type=MESH)

    def pass_along(steps):
        for r in steps:
            pl.semaphore_wait(line_sem.at[r], above + below)
            if r + 1 < n_outer - 2:
                signal_line(line_sem.at[r + 1])

    barrier = pltpu.get_barrier_semaphore()
    for to in (partner, 2 * side + c, 2 * over + c):
        pl.semaphore_signal(barrier, inc=1, device_id=(z, to), device_id_type=MESH)
    pl.semaphore_signal(barrier, inc=1, device_id=(mate, partner), device_id_type=MESH)
    signal_line(barrier)

    def rows_of(to, start, count):
        return partials.at[pl.ds(pl.multiple_of(to * rows + start, 16), count)]

    own_loads = [
        pltpu.make_async_copy(rows_of(2 * k + c, window, kept), own.at[i], own_sem.at[i])
        for i, k in enumerate(chips)
    ]
    own_loads[0].start()
    pl.semaphore_wait(barrier, 4 + above + below)

    def moment_copy(i, j):
        return pltpu.make_async_remote_copy(
            src_ref=(m_old, v_old)[i],
            dst_ref=moments.at[i, q],
            send_sem=mom_send.at[i, j],
            recv_sem=mom_recv.at[i, j],
            device_id=(z, 2 * (side, over)[j] + c),
            device_id_type=MESH,
        )

    def moment_relay(i):
        came_from = (side, over)[i]
        return pltpu.make_async_remote_copy(
            src_ref=moments.at[i, came_from],
            dst_ref=moments.at[i, came_from],
            send_sem=mom_send.at[i, 2],
            recv_sem=mom_recv.at[i, 2],
            device_id=(z, 2 * (over, side)[i] + c),
            device_id_type=MESH,
        )

    def moment_load(i):
        return pltpu.make_async_copy((m_old, v_old)[i], moments.at[i, q], load_sem.at[2 + i])

    moment_forward = pltpu.make_async_remote_copy(
        src_ref=moments,
        dst_ref=moments,
        send_sem=fwd_send,
        recv_sem=fwd_recv,
        device_id=(z, partner),
        device_id_type=MESH,
    )

    def pair_start(i):
        own_rows = rows_of(2 * chips[i] + 1 - c, window, kept)
        return copies.start(own_rows, pair.at[i], (z, partner))

    def cross_start(i):
        return [
            copies.start(rows_of(2 * chips[i] + c, given_at, few), plane_own.at[i], (mate, d)),
            copies.start(rows_of(2 * chips[i] + 1 - c, given_at, few), plane_pair.at[i], (mate, partner)),
        ]

    pairs = [pair_start(0)]
    crossed = [cross_start(0)]
    for i in (1, 2):
        own_loads[i].start()
        pairs.append(pair_start(i))
    @pl.when(c == group_of)
    def _():
        for j in range(2):
            for i in range(2):
                moment_copy(i, j).start()
        for i in range(2):
            moment_load(i).start()

    arrived = set()

    def arrive(i, group):
        if i not in arrived:
            arrived.add(i)
            pairs[i].wait_recv()
            own_loads[i].wait()
        if group == 0:
            for copy in crossed[i]:
                copy.wait_recv()

    def rows_at(group, h):
        start, count = ((few_at, few // 2), (many_at, many // 2))[group]
        return pl.ds(pl.multiple_of(start + h * count, 16), count)

    def chip_sum(i, h):
        at = rows_at(1, h)
        return own[i, at].astype(F32) + pair[i, at].astype(F32)

    def plane_sum(i, h):
        at, near = rows_at(0, h), slice(h * few // 2, (h + 1) * few // 2)
        total = own[i, at].astype(F32) + pair[i, at].astype(F32)
        return total + (plane_own[i, near].astype(F32) + plane_pair[i, near].astype(F32))

    sums = (plane_sum, chip_sum)
    merging = Copies(merge_send, merge_recv)
    relays, directs, merges = {}, {}, {}

    def send_far(group):
        arrive(0, group)
        for h, chip in enumerate((side, over)):
            at = rows_at(group, h)
            far_sum[at] = sums[group](0, h).astype(BF16)
            relays[group, h] = copies.start(far_sum.at[at], relay_in.at[at], (z, 2 * chip + c))

    def send_direct(group):
        for h, chip in enumerate((side, over)):
            arrive(1 + h, group)
            at = rows_at(group, h)
            direct_out[at] = sums[group](1 + h, h).astype(BF16)
            directs[group, h] = copies.start(direct_out.at[at], direct_in.at[at], (z, 2 * chip + c))

    def send_merged(group):
        for h, (i, chip) in enumerate(((2, over), (1, side))):
            at = rows_at(group, h)
            relays[group, h].wait_recv()
            merged[at] = sums[group](i, h) + relay_in[at].astype(F32)
            merges[group, h] = merging.start(merged.at[at], merged_in.at[at], (z, 2 * chip + c))

    send_far(1)
    crossed += [cross_start(1), cross_start(2)]
    send_direct(1)
    load_new = pltpu.make_async_copy(p_new, basis, load_sem.at[0])
    load_new.start()
    old_loads = [
        pltpu.make_async_copy(
            p_old.at[:, pl.ds(pl.multiple_of((2 * k + group_of) * blk, blk), blk)],
            basis_old.at[:, k * blk : (k + 1) * blk],
            old_sem.at[k],
        )
        for k in range(4)
    ]
    for load in old_loads:
        load.start()
    own_loads[3].start()
    load_weight = pltpu.make_async_copy(weight, weights, load_sem.at[1])
    load_weight.start()
    pairs.append(pair_start(3))
    crossed.append(cross_start(3))
    if n_outer > 2:
        signal_line(line_sem.at[0])

    load_new.wait()
    for load in old_loads:
        load.wait()

    def chip_ranks(k):
        return pl.ds(pl.multiple_of(k * 2 * blk, 2 * blk), 2 * blk)

    for i, k in enumerate(chips):
        part = contract_rows(basis[:, chip_ranks(k)], basis_old[...])
        margin[:, i] = part.reshape(2, n_outer // 2, 2, sub, 4 * blk)
    margin_pair = copies.start(margin.at[1 - c, :, turn], margin_partner, (z, partner))

    send_far(0)
    send_merged(1)
    margin_pair.wait_recv()
    margin_sum[...] = margin[c, :, turn] + margin_partner[...]

    @pl.when(c == group_of)
    def _():
        for i in range(2):
            moment_copy(i, i).wait_recv()
            moment_relay(i).start()

    send_direct(0)
    send_merged(0)
    for copy in merging.started:
        copy.wait_send()
    margin_relays = [
        copies.start(margin_sum.at[0, h], margin_relay.at[h], (z, 2 * chip + c))
        for h, chip in enumerate((side, over))
    ]
    margin_copies = [
        copies.start(margin_sum.at[1 + h, h], margin_in.at[0, h], (z, 2 * chip + c))
        for h, chip in enumerate((side, over))
    ]

    for group in (1, 0):
        arrive(3, group)
        for h in range(2):
            at = rows_at(group, h)
            directs[group, h].wait_recv()
            total = sums[group](3, h) + direct_in[at].astype(F32)
            merges[group, h].wait_recv()
            total = total + merged_in[at]
            high = total.astype(BF16)
            terms[at, :cols] = high
            terms[at, cols:] = (total - high.astype(F32)).astype(BF16)

    for i, k in enumerate(chips):
        kept_rows = pl.ds(pl.multiple_of(window, 16), kept)
        part = contract_rows(basis[kept_rows, chip_ranks(k)], terms[...])
        part = (part[:, :cols] + part[:, cols:]).reshape(2, n_outer, pieces, fine, cols)
        for h in range(pieces):
            projected[h, :, i] = part[:, :, h]
    projected_pairs = [
        copies.start(projected.at[h, 1 - c], projected_partner.at[h], (z, partner)) for h in (1, 0)
    ][::-1]
    for h, (i, chip) in enumerate(((2, over), (1, side))):
        margin_relays[h].wait_recv()
        margin_sum[i, h] = margin_sum[i, h] + margin_relay[h]
        margin_copies.append(copies.start(margin_sum.at[i, h], margin_in.at[1, h], (z, 2 * chip + c)))

    planes = [lax.rem(z + j, n_outer) for j in range(1, n_outer)]
    pass_along(range(n_outer - 2))
    projected_pairs[1].wait_recv()
    projected_sum[1] = projected[1, c] + projected_partner[1]
    column_copies = [
        copies.start(projected_sum.at[1, :, to], column_in.at[j], (to, d)) for j, to in enumerate(planes)
    ]

    projected_pairs[0].wait_recv()
    projected_copies = []
    for i, k in enumerate(chips):
        projected_sum[0, i] = projected[0, c, i] + projected_partner[0, i]
        if i < 3:
            projected_copies.append(
                copies.start(projected_sum.at[0, i], projected_in.at[i], (z, 2 * k + c))
            )
    @pl.when(c == group_of)
    def _():
        for i in range(2):
            moment_load(i).wait()
            moment_copy(i, 1 - i).wait_recv()
            moment_relay(i).wait_recv()
        moment_forward.start()

    @pl.when(c != group_of)
    def _():
        moment_forward.wait_recv()

    for copy in projected_copies:
        copy.wait_recv()
    block[...] = projected_sum[0, 3] + projected_in[0] + projected_in[1] + projected_in[2]
    block_copies = [copies.start(block.at[to], block_in.at[j], (to, d)) for j, to in enumerate(planes)]
    for copy in margin_copies:
        copy.wait_recv()
    margin_rows = margin_sum[3] + margin_in[0] + margin_in[1]
    margin_rows = margin_rows.reshape(2 * sub, 4 * blk)
    old = moments[...].reshape(2, 4 * blk, cols)
    for i, rows_in in enumerate((margin_rows, margin_rows * margin_rows)):
        turned = jnp.dot(rows_in, old[i], precision=lax.Precision.HIGHEST, preferred_element_type=F32)
        rotated[:, i] = turned.reshape(2, sub, cols)
    rot_copy = copies.start(rotated.at[1 - group_of], rotated_in, (mate, d))

    for copy in column_copies:
        copy.wait_recv()
    for i in range(4):
        total = projected_sum[1, i, z]
        for j in range(n_outer - 1):
            total = total + column_in[j, i]
        column[i] = total
    chip_copies = [
        copies.start(column.at[i], chip_in.at[i], (z, 2 * k + c)) for i, k in enumerate(chips[:3])
    ]

    rot_copy.wait_recv()
    first = rotated[group_of, 0] + rotated_in[0]
    second = rotated[group_of, 1] + rotated_in[1]
    for h in range(pieces):
        at = slice(h * fine, (h + 1) * fine)
        if h == 0:
            proj = block[z]
            for j, copy in enumerate(block_copies):
                copy.wait_recv()
                proj = proj + block_in[j]
        else:
            proj = column[3]
            for i, copy in enumerate(chip_copies):
                copy.wait_recv()
                proj = proj + chip_in[i]
        mean = beta_mean * first[at] + (1.0 - beta_mean) * proj
        square = beta_square * second[at] + (1.0 - beta_square) * proj * proj
        moments_new[z, 0, at] = mean
        moments_new[z, 1, at] = square
        direction[d, z, at] = (
            mean / bias_mean / (jnp.sqrt(square / bias_square) + adam_epsilon)
        ).astype(BF16)

    settled = len(copies.started)
    spread = []
    spread = [[], [], [], []]
    for to in [planes[0], planes[2], planes[1], z]:
        for i, k in enumerate(chips):
            if i < 3 or to is not z:
                spread[i].append(copies.start(direction.at[d, z], direction.at[d, z], (to, 2 * k + c)))
    moment_spread = [copies.start(moments_new.at[z], moments_new.at[z], (to, d)) for to in planes]
    for copy in copies.started[:settled]:
        copy.wait_send()

    @pl.when(c == group_of)
    def _():
        for i in range(2):
            for j in range(2):
                moment_copy(i, j).wait_send()
            moment_relay(i).wait_send()
        moment_forward.wait_send()

    forwards = []
    for i in (3, 1, 2, 0):
        for copy in spread[i]:
            copy.wait_recv()
        mine = direction.at[2 * chips[i] + c]
        forwards.append(copies.start(mine, mine, (z, partner)))
    load_weight.wait()
    for copy in sum(spread, moment_spread):
        copy.wait_send()
    for copy in forwards:
        copy.wait_recv()
    directions = direction[...].reshape(rank, cols)
    tall = min(rows, 256)
    for s in range(0, rows, tall):
        update = jnp.dot(basis[s : s + tall, :], directions, preferred_element_type=F32)
        new_weight[s : s + tall, :] = weights[s : s + tall, :] - step_scale * update
    for copy in moment_spread:
        copy.wait_recv()
    m_new[...] = moments_new[:, 0].reshape(blk, cols)
    v_new[...] = moments_new[:, 1].reshape(blk, cols)

    for copy in forwards:
        copy.wait_send()


def shared_rows(rows):
    top, bottom = shared_part
    return rows * top // bottom // 32 * 32


def square_scratch(n_outer, n_dev, rows, cols, rank):
    blk = rank // n_dev
    sub = blk // n_outer
    fine = sub // pieces
    span = 4 * blk
    dma = pltpu.SemaphoreType.DMA
    few = shared_rows(rows)
    kept = rows - few
    count = 50 + 15 * pieces + 6 * n_outer
    return [
        pltpu.VMEM((4, kept, cols), BF16),
        pltpu.VMEM((4, kept, cols), BF16),
        pltpu.VMEM((4, few, cols), BF16),
        pltpu.VMEM((4, few, cols), BF16),
        pltpu.VMEM((kept, cols), BF16),
        pltpu.VMEM((kept, cols), BF16),
        pltpu.VMEM((kept, cols), BF16),
        pltpu.VMEM((kept, cols), BF16),
        pltpu.VMEM((kept, cols), F32),
        pltpu.VMEM((kept, cols), F32),
        pltpu.VMEM((kept, 2 * cols), BF16),
        pltpu.VMEM((rows, rank), BF16),
        pltpu.VMEM((rows, span), BF16),
        pltpu.VMEM((rows, cols), F32),
        pltpu.VMEM((2, 4, blk, cols), F32),
        pltpu.VMEM((2, 4, n_outer // 2, 2, sub, span), F32),
        pltpu.VMEM((4, 2, sub, span), F32),
        pltpu.VMEM((4, 2, sub, span), F32),
        pltpu.VMEM((2, 2, sub, span), F32),
        pltpu.VMEM((2, sub, span), F32),
        pltpu.VMEM((2, 2, sub, cols), F32),
        pltpu.VMEM((2, sub, cols), F32),
        pltpu.VMEM((pieces, 2, 4, n_outer, fine, cols), F32),
        pltpu.VMEM((pieces, 4, n_outer, fine, cols), F32),
        pltpu.VMEM((pieces, 4, n_outer, fine, cols), F32),
        pltpu.VMEM((3, n_outer, fine, cols), F32),
        pltpu.VMEM((n_outer, fine, cols), F32),
        pltpu.VMEM((n_outer - 1, fine, cols), F32),
        pltpu.VMEM((4, fine, cols), F32),
        pltpu.VMEM((n_outer - 1, 4, fine, cols), F32),
        pltpu.VMEM((3, fine, cols), F32),
        pltpu.VMEM((n_dev, n_outer, sub, cols), BF16),
        pltpu.VMEM((n_outer, 2, sub, cols), F32),
        dma((4,)),
        dma((4,)),
        dma((4,)),
        dma((2, 3)),
        dma((2, 3)),
        dma,
        dma,
        dma((count,)),
        dma((count,)),
        dma((4,)),
        dma((4,)),
        pltpu.SemaphoreType.REGULAR((max(n_outer - 2, 1),)),
    ]


def plain_scratch(n_outer, n_dev, rows, cols, rank):
    blk = rank // n_dev
    per = n_dev // n_outer
    span = per * blk
    n_chip = n_dev // 2
    dma = pltpu.SemaphoreType.DMA
    return (
        [
            pltpu.VMEM((n_dev, rows, cols), BF16),
            pltpu.VMEM((rows, rank), BF16),
            pltpu.VMEM((rows, span), BF16),
            pltpu.VMEM((rows, cols), F32),
            pltpu.VMEM((2, per, blk, cols), F32),
            pltpu.VMEM((n_dev, blk, span), F32),
            pltpu.VMEM((n_chip, blk, span), F32),
            pltpu.VMEM((n_chip, blk, span), F32),
            pltpu.VMEM((n_chip, blk, span), F32),
            pltpu.VMEM((2, blk, cols), F32),
            pltpu.VMEM((n_outer, 2, blk, cols), F32),
            pltpu.VMEM((n_dev, blk, cols), F32),
            pltpu.VMEM((n_chip, blk, cols), F32),
            pltpu.VMEM((n_chip, blk, cols), F32),
            pltpu.VMEM((n_chip, blk, cols), F32),
            pltpu.VMEM((blk, cols), F32),
            pltpu.VMEM((n_outer, blk, cols), F32),
            pltpu.VMEM((n_dev, blk, cols), BF16),
            dma((6,)),
            dma((per,)),
            dma((chunks, n_dev)),
            dma((chunks, n_dev)),
            dma((2, per, n_chip)),
            dma((2, per)),
            dma((2, per)),
            dma((2, per)),
        ]
        + [dma((n_chip,))] * 4
        + [dma((n_outer,))] * 2
        + [dma((parts, n_chip))] * 4
        + [dma((parts, n_outer))] * 2
        + [dma((parts, n_dev))] * 2
    )


def hand_over(weight_in, m_in, v_in, weight_out, m_out, v_out):
    weight_out[...] = weight_in[...]
    m_out[...] = m_in[...]
    v_out[...] = v_in[...]


def on_device(n_outer, n_dev, partials, p_old, p_new, weight, m_old, v_old):
    rows, cols = weight.shape
    rank = p_new.shape[1]
    blk = rank // n_dev
    per = n_dev // n_outer
    span = per * blk
    n_chip = n_dev // 2
    squared = n_chip == 4 and n_dev % n_outer == 0 and n_outer % 2 == 0 and rows % 64 == 0 and blk % 128 == 0 and pieces == 2 and blk % (16 * pieces * n_outer) == 0
    if blk % 128 and not squared:
        z = lax.axis_index("outer")
        p_old = jnp.concatenate(
            [
                lax.dynamic_slice_in_dim(p_old, (k * n_outer + z) * blk, blk, axis=1)
                for k in range(per)
            ],
            axis=1,
        )
    anywhere = pl.BlockSpec(memory_space=pltpu.HBM)
    vmem = pl.BlockSpec(memory_space=pltpu.VMEM)
    if squared:
        body, scratch = square_kernel, square_scratch(n_outer, n_dev, rows, cols, rank)
    else:
        body, scratch = kernel, plain_scratch(n_outer, n_dev, rows, cols, rank)
    operands = (partials[0], p_old, p_new, weight, m_old, v_old)
    results = pl.pallas_call(
        functools.partial(body, n_outer, n_dev),
        out_shape=(
            jax.ShapeDtypeStruct((rows, cols), F32),
            jax.ShapeDtypeStruct((blk, cols), F32),
            jax.ShapeDtypeStruct((blk, cols), F32),
        ),
        in_specs=[anywhere] * 6,
        out_specs=(vmem, vmem, vmem),
        scratch_shapes=scratch,
        compiler_params=pltpu.CompilerParams(
            collective_id=0, has_side_effects=True, vmem_limit_bytes=vmem_limit
        ),
    )(*[pltpu.with_memory_space_constraint(a, pltpu.HBM) for a in operands])
    return pl.pallas_call(
        hand_over,
        out_shape=tuple(jax.ShapeDtypeStruct(r.shape, r.dtype) for r in results),
        in_specs=[vmem] * 3,
        out_specs=(vmem,) * 3,
        compiler_params=pltpu.CompilerParams(vmem_limit_bytes=finish_limit),
    )(*results)


def solution(mesh):
    in_specs = (
        P(("outer", "dev"), None, None),
        P("dev", None),
        P("dev", None),
        P("dev", None),
        P("dev", None),
        P("dev", None),
    )
    out_specs = (P("dev", None), P("dev", None), P("dev", None))
    return jax.shard_map(
        functools.partial(on_device, mesh.shape["outer"], mesh.shape["dev"]),
        mesh=mesh,
        in_specs=in_specs,
        out_specs=out_specs,
        check_vma=False,
    )
```

```python
import functools

import jax
import jax.numpy as jnp
from jax import lax
from jax.experimental import pallas as pl
from jax.experimental.pallas import tpu as pltpu
from jax.sharding import PartitionSpec as P

beta_mean = 0.9
beta_square = 0.95
bias_mean = 0.9999734386011124
bias_square = 0.9940794707796659
adam_epsilon = 1e-08
step_scale = 0.5

chunks = 2
early = 1
parts = 2
pieces = 2
shared_part = (7, 32)
vmem_limit = 50331648
finish_limit = 4194304

MESH = pl.DeviceIdType.MESH
F32 = jnp.float32
BF16 = jnp.bfloat16


def contract_rows(a, b):
    return lax.dot_general(a, b, (((0,), (0,)), ((), ())), preferred_element_type=F32)


def kernel(
    n_outer,
    n_dev,
    partials,
    p_old,
    p_new,
    weight,
    m_old,
    v_old,
    new_weight,
    m_new,
    v_new,
    grads,
    basis,
    basis_old,
    weights,
    moments,
    margin,
    margin_partner,
    margin_sum,
    margin_in,
    rotated,
    rotated_in,
    projected,
    projected_partner,
    projected_sum,
    projected_in,
    block,
    block_in,
    direction,
    load_sem,
    old_sem,
    grad_send,
    grad_recv,
    mom_send,
    mom_recv,
    fwd_send,
    fwd_recv,
    mp_send,
    mp_recv,
    ms_send,
    ms_recv,
    rot_send,
    rot_recv,
    pp_send,
    pp_recv,
    ps_send,
    ps_recv,
    blk_send,
    blk_recv,
    dir_send,
    dir_recv,
):
    z = lax.axis_index("outer")
    d = lax.axis_index("dev")
    n_chip = n_dev // 2
    q = d // 2
    c = d % 2
    partner = q * 2 + 1 - c
    rows, cols = weight.shape
    rank = p_new.shape[1]
    blk = rank // n_dev
    per = n_dev // n_outer

    def remote(src, dst, send, recv, where):
        return pltpu.make_async_remote_copy(
            src_ref=src, dst_ref=dst, send_sem=send, recv_sem=recv, device_id=where, device_id_type=MESH
        )

    barrier = pltpu.get_barrier_semaphore()
    for j in range(1, n_dev):
        pl.semaphore_signal(barrier, inc=1, device_id=(z, lax.rem(d + j, n_dev)), device_id_type=MESH)
    for j in range(1, n_outer):
        pl.semaphore_signal(barrier, inc=1, device_id=(lax.rem(z + j, n_outer), d), device_id_type=MESH)

    load_new = pltpu.make_async_copy(p_new, basis, load_sem.at[0])
    load_new.start()
    if p_old.shape[1] == per * blk:
        old_loads = [pltpu.make_async_copy(p_old, basis_old, old_sem.at[0])]
    else:
        old_loads = [
            pltpu.make_async_copy(
                p_old.at[:, pl.ds(pl.multiple_of((k * n_outer + z) * blk, blk), blk)],
                basis_old.at[:, k * blk : (k + 1) * blk],
                old_sem.at[k],
            )
            for k in range(per)
        ]
    for load in old_loads:
        load.start()
    load_weight = pltpu.make_async_copy(weight, weights, load_sem.at[2])
    load_weight.start()
    load_own = pltpu.make_async_copy(
        partials.at[pl.ds(pl.multiple_of(d * rows, rows), rows)], grads.at[0], load_sem.at[3]
    )
    load_own.start()

    pl.semaphore_wait(barrier, n_dev - 1 + n_outer - 1)

    def moment_copies(k, owner):
        copies = []
        for j in range(1, n_chip):
            to = (z, lax.rem(q + j, n_chip) * 2 + c)
            for i, src in enumerate((m_old, v_old)):
                copies.append(remote(src, moments.at[i, k], mom_send.at[i, k, j], mom_recv.at[i, k], to))
        return copies

    for k in range(per):
        owner = k * n_outer + z

        @pl.when(d == owner)
        def _():
            for copy in moment_copies(k, owner):
                copy.start()
            for i, src in enumerate((m_old, v_old)):
                pltpu.make_async_copy(src, moments.at[i, k], load_sem.at[4 + i]).start()

    tall = rows // chunks

    def send_gradients(chunk):
        copies = []
        for j in range(1, n_dev):
            to = lax.rem(d + j, n_dev)
            copy = remote(
                partials.at[pl.ds(pl.multiple_of(to * rows + chunk * tall, tall), tall)],
                grads.at[j, chunk * tall : (chunk + 1) * tall],
                grad_send.at[chunk, j],
                grad_recv.at[chunk, j],
                (z, to),
            )
            copy.start()
            copies.append(copy)
        return copies

    grad_copies = [send_gradients(chunk) for chunk in range(early)]

    load_new.wait()
    for load in old_loads:
        load.wait()
    width = min(rank, 256)
    for s in range(0, rank, width):
        part = contract_rows(basis[:, s : s + width], basis_old[...])
        margin[s // blk : (s + width) // blk] = part.reshape(width // blk, blk, part.shape[1])

    def scatter_start(val, prt, send, recv):
        copies = []
        for j in list(range(1, n_chip)) + [0]:
            k = lax.rem(q + j, n_chip)
            copy = remote(val.at[2 * k + 1 - c], prt.at[j], send.at[j], recv.at[j], (z, partner))
            copy.start()
            copies.append((j, k, copy))
        return copies

    def scatter_middle(pairs, val, prt, tot, arr, send, recv):
        copies = []
        for j, k, pair in pairs:
            pair.wait_recv()
            tot[j] = val[2 * k + c] + prt[j]
            if j:
                copy = remote(tot.at[j], arr.at[j], send.at[j], recv.at[j], (z, 2 * k + c))
                copy.start()
                copies.append((j, copy))
        return copies

    def scatter_end(copies, tot, arr):
        total = tot[0]
        for j, copy in copies:
            copy.wait_recv()
            total = total + arr[j]
        return total

    margin_pairs = scatter_start(margin, margin_partner, mp_send, mp_recv)

    for k in range(per):
        owner = k * n_outer + z
        mine = c == owner % 2

        @pl.when(d == owner)
        def _():
            for i, src in enumerate((m_old, v_old)):
                pltpu.make_async_copy(src, moments.at[i, k], load_sem.at[4 + i]).wait()

        @pl.when(jnp.logical_and(mine, d != owner))
        def _():
            for i, src in enumerate((m_old, v_old)):
                remote(src, moments.at[i, k], mom_send.at[i, k, 0], mom_recv.at[i, k], (z, d)).wait_recv()

        @pl.when(mine)
        def _():
            for i in range(2):
                remote(
                    moments.at[i, k], moments.at[i, k], fwd_send.at[i, k], fwd_recv.at[i, k], (z, partner)
                ).start()

    margin_copies = scatter_middle(
        margin_pairs, margin, margin_partner, margin_sum, margin_in, ms_send, ms_recv
    )

    for chunk in range(early, chunks):
        grad_copies.append(send_gradients(chunk))

    for k in range(per):
        mine = c == (k * n_outer + z) % 2

        @pl.when(jnp.logical_not(mine))
        def _():
            for i in range(2):
                remote(
                    moments.at[i, k], moments.at[i, k], fwd_send.at[i, k], fwd_recv.at[i, k], (z, partner)
                ).wait_recv()

    margin_rows = scatter_end(margin_copies, margin_sum, margin_in)
    old = moments[...].reshape(2, per * blk, cols)
    rotated[0] = jnp.dot(margin_rows, old[0], precision=lax.Precision.HIGHEST, preferred_element_type=F32)
    rotated[1] = jnp.dot(
        margin_rows * margin_rows, old[1], precision=lax.Precision.HIGHEST, preferred_element_type=F32
    )
    rot_copies = []
    for j in range(1, n_outer):
        copy = remote(
            rotated, rotated_in.at[j], rot_send.at[j], rot_recv.at[j], (lax.rem(z + j, n_outer), d)
        )
        copy.start()
        rot_copies.append(copy)

    load_own.wait()
    for chunk in range(chunks):
        for copy in grad_copies[chunk]:
            copy.wait_recv()
        part_rows = slice(chunk * tall, (chunk + 1) * tall)
        total = grads[0, part_rows].astype(F32)
        for j in range(1, n_dev):
            total = total + grads[j, part_rows].astype(F32)
        high = total.astype(BF16)
        low = (total - high.astype(F32)).astype(BF16)
        both = jnp.concatenate([high, low], axis=1)
        for s in range(0, rank, width):
            part = contract_rows(basis[part_rows, s : s + width], both)
            part = (part[:, :cols] + part[:, cols:]).reshape(width // blk, blk, cols)
            blocks = slice(s // blk, (s + width) // blk)
            projected[blocks] = part if chunk == 0 else projected[blocks] + part
    half = blk // parts
    views = [slice(h * half, (h + 1) * half) for h in range(parts)]
    pairs = [
        scatter_start(projected.at[:, v], projected_partner.at[:, v], pp_send.at[h], pp_recv.at[h])
        for h, v in enumerate(views)
    ]
    copies = [
        scatter_middle(
            pairs[h],
            projected.at[:, v],
            projected_partner.at[:, v],
            projected_sum.at[:, v],
            projected_in.at[:, v],
            ps_send.at[h],
            ps_recv.at[h],
        )
        for h, v in enumerate(views)
    ]
    blk_copies = []
    for h, v in enumerate(views):
        block[v] = scatter_end(copies[h], projected_sum.at[:, v], projected_in.at[:, v])
        for j in range(1, n_outer):
            copy = remote(
                block.at[v],
                block_in.at[j, v],
                blk_send.at[h, j],
                blk_recv.at[h, j],
                (lax.rem(z + j, n_outer), d),
            )
            copy.start()
            blk_copies.append(copy)
    for copy in rot_copies:
        copy.wait_recv()
    dir_copies = []
    for h, v in enumerate(views):
        for copy in blk_copies[h * (n_outer - 1) : (h + 1) * (n_outer - 1)]:
            copy.wait_recv()
        first = rotated[0, v]
        second = rotated[1, v]
        proj = block[v]
        for j in range(1, n_outer):
            first = first + rotated_in[j, 0, v]
            second = second + rotated_in[j, 1, v]
            proj = proj + block_in[j, v]
        mean = beta_mean * first + (1.0 - beta_mean) * proj
        square = beta_square * second + (1.0 - beta_square) * proj * proj
        m_new[v] = mean
        v_new[v] = square
        direction[d, v] = (mean / bias_mean / (jnp.sqrt(square / bias_square) + adam_epsilon)).astype(BF16)
        for j in range(1, n_dev):
            copy = remote(
                direction.at[d, v],
                direction.at[d, v],
                dir_send.at[h, j],
                dir_recv.at[h, j],
                (z, lax.rem(d + j, n_dev)),
            )
            copy.start()
            dir_copies.append(copy)
    load_weight.wait()
    for copy in dir_copies:
        copy.wait_recv()
    directions = direction[...].reshape(rank, cols)
    tall = min(rows, 256)
    for s in range(0, rows, tall):
        update = jnp.dot(basis[s : s + tall, :], directions, preferred_element_type=F32)
        new_weight[s : s + tall, :] = weights[s : s + tall, :] - step_scale * update

    for k in range(per):
        owner = k * n_outer + z
        mine = c == owner % 2

        @pl.when(d == owner)
        def _():
            for copy in moment_copies(k, owner):
                copy.wait_send()

        @pl.when(mine)
        def _():
            for i in range(2):
                remote(
                    moments.at[i, k], moments.at[i, k], fwd_send.at[i, k], fwd_recv.at[i, k], (z, partner)
                ).wait_send()

    for copy in sum(grad_copies, []) + rot_copies + blk_copies + dir_copies:
        copy.wait_send()
    for group in [margin_pairs] + pairs:
        for _, _, copy in group:
            copy.wait_send()
    for group in [margin_copies] + copies:
        for _, copy in group:
            copy.wait_send()

class Copies:
    def __init__(self, send, recv):
        self.send, self.recv, self.started = send, recv, []

    def start(self, src, dst, to):
        i = len(self.started)
        copy = pltpu.make_async_remote_copy(
            src_ref=src,
            dst_ref=dst,
            send_sem=self.send.at[i],
            recv_sem=self.recv.at[i],
            device_id=to,
            device_id_type=MESH,
        )
        copy.start()
        self.started.append(copy)
        return copy


def square_kernel(
    n_outer,
    n_dev,
    partials,
    p_old,
    p_new,
    weight,
    m_old,
    v_old,
    new_weight,
    m_new,
    v_new,
    own,
    pair,
    plane_own,
    plane_pair,
    far_sum,
    relay_in,
    direct_out,
    direct_in,
    merged,
    merged_in,
    terms,
    basis,
    basis_old,
    weights,
    moments,
    margin,
    margin_partner,
    margin_sum,
    margin_in,
    margin_relay,
    rotated,
    rotated_in,
    projected,
    projected_partner,
    projected_sum,
    projected_in,
    block,
    block_in,
    column,
    column_in,
    chip_in,
    direction,
    moments_new,
    load_sem,
    old_sem,
    own_sem,
    mom_send,
    mom_recv,
    fwd_send,
    fwd_recv,
    send_sem,
    recv_sem,
    merge_send,
    merge_recv,
    line_sem,
):
    z = lax.axis_index("outer")
    d = lax.axis_index("dev")
    q = d // 2
    c = d % 2
    partner = q * 2 + 1 - c
    side = q + 1 - 2 * (q % 2)
    over = lax.rem(q + 2, 4)
    far = lax.rem(side + 2, 4)
    chips = (far, side, over, q)
    rows, cols = weight.shape
    rank = p_new.shape[1]
    blk = rank // n_dev
    sub = blk // n_outer
    fine = sub // pieces
    few = shared_rows(rows)
    many = rows - 2 * few
    kept = few + many
    mate = z + 1 - 2 * (z % 2)
    odd = z % 2
    window = odd * few
    group_of = odd
    turn = z // 2
    few_at = odd * many
    many_at = few - window
    given_at = (1 - odd) * kept
    copies = Copies(send_sem, recv_sem)
    above = (2 * n_outer - 2 - z) // n_outer
    below = (z + n_outer - 1) // n_outer

    def signal_line(sem):
        @pl.when(z > 0)
        def _():
            pl.semaphore_signal(sem, inc=1, device_id=(z - 1, d), device_id_type=MESH)

        @pl.when(z < n_outer - 1)
        def _():
            pl.semaphore_signal(sem, inc=1, device_id=(z + 1, d), device_id_type=MESH)

    def pass_along(steps):
        for r in steps:
            pl.semaphore_wait(line_sem.at[r], above + below)
            if r + 1 < n_outer - 2:
                signal_line(line_sem.at[r + 1])

    barrier = pltpu.get_barrier_semaphore()
    for to in (partner, 2 * side + c, 2 * over + c):
        pl.semaphore_signal(barrier, inc=1, device_id=(z, to), device_id_type=MESH)
    pl.semaphore_signal(barrier, inc=1, device_id=(mate, partner), device_id_type=MESH)
    signal_line(barrier)

    def rows_of(to, start, count):
        return partials.at[pl.ds(pl.multiple_of(to * rows + start, 16), count)]

    own_loads = [
        pltpu.make_async_copy(rows_of(2 * k + c, window, kept), own.at[i], own_sem.at[i])
        for i, k in enumerate(chips)
    ]
    own_loads[0].start()
    pl.semaphore_wait(barrier, 4 + above + below)

    def moment_copy(i, j):
        return pltpu.make_async_remote_copy(
            src_ref=(m_old, v_old)[i],
            dst_ref=moments.at[i, q],
            send_sem=mom_send.at[i, j],
            recv_sem=mom_recv.at[i, j],
            device_id=(z, 2 * (side, over)[j] + c),
            device_id_type=MESH,
        )

    def moment_relay(i):
        came_from = (side, over)[i]
        return pltpu.make_async_remote_copy(
            src_ref=moments.at[i, came_from],
            dst_ref=moments.at[i, came_from],
            send_sem=mom_send.at[i, 2],
            recv_sem=mom_recv.at[i, 2],
            device_id=(z, 2 * (over, side)[i] + c),
            device_id_type=MESH,
        )

    def moment_load(i):
        return pltpu.make_async_copy((m_old, v_old)[i], moments.at[i, q], load_sem.at[2 + i])

    moment_forward = pltpu.make_async_remote_copy(
        src_ref=moments,
        dst_ref=moments,
        send_sem=fwd_send,
        recv_sem=fwd_recv,
        device_id=(z, partner),
        device_id_type=MESH,
    )

    def pair_start(i):
        own_rows = rows_of(2 * chips[i] + 1 - c, window, kept)
        return copies.start(own_rows, pair.at[i], (z, partner))

    def cross_start(i):
        return [
            copies.start(rows_of(2 * chips[i] + c, given_at, few), plane_own.at[i], (mate, d)),
            copies.start(rows_of(2 * chips[i] + 1 - c, given_at, few), plane_pair.at[i], (mate, partner)),
        ]

    pairs = [pair_start(0)]
    crossed = [cross_start(0)]
    for i in (1, 2):
        own_loads[i].start()
        pairs.append(pair_start(i))
    @pl.when(c == group_of)
    def _():
        for j in range(2):
            for i in range(2):
                moment_copy(i, j).start()
        for i in range(2):
            moment_load(i).start()

    arrived = set()

    def arrive(i, group):
        if i not in arrived:
            arrived.add(i)
            pairs[i].wait_recv()
            own_loads[i].wait()
        if group == 0:
            for copy in crossed[i]:
                copy.wait_recv()

    def rows_at(group, h):
        start, count = ((few_at, few // 2), (many_at, many // 2))[group]
        return pl.ds(pl.multiple_of(start + h * count, 16), count)

    def chip_sum(i, h):
        at = rows_at(1, h)
        return own[i, at].astype(F32) + pair[i, at].astype(F32)

    def plane_sum(i, h):
        at, near = rows_at(0, h), slice(h * few // 2, (h + 1) * few // 2)
        total = own[i, at].astype(F32) + pair[i, at].astype(F32)
        return total + (plane_own[i, near].astype(F32) + plane_pair[i, near].astype(F32))

    sums = (plane_sum, chip_sum)
    merging = Copies(merge_send, merge_recv)
    relays, directs, merges = {}, {}, {}

    def send_far(group):
        arrive(0, group)
        for h, chip in enumerate((side, over)):
            at = rows_at(group, h)
            far_sum[at] = sums[group](0, h).astype(BF16)
            relays[group, h] = copies.start(far_sum.at[at], relay_in.at[at], (z, 2 * chip + c))

    def send_direct(group):
        for h, chip in enumerate((side, over)):
            arrive(1 + h, group)
            at = rows_at(group, h)
            direct_out[at] = sums[group](1 + h, h).astype(BF16)
            directs[group, h] = copies.start(direct_out.at[at], direct_in.at[at], (z, 2 * chip + c))

    def send_merged(group):
        for h, (i, chip) in enumerate(((2, over), (1, side))):
            at = rows_at(group, h)
            relays[group, h].wait_recv()
            merged[at] = sums[group](i, h) + relay_in[at].astype(F32)
            merges[group, h] = merging.start(merged.at[at], merged_in.at[at], (z, 2 * chip + c))

    send_far(1)
    crossed += [cross_start(1), cross_start(2)]
    send_direct(1)
    load_new = pltpu.make_async_copy(p_new, basis, load_sem.at[0])
    load_new.start()
    old_loads = [
        pltpu.make_async_copy(
            p_old.at[:, pl.ds(pl.multiple_of((2 * k + group_of) * blk, blk), blk)],
            basis_old.at[:, k * blk : (k + 1) * blk],
            old_sem.at[k],
        )
        for k in range(4)
    ]
    for load in old_loads:
        load.start()
    own_loads[3].start()
    load_weight = pltpu.make_async_copy(weight, weights, load_sem.at[1])
    load_weight.start()
    pairs.append(pair_start(3))
    crossed.append(cross_start(3))
    if n_outer > 2:
        signal_line(line_sem.at[0])

    send_far(0)
    send_merged(1)
    load_new.wait()
    for load in old_loads:
        load.wait()

    def chip_ranks(k):
        return pl.ds(pl.multiple_of(k * 2 * blk, 2 * blk), 2 * blk)

    for i, k in enumerate(chips):
        part = contract_rows(basis[:, chip_ranks(k)], basis_old[...])
        margin[:, i] = part.reshape(2, n_outer // 2, 2, sub, 4 * blk)
    margin_pair = copies.start(margin.at[1 - c, :, turn], margin_partner, (z, partner))

    margin_pair.wait_recv()
    margin_sum[...] = margin[c, :, turn] + margin_partner[...]

    @pl.when(c == group_of)
    def _():
        for i in range(2):
            moment_copy(i, i).wait_recv()
            moment_relay(i).start()

    send_direct(0)
    send_merged(0)
    for copy in merging.started:
        copy.wait_send()
    margin_relays = [
        copies.start(margin_sum.at[0, h], margin_relay.at[h], (z, 2 * chip + c))
        for h, chip in enumerate((side, over))
    ]
    margin_copies = [
        copies.start(margin_sum.at[1 + h, h], margin_in.at[0, h], (z, 2 * chip + c))
        for h, chip in enumerate((side, over))
    ]

    for group in (1, 0):
        arrive(3, group)
        for h in range(2):
            at = rows_at(group, h)
            directs[group, h].wait_recv()
            total = sums[group](3, h) + direct_in[at].astype(F32)
            merges[group, h].wait_recv()
            total = total + merged_in[at]
            high = total.astype(BF16)
            terms[at, :cols] = high
            terms[at, cols:] = (total - high.astype(F32)).astype(BF16)

    for i, k in enumerate(chips):
        kept_rows = pl.ds(pl.multiple_of(window, 16), kept)
        part = contract_rows(basis[kept_rows, chip_ranks(k)], terms[...])
        part = (part[:, :cols] + part[:, cols:]).reshape(2, n_outer, pieces, fine, cols)
        for h in range(pieces):
            projected[h, :, i] = part[:, :, h]
    projected_pairs = [
        copies.start(projected.at[h, 1 - c], projected_partner.at[h], (z, partner)) for h in (1, 0)
    ][::-1]
    for h, (i, chip) in enumerate(((2, over), (1, side))):
        margin_relays[h].wait_recv()
        margin_sum[i, h] = margin_sum[i, h] + margin_relay[h]
        margin_copies.append(copies.start(margin_sum.at[i, h], margin_in.at[1, h], (z, 2 * chip + c)))

    planes = [lax.rem(z + j, n_outer) for j in range(1, n_outer)]
    pass_along(range(n_outer - 2))
    projected_pairs[1].wait_recv()
    projected_sum[1] = projected[1, c] + projected_partner[1]
    column_copies = [
        copies.start(projected_sum.at[1, :, to], column_in.at[j], (to, d)) for j, to in enumerate(planes)
    ]

    projected_pairs[0].wait_recv()
    projected_copies = []
    for i, k in enumerate(chips):
        projected_sum[0, i] = projected[0, c, i] + projected_partner[0, i]
        if i < 3:
            projected_copies.append(
                copies.start(projected_sum.at[0, i], projected_in.at[i], (z, 2 * k + c))
            )
    @pl.when(c == group_of)
    def _():
        for i in range(2):
            moment_load(i).wait()
            moment_copy(i, 1 - i).wait_recv()
            moment_relay(i).wait_recv()
        moment_forward.start()

    @pl.when(c != group_of)
    def _():
        moment_forward.wait_recv()

    for copy in projected_copies:
        copy.wait_recv()
    block[...] = projected_sum[0, 3] + projected_in[0] + projected_in[1] + projected_in[2]
    block_copies = [copies.start(block.at[to], block_in.at[j], (to, d)) for j, to in enumerate(planes)]
    for copy in margin_copies:
        copy.wait_recv()
    margin_rows = margin_sum[3] + margin_in[0] + margin_in[1]
    margin_rows = margin_rows.reshape(2 * sub, 4 * blk)
    old = moments[...].reshape(2, 4 * blk, cols)
    for i, rows_in in enumerate((margin_rows, margin_rows * margin_rows)):
        turned = jnp.dot(rows_in, old[i], precision=lax.Precision.HIGHEST, preferred_element_type=F32)
        rotated[:, i] = turned.reshape(2, sub, cols)
    rot_copy = copies.start(rotated.at[1 - group_of], rotated_in, (mate, d))

    for copy in column_copies:
        copy.wait_recv()
    for i in range(4):
        total = projected_sum[1, i, z]
        for j in range(n_outer - 1):
            total = total + column_in[j, i]
        column[i] = total
    chip_copies = [
        copies.start(column.at[i], chip_in.at[i], (z, 2 * k + c)) for i, k in enumerate(chips[:3])
    ]

    rot_copy.wait_recv()
    first = rotated[group_of, 0] + rotated_in[0]
    second = rotated[group_of, 1] + rotated_in[1]
    for h in range(pieces):
        at = slice(h * fine, (h + 1) * fine)
        if h == 0:
            proj = block[z]
            for j, copy in enumerate(block_copies):
                copy.wait_recv()
                proj = proj + block_in[j]
        else:
            proj = column[3]
            for i, copy in enumerate(chip_copies):
                copy.wait_recv()
                proj = proj + chip_in[i]
        mean = beta_mean * first[at] + (1.0 - beta_mean) * proj
        square = beta_square * second[at] + (1.0 - beta_square) * proj * proj
        moments_new[z, 0, at] = mean
        moments_new[z, 1, at] = square
        direction[d, z, at] = (
            mean / bias_mean / (jnp.sqrt(square / bias_square) + adam_epsilon)
        ).astype(BF16)

    settled = len(copies.started)
    spread = []
    spread = [[], [], [], []]
    for to in [planes[0], planes[2], planes[1], z]:
        for i, k in enumerate(chips):
            if i < 3 or to is not z:
                spread[i].append(copies.start(direction.at[d, z], direction.at[d, z], (to, 2 * k + c)))
    moment_spread = [copies.start(moments_new.at[z], moments_new.at[z], (to, d)) for to in planes]
    for copy in copies.started[:settled]:
        copy.wait_send()

    @pl.when(c == group_of)
    def _():
        for i in range(2):
            for j in range(2):
                moment_copy(i, j).wait_send()
            moment_relay(i).wait_send()
        moment_forward.wait_send()

    forwards = []
    for i in (3, 1, 2, 0):
        for copy in spread[i]:
            copy.wait_recv()
        mine = direction.at[2 * chips[i] + c]
        forwards.append(copies.start(mine, mine, (z, partner)))
    load_weight.wait()
    for copy in sum(spread, moment_spread):
        copy.wait_send()
    for copy in forwards:
        copy.wait_recv()
    directions = direction[...].reshape(rank, cols)
    tall = min(rows, 256)
    for s in range(0, rows, tall):
        update = jnp.dot(basis[s : s + tall, :], directions, preferred_element_type=F32)
        new_weight[s : s + tall, :] = weights[s : s + tall, :] - step_scale * update
    for copy in moment_spread:
        copy.wait_recv()
    m_new[...] = moments_new[:, 0].reshape(blk, cols)
    v_new[...] = moments_new[:, 1].reshape(blk, cols)

    for copy in forwards:
        copy.wait_send()


def shared_rows(rows):
    top, bottom = shared_part
    return rows * top // bottom // 32 * 32


def square_scratch(n_outer, n_dev, rows, cols, rank):
    blk = rank // n_dev
    sub = blk // n_outer
    fine = sub // pieces
    span = 4 * blk
    dma = pltpu.SemaphoreType.DMA
    few = shared_rows(rows)
    kept = rows - few
    count = 50 + 15 * pieces + 6 * n_outer
    return [
        pltpu.VMEM((4, kept, cols), BF16),
        pltpu.VMEM((4, kept, cols), BF16),
        pltpu.VMEM((4, few, cols), BF16),
        pltpu.VMEM((4, few, cols), BF16),
        pltpu.VMEM((kept, cols), BF16),
        pltpu.VMEM((kept, cols), BF16),
        pltpu.VMEM((kept, cols), BF16),
        pltpu.VMEM((kept, cols), BF16),
        pltpu.VMEM((kept, cols), F32),
        pltpu.VMEM((kept, cols), F32),
        pltpu.VMEM((kept, 2 * cols), BF16),
        pltpu.VMEM((rows, rank), BF16),
        pltpu.VMEM((rows, span), BF16),
        pltpu.VMEM((rows, cols), F32),
        pltpu.VMEM((2, 4, blk, cols), F32),
        pltpu.VMEM((2, 4, n_outer // 2, 2, sub, span), F32),
        pltpu.VMEM((4, 2, sub, span), F32),
        pltpu.VMEM((4, 2, sub, span), F32),
        pltpu.VMEM((2, 2, sub, span), F32),
        pltpu.VMEM((2, sub, span), F32),
        pltpu.VMEM((2, 2, sub, cols), F32),
        pltpu.VMEM((2, sub, cols), F32),
        pltpu.VMEM((pieces, 2, 4, n_outer, fine, cols), F32),
        pltpu.VMEM((pieces, 4, n_outer, fine, cols), F32),
        pltpu.VMEM((pieces, 4, n_outer, fine, cols), F32),
        pltpu.VMEM((3, n_outer, fine, cols), F32),
        pltpu.VMEM((n_outer, fine, cols), F32),
        pltpu.VMEM((n_outer - 1, fine, cols), F32),
        pltpu.VMEM((4, fine, cols), F32),
        pltpu.VMEM((n_outer - 1, 4, fine, cols), F32),
        pltpu.VMEM((3, fine, cols), F32),
        pltpu.VMEM((n_dev, n_outer, sub, cols), BF16),
        pltpu.VMEM((n_outer, 2, sub, cols), F32),
        dma((4,)),
        dma((4,)),
        dma((4,)),
        dma((2, 3)),
        dma((2, 3)),
        dma,
        dma,
        dma((count,)),
        dma((count,)),
        dma((4,)),
        dma((4,)),
        pltpu.SemaphoreType.REGULAR((max(n_outer - 2, 1),)),
    ]


def plain_scratch(n_outer, n_dev, rows, cols, rank):
    blk = rank // n_dev
    per = n_dev // n_outer
    span = per * blk
    n_chip = n_dev // 2
    dma = pltpu.SemaphoreType.DMA
    return (
        [
            pltpu.VMEM((n_dev, rows, cols), BF16),
            pltpu.VMEM((rows, rank), BF16),
            pltpu.VMEM((rows, span), BF16),
            pltpu.VMEM((rows, cols), F32),
            pltpu.VMEM((2, per, blk, cols), F32),
            pltpu.VMEM((n_dev, blk, span), F32),
            pltpu.VMEM((n_chip, blk, span), F32),
            pltpu.VMEM((n_chip, blk, span), F32),
            pltpu.VMEM((n_chip, blk, span), F32),
            pltpu.VMEM((2, blk, cols), F32),
            pltpu.VMEM((n_outer, 2, blk, cols), F32),
            pltpu.VMEM((n_dev, blk, cols), F32),
            pltpu.VMEM((n_chip, blk, cols), F32),
            pltpu.VMEM((n_chip, blk, cols), F32),
            pltpu.VMEM((n_chip, blk, cols), F32),
            pltpu.VMEM((blk, cols), F32),
            pltpu.VMEM((n_outer, blk, cols), F32),
            pltpu.VMEM((n_dev, blk, cols), BF16),
            dma((6,)),
            dma((per,)),
            dma((chunks, n_dev)),
            dma((chunks, n_dev)),
            dma((2, per, n_chip)),
            dma((2, per)),
            dma((2, per)),
            dma((2, per)),
        ]
        + [dma((n_chip,))] * 4
        + [dma((n_outer,))] * 2
        + [dma((parts, n_chip))] * 4
        + [dma((parts, n_outer))] * 2
        + [dma((parts, n_dev))] * 2
    )


def hand_over(weight_in, m_in, v_in, weight_out, m_out, v_out):
    weight_out[...] = weight_in[...]
    m_out[...] = m_in[...]
    v_out[...] = v_in[...]


def on_device(n_outer, n_dev, partials, p_old, p_new, weight, m_old, v_old):
    rows, cols = weight.shape
    rank = p_new.shape[1]
    blk = rank // n_dev
    per = n_dev // n_outer
    span = per * blk
    n_chip = n_dev // 2
    squared = n_chip == 4 and n_dev % n_outer == 0 and n_outer % 2 == 0 and rows % 64 == 0 and blk % 128 == 0 and pieces == 2 and blk % (16 * pieces * n_outer) == 0
    if blk % 128 and not squared:
        z = lax.axis_index("outer")
        p_old = jnp.concatenate(
            [
                lax.dynamic_slice_in_dim(p_old, (k * n_outer + z) * blk, blk, axis=1)
                for k in range(per)
            ],
            axis=1,
        )
    anywhere = pl.BlockSpec(memory_space=pltpu.HBM)
    vmem = pl.BlockSpec(memory_space=pltpu.VMEM)
    if squared:
        body, scratch = square_kernel, square_scratch(n_outer, n_dev, rows, cols, rank)
    else:
        body, scratch = kernel, plain_scratch(n_outer, n_dev, rows, cols, rank)
    operands = (partials[0], p_old, p_new, weight, m_old, v_old)
    results = pl.pallas_call(
        functools.partial(body, n_outer, n_dev),
        out_shape=(
            jax.ShapeDtypeStruct((rows, cols), F32),
            jax.ShapeDtypeStruct((blk, cols), F32),
            jax.ShapeDtypeStruct((blk, cols), F32),
        ),
        in_specs=[anywhere] * 6,
        out_specs=(vmem, vmem, vmem),
        scratch_shapes=scratch,
        compiler_params=pltpu.CompilerParams(
            collective_id=0, has_side_effects=True, vmem_limit_bytes=vmem_limit
        ),
    )(*[pltpu.with_memory_space_constraint(a, pltpu.HBM) for a in operands])
    return pl.pallas_call(
        hand_over,
        out_shape=tuple(jax.ShapeDtypeStruct(r.shape, r.dtype) for r in results),
        in_specs=[vmem] * 3,
        out_specs=(vmem,) * 3,
        compiler_params=pltpu.CompilerParams(vmem_limit_bytes=finish_limit),
    )(*results)


def solution(mesh):
    in_specs = (
        P(("outer", "dev"), None, None),
        P("dev", None),
        P("dev", None),
        P("dev", None),
        P("dev", None),
        P("dev", None),
    )
    out_specs = (P("dev", None), P("dev", None), P("dev", None))
    return jax.shard_map(
        functools.partial(on_device, mesh.shape["outer"], mesh.shape["dev"]),
        mesh=mesh,
        in_specs=in_specs,
        out_specs=out_specs,
        check_vma=False,
    )
```

```python
import functools

import jax
import jax.numpy as jnp
from jax import lax
from jax.experimental import pallas as pl
from jax.experimental.pallas import tpu as pltpu
from jax.sharding import PartitionSpec as P

beta_mean = 0.9
beta_square = 0.95
bias_mean = 0.9999734386011124
bias_square = 0.9940794707796659
adam_epsilon = 1e-08
step_scale = 0.5

chunks = 2
early = 1
parts = 2
pieces = 2
shared_part = (7, 32)
vmem_limit = 50331648
finish_limit = 4194304

MESH = pl.DeviceIdType.MESH
F32 = jnp.float32
BF16 = jnp.bfloat16


def contract_rows(a, b):
    return lax.dot_general(a, b, (((0,), (0,)), ((), ())), preferred_element_type=F32)


def kernel(
    n_outer,
    n_dev,
    partials,
    p_old,
    p_new,
    weight,
    m_old,
    v_old,
    new_weight,
    m_new,
    v_new,
    grads,
    basis,
    basis_old,
    weights,
    moments,
    margin,
    margin_partner,
    margin_sum,
    margin_in,
    rotated,
    rotated_in,
    projected,
    projected_partner,
    projected_sum,
    projected_in,
    block,
    block_in,
    direction,
    load_sem,
    old_sem,
    grad_send,
    grad_recv,
    mom_send,
    mom_recv,
    fwd_send,
    fwd_recv,
    mp_send,
    mp_recv,
    ms_send,
    ms_recv,
    rot_send,
    rot_recv,
    pp_send,
    pp_recv,
    ps_send,
    ps_recv,
    blk_send,
    blk_recv,
    dir_send,
    dir_recv,
):
    z = lax.axis_index("outer")
    d = lax.axis_index("dev")
    n_chip = n_dev // 2
    q = d // 2
    c = d % 2
    partner = q * 2 + 1 - c
    rows, cols = weight.shape
    rank = p_new.shape[1]
    blk = rank // n_dev
    per = n_dev // n_outer

    def remote(src, dst, send, recv, where):
        return pltpu.make_async_remote_copy(
            src_ref=src, dst_ref=dst, send_sem=send, recv_sem=recv, device_id=where, device_id_type=MESH
        )

    barrier = pltpu.get_barrier_semaphore()
    for j in range(1, n_dev):
        pl.semaphore_signal(barrier, inc=1, device_id=(z, lax.rem(d + j, n_dev)), device_id_type=MESH)
    for j in range(1, n_outer):
        pl.semaphore_signal(barrier, inc=1, device_id=(lax.rem(z + j, n_outer), d), device_id_type=MESH)

    load_new = pltpu.make_async_copy(p_new, basis, load_sem.at[0])
    load_new.start()
    if p_old.shape[1] == per * blk:
        old_loads = [pltpu.make_async_copy(p_old, basis_old, old_sem.at[0])]
    else:
        old_loads = [
            pltpu.make_async_copy(
                p_old.at[:, pl.ds(pl.multiple_of((k * n_outer + z) * blk, blk), blk)],
                basis_old.at[:, k * blk : (k + 1) * blk],
                old_sem.at[k],
            )
            for k in range(per)
        ]
    for load in old_loads:
        load.start()
    load_weight = pltpu.make_async_copy(weight, weights, load_sem.at[2])
    load_weight.start()
    load_own = pltpu.make_async_copy(
        partials.at[pl.ds(pl.multiple_of(d * rows, rows), rows)], grads.at[0], load_sem.at[3]
    )
    load_own.start()

    pl.semaphore_wait(barrier, n_dev - 1 + n_outer - 1)

    def moment_copies(k, owner):
        copies = []
        for j in range(1, n_chip):
            to = (z, lax.rem(q + j, n_chip) * 2 + c)
            for i, src in enumerate((m_old, v_old)):
                copies.append(remote(src, moments.at[i, k], mom_send.at[i, k, j], mom_recv.at[i, k], to))
        return copies

    for k in range(per):
        owner = k * n_outer + z

        @pl.when(d == owner)
        def _():
            for copy in moment_copies(k, owner):
                copy.start()
            for i, src in enumerate((m_old, v_old)):
                pltpu.make_async_copy(src, moments.at[i, k], load_sem.at[4 + i]).start()

    tall = rows // chunks

    def send_gradients(chunk):
        copies = []
        for j in range(1, n_dev):
            to = lax.rem(d + j, n_dev)
            copy = remote(
                partials.at[pl.ds(pl.multiple_of(to * rows + chunk * tall, tall), tall)],
                grads.at[j, chunk * tall : (chunk + 1) * tall],
                grad_send.at[chunk, j],
                grad_recv.at[chunk, j],
                (z, to),
            )
            copy.start()
            copies.append(copy)
        return copies

    grad_copies = [send_gradients(chunk) for chunk in range(early)]

    load_new.wait()
    for load in old_loads:
        load.wait()
    width = min(rank, 256)
    for s in range(0, rank, width):
        part = contract_rows(basis[:, s : s + width], basis_old[...])
        margin[s // blk : (s + width) // blk] = part.reshape(width // blk, blk, part.shape[1])

    def scatter_start(val, prt, send, recv):
        copies = []
        for j in list(range(1, n_chip)) + [0]:
            k = lax.rem(q + j, n_chip)
            copy = remote(val.at[2 * k + 1 - c], prt.at[j], send.at[j], recv.at[j], (z, partner))
            copy.start()
            copies.append((j, k, copy))
        return copies

    def scatter_middle(pairs, val, prt, tot, arr, send, recv):
        copies = []
        for j, k, pair in pairs:
            pair.wait_recv()
            tot[j] = val[2 * k + c] + prt[j]
            if j:
                copy = remote(tot.at[j], arr.at[j], send.at[j], recv.at[j], (z, 2 * k + c))
                copy.start()
                copies.append((j, copy))
        return copies

    def scatter_end(copies, tot, arr):
        total = tot[0]
        for j, copy in copies:
            copy.wait_recv()
            total = total + arr[j]
        return total

    margin_pairs = scatter_start(margin, margin_partner, mp_send, mp_recv)

    for k in range(per):
        owner = k * n_outer + z
        mine = c == owner % 2

        @pl.when(d == owner)
        def _():
            for i, src in enumerate((m_old, v_old)):
                pltpu.make_async_copy(src, moments.at[i, k], load_sem.at[4 + i]).wait()

        @pl.when(jnp.logical_and(mine, d != owner))
        def _():
            for i, src in enumerate((m_old, v_old)):
                remote(src, moments.at[i, k], mom_send.at[i, k, 0], mom_recv.at[i, k], (z, d)).wait_recv()

        @pl.when(mine)
        def _():
            for i in range(2):
                remote(
                    moments.at[i, k], moments.at[i, k], fwd_send.at[i, k], fwd_recv.at[i, k], (z, partner)
                ).start()

    margin_copies = scatter_middle(
        margin_pairs, margin, margin_partner, margin_sum, margin_in, ms_send, ms_recv
    )

    for chunk in range(early, chunks):
        grad_copies.append(send_gradients(chunk))

    for k in range(per):
        mine = c == (k * n_outer + z) % 2

        @pl.when(jnp.logical_not(mine))
        def _():
            for i in range(2):
                remote(
                    moments.at[i, k], moments.at[i, k], fwd_send.at[i, k], fwd_recv.at[i, k], (z, partner)
                ).wait_recv()

    margin_rows = scatter_end(margin_copies, margin_sum, margin_in)
    old = moments[...].reshape(2, per * blk, cols)
    rotated[0] = jnp.dot(margin_rows, old[0], precision=lax.Precision.HIGHEST, preferred_element_type=F32)
    rotated[1] = jnp.dot(
        margin_rows * margin_rows, old[1], precision=lax.Precision.HIGHEST, preferred_element_type=F32
    )
    rot_copies = []
    for j in range(1, n_outer):
        copy = remote(
            rotated, rotated_in.at[j], rot_send.at[j], rot_recv.at[j], (lax.rem(z + j, n_outer), d)
        )
        copy.start()
        rot_copies.append(copy)

    load_own.wait()
    for chunk in range(chunks):
        for copy in grad_copies[chunk]:
            copy.wait_recv()
        part_rows = slice(chunk * tall, (chunk + 1) * tall)
        total = grads[0, part_rows].astype(F32)
        for j in range(1, n_dev):
            total = total + grads[j, part_rows].astype(F32)
        high = total.astype(BF16)
        low = (total - high.astype(F32)).astype(BF16)
        both = jnp.concatenate([high, low], axis=1)
        for s in range(0, rank, width):
            part = contract_rows(basis[part_rows, s : s + width], both)
            part = (part[:, :cols] + part[:, cols:]).reshape(width // blk, blk, cols)
            blocks = slice(s // blk, (s + width) // blk)
            projected[blocks] = part if chunk == 0 else projected[blocks] + part
    half = blk // parts
    views = [slice(h * half, (h + 1) * half) for h in range(parts)]
    pairs = [
        scatter_start(projected.at[:, v], projected_partner.at[:, v], pp_send.at[h], pp_recv.at[h])
        for h, v in enumerate(views)
    ]
    copies = [
        scatter_middle(
            pairs[h],
            projected.at[:, v],
            projected_partner.at[:, v],
            projected_sum.at[:, v],
            projected_in.at[:, v],
            ps_send.at[h],
            ps_recv.at[h],
        )
        for h, v in enumerate(views)
    ]
    blk_copies = []
    for h, v in enumerate(views):
        block[v] = scatter_end(copies[h], projected_sum.at[:, v], projected_in.at[:, v])
        for j in range(1, n_outer):
            copy = remote(
                block.at[v],
                block_in.at[j, v],
                blk_send.at[h, j],
                blk_recv.at[h, j],
                (lax.rem(z + j, n_outer), d),
            )
            copy.start()
            blk_copies.append(copy)
    for copy in rot_copies:
        copy.wait_recv()
    dir_copies = []
    for h, v in enumerate(views):
        for copy in blk_copies[h * (n_outer - 1) : (h + 1) * (n_outer - 1)]:
            copy.wait_recv()
        first = rotated[0, v]
        second = rotated[1, v]
        proj = block[v]
        for j in range(1, n_outer):
            first = first + rotated_in[j, 0, v]
            second = second + rotated_in[j, 1, v]
            proj = proj + block_in[j, v]
        mean = beta_mean * first + (1.0 - beta_mean) * proj
        square = beta_square * second + (1.0 - beta_square) * proj * proj
        m_new[v] = mean
        v_new[v] = square
        direction[d, v] = (mean / bias_mean / (jnp.sqrt(square / bias_square) + adam_epsilon)).astype(BF16)
        for j in range(1, n_dev):
            copy = remote(
                direction.at[d, v],
                direction.at[d, v],
                dir_send.at[h, j],
                dir_recv.at[h, j],
                (z, lax.rem(d + j, n_dev)),
            )
            copy.start()
            dir_copies.append(copy)
    load_weight.wait()
    for copy in dir_copies:
        copy.wait_recv()
    directions = direction[...].reshape(rank, cols)
    tall = min(rows, 256)
    for s in range(0, rows, tall):
        update = jnp.dot(basis[s : s + tall, :], directions, preferred_element_type=F32)
        new_weight[s : s + tall, :] = weights[s : s + tall, :] - step_scale * update

    for k in range(per):
        owner = k * n_outer + z
        mine = c == owner % 2

        @pl.when(d == owner)
        def _():
            for copy in moment_copies(k, owner):
                copy.wait_send()

        @pl.when(mine)
        def _():
            for i in range(2):
                remote(
                    moments.at[i, k], moments.at[i, k], fwd_send.at[i, k], fwd_recv.at[i, k], (z, partner)
                ).wait_send()

    for copy in sum(grad_copies, []) + rot_copies + blk_copies + dir_copies:
        copy.wait_send()
    for group in [margin_pairs] + pairs:
        for _, _, copy in group:
            copy.wait_send()
    for group in [margin_copies] + copies:
        for _, copy in group:
            copy.wait_send()

class Copies:
    def __init__(self, send, recv):
        self.send, self.recv, self.started = send, recv, []

    def start(self, src, dst, to):
        i = len(self.started)
        copy = pltpu.make_async_remote_copy(
            src_ref=src,
            dst_ref=dst,
            send_sem=self.send.at[i],
            recv_sem=self.recv.at[i],
            device_id=to,
            device_id_type=MESH,
        )
        copy.start()
        self.started.append(copy)
        return copy


def square_kernel(
    n_outer,
    n_dev,
    partials,
    p_old,
    p_new,
    weight,
    m_old,
    v_old,
    new_weight,
    m_new,
    v_new,
    own,
    pair,
    plane_own,
    plane_pair,
    far_sum,
    relay_in,
    direct_out,
    direct_in,
    merged,
    merged_in,
    terms,
    basis,
    basis_old,
    weights,
    moments,
    margin,
    margin_partner,
    margin_sum,
    margin_in,
    margin_relay,
    rotated,
    rotated_in,
    projected,
    projected_partner,
    projected_sum,
    projected_in,
    block,
    block_in,
    column,
    column_in,
    chip_in,
    direction,
    moments_new,
    load_sem,
    old_sem,
    own_sem,
    mom_send,
    mom_recv,
    fwd_send,
    fwd_recv,
    send_sem,
    recv_sem,
    merge_send,
    merge_recv,
    line_sem,
):
    z = lax.axis_index("outer")
    d = lax.axis_index("dev")
    q = d // 2
    c = d % 2
    partner = q * 2 + 1 - c
    side = q + 1 - 2 * (q % 2)
    over = lax.rem(q + 2, 4)
    far = lax.rem(side + 2, 4)
    chips = (far, side, over, q)
    rows, cols = weight.shape
    rank = p_new.shape[1]
    blk = rank // n_dev
    sub = blk // n_outer
    fine = sub // pieces
    few = shared_rows(rows)
    many = rows - 2 * few
    kept = few + many
    mate = z + 1 - 2 * (z % 2)
    odd = z % 2
    window = odd * few
    group_of = odd
    turn = z // 2
    few_at = odd * many
    many_at = few - window
    given_at = (1 - odd) * kept
    copies = Copies(send_sem, recv_sem)
    above = (2 * n_outer - 2 - z) // n_outer
    below = (z + n_outer - 1) // n_outer

    def signal_line(sem):
        @pl.when(z > 0)
        def _():
            pl.semaphore_signal(sem, inc=1, device_id=(z - 1, d), device_id_type=MESH)

        @pl.when(z < n_outer - 1)
        def _():
            pl.semaphore_signal(sem, inc=1, device_id=(z + 1, d), device_id_type=MESH)

    def pass_along(steps):
        for r in steps:
            pl.semaphore_wait(line_sem.at[r], above + below)
            if r + 1 < n_outer - 2:
                signal_line(line_sem.at[r + 1])

    barrier = pltpu.get_barrier_semaphore()
    for to in (partner, 2 * side + c, 2 * over + c):
        pl.semaphore_signal(barrier, inc=1, device_id=(z, to), device_id_type=MESH)
    pl.semaphore_signal(barrier, inc=1, device_id=(mate, partner), device_id_type=MESH)
    signal_line(barrier)

    def rows_of(to, start, count):
        return partials.at[pl.ds(pl.multiple_of(to * rows + start, 16), count)]

    own_loads = [
        pltpu.make_async_copy(rows_of(2 * k + c, window, kept), own.at[i], own_sem.at[i])
        for i, k in enumerate(chips)
    ]
    own_loads[0].start()
    pl.semaphore_wait(barrier, 4 + above + below)

    def moment_copy(i, j):
        return pltpu.make_async_remote_copy(
            src_ref=(m_old, v_old)[i],
            dst_ref=moments.at[i, q],
            send_sem=mom_send.at[i, j],
            recv_sem=mom_recv.at[i, j],
            device_id=(z, 2 * (side, over)[j] + c),
            device_id_type=MESH,
        )

    def moment_relay(i):
        came_from = (side, over)[i]
        return pltpu.make_async_remote_copy(
            src_ref=moments.at[i, came_from],
            dst_ref=moments.at[i, came_from],
            send_sem=mom_send.at[i, 2],
            recv_sem=mom_recv.at[i, 2],
            device_id=(z, 2 * (over, side)[i] + c),
            device_id_type=MESH,
        )

    def moment_load(i):
        return pltpu.make_async_copy((m_old, v_old)[i], moments.at[i, q], load_sem.at[2 + i])

    moment_forward = pltpu.make_async_remote_copy(
        src_ref=moments,
        dst_ref=moments,
        send_sem=fwd_send,
        recv_sem=fwd_recv,
        device_id=(z, partner),
        device_id_type=MESH,
    )

    def pair_start(i):
        own_rows = rows_of(2 * chips[i] + 1 - c, window, kept)
        return copies.start(own_rows, pair.at[i], (z, partner))

    def cross_start(i):
        return [
            copies.start(rows_of(2 * chips[i] + c, given_at, few), plane_own.at[i], (mate, d)),
            copies.start(rows_of(2 * chips[i] + 1 - c, given_at, few), plane_pair.at[i], (mate, partner)),
        ]

    pairs = [pair_start(0)]
    @pl.when(c == group_of)
    def _():
        for j in range(2):
            for i in range(2):
                moment_copy(i, j).start()
        for i in range(2):
            moment_load(i).start()

    crossed = [cross_start(0)]
    for i in (1, 2):
        own_loads[i].start()
        pairs.append(pair_start(i))
    arrived = set()

    def arrive(i, group):
        if i not in arrived:
            arrived.add(i)
            pairs[i].wait_recv()
            own_loads[i].wait()
        if group == 0:
            for copy in crossed[i]:
                copy.wait_recv()

    def rows_at(group, h):
        start, count = ((few_at, few // 2), (many_at, many // 2))[group]
        return pl.ds(pl.multiple_of(start + h * count, 16), count)

    def chip_sum(i, h):
        at = rows_at(1, h)
        return own[i, at].astype(F32) + pair[i, at].astype(F32)

    def plane_sum(i, h):
        at, near = rows_at(0, h), slice(h * few // 2, (h + 1) * few // 2)
        total = own[i, at].astype(F32) + pair[i, at].astype(F32)
        return total + (plane_own[i, near].astype(F32) + plane_pair[i, near].astype(F32))

    sums = (plane_sum, chip_sum)
    merging = Copies(merge_send, merge_recv)
    relays, directs, merges = {}, {}, {}

    def send_far(group):
        arrive(0, group)
        for h, chip in enumerate((side, over)):
            at = rows_at(group, h)
            far_sum[at] = sums[group](0, h).astype(BF16)
            relays[group, h] = copies.start(far_sum.at[at], relay_in.at[at], (z, 2 * chip + c))

    def send_direct(group):
        for h, chip in enumerate((side, over)):
            arrive(1 + h, group)
            at = rows_at(group, h)
            direct_out[at] = sums[group](1 + h, h).astype(BF16)
            directs[group, h] = copies.start(direct_out.at[at], direct_in.at[at], (z, 2 * chip + c))

    def send_merged(group):
        for h, (i, chip) in enumerate(((2, over), (1, side))):
            at = rows_at(group, h)
            relays[group, h].wait_recv()
            merged[at] = sums[group](i, h) + relay_in[at].astype(F32)
            merges[group, h] = merging.start(merged.at[at], merged_in.at[at], (z, 2 * chip + c))

    send_far(1)
    crossed += [cross_start(1), cross_start(2)]
    send_direct(1)
    load_new = pltpu.make_async_copy(p_new, basis, load_sem.at[0])
    load_new.start()
    old_loads = [
        pltpu.make_async_copy(
            p_old.at[:, pl.ds(pl.multiple_of((2 * k + group_of) * blk, blk), blk)],
            basis_old.at[:, k * blk : (k + 1) * blk],
            old_sem.at[k],
        )
        for k in range(4)
    ]
    for load in old_loads:
        load.start()
    own_loads[3].start()
    load_weight = pltpu.make_async_copy(weight, weights, load_sem.at[1])
    load_weight.start()
    pairs.append(pair_start(3))
    crossed.append(cross_start(3))
    if n_outer > 2:
        signal_line(line_sem.at[0])

    send_far(0)
    send_merged(1)
    load_new.wait()
    for load in old_loads:
        load.wait()

    def chip_ranks(k):
        return pl.ds(pl.multiple_of(k * 2 * blk, 2 * blk), 2 * blk)

    for i, k in enumerate(chips):
        part = contract_rows(basis[:, chip_ranks(k)], basis_old[...])
        margin[:, i] = part.reshape(2, n_outer // 2, 2, sub, 4 * blk)
    margin_pair = copies.start(margin.at[1 - c, :, turn], margin_partner, (z, partner))

    margin_pair.wait_recv()
    margin_sum[...] = margin[c, :, turn] + margin_partner[...]

    @pl.when(c == group_of)
    def _():
        for i in range(2):
            moment_copy(i, i).wait_recv()
            moment_relay(i).start()

    send_direct(0)
    send_merged(0)
    for copy in merging.started:
        copy.wait_send()
    margin_relays = [
        copies.start(margin_sum.at[0, h], margin_relay.at[h], (z, 2 * chip + c))
        for h, chip in enumerate((side, over))
    ]
    margin_copies = [
        copies.start(margin_sum.at[1 + h, h], margin_in.at[0, h], (z, 2 * chip + c))
        for h, chip in enumerate((side, over))
    ]

    for group in (1, 0):
        arrive(3, group)
        for h in range(2):
            at = rows_at(group, h)
            directs[group, h].wait_recv()
            total = sums[group](3, h) + direct_in[at].astype(F32)
            merges[group, h].wait_recv()
            total = total + merged_in[at]
            high = total.astype(BF16)
            terms[at, :cols] = high
            terms[at, cols:] = (total - high.astype(F32)).astype(BF16)

    for i, k in enumerate(chips):
        kept_rows = pl.ds(pl.multiple_of(window, 16), kept)
        part = contract_rows(basis[kept_rows, chip_ranks(k)], terms[...])
        part = (part[:, :cols] + part[:, cols:]).reshape(2, n_outer, pieces, fine, cols)
        for h in range(pieces):
            projected[h, :, i] = part[:, :, h]
    projected_pairs = [
        copies.start(projected.at[h, 1 - c], projected_partner.at[h], (z, partner)) for h in (1, 0)
    ][::-1]
    for h, (i, chip) in enumerate(((2, over), (1, side))):
        margin_relays[h].wait_recv()
        margin_sum[i, h] = margin_sum[i, h] + margin_relay[h]
        margin_copies.append(copies.start(margin_sum.at[i, h], margin_in.at[1, h], (z, 2 * chip + c)))

    planes = [lax.rem(z + j, n_outer) for j in range(1, n_outer)]
    pass_along(range(n_outer - 2))
    projected_pairs[1].wait_recv()
    projected_sum[1] = projected[1, c] + projected_partner[1]
    column_copies = [
        copies.start(projected_sum.at[1, :, to], column_in.at[j], (to, d)) for j, to in enumerate(planes)
    ]

    projected_pairs[0].wait_recv()
    projected_copies = []
    for i, k in enumerate(chips):
        projected_sum[0, i] = projected[0, c, i] + projected_partner[0, i]
        if i < 3:
            projected_copies.append(
                copies.start(projected_sum.at[0, i], projected_in.at[i], (z, 2 * k + c))
            )
    @pl.when(c == group_of)
    def _():
        for i in range(2):
            moment_load(i).wait()
            moment_copy(i, 1 - i).wait_recv()
            moment_relay(i).wait_recv()
        moment_forward.start()

    @pl.when(c != group_of)
    def _():
        moment_forward.wait_recv()

    for copy in projected_copies:
        copy.wait_recv()
    block[...] = projected_sum[0, 3] + projected_in[0] + projected_in[1] + projected_in[2]
    block_copies = [copies.start(block.at[to], block_in.at[j], (to, d)) for j, to in enumerate(planes)]
    for copy in margin_copies:
        copy.wait_recv()
    margin_rows = margin_sum[3] + margin_in[0] + margin_in[1]
    margin_rows = margin_rows.reshape(2 * sub, 4 * blk)
    old = moments[...].reshape(2, 4 * blk, cols)
    for i, rows_in in enumerate((margin_rows, margin_rows * margin_rows)):
        turned = jnp.dot(rows_in, old[i], precision=lax.Precision.HIGHEST, preferred_element_type=F32)
        rotated[:, i] = turned.reshape(2, sub, cols)
    rot_copy = copies.start(rotated.at[1 - group_of], rotated_in, (mate, d))

    for copy in column_copies:
        copy.wait_recv()
    for i in range(4):
        total = projected_sum[1, i, z]
        for j in range(n_outer - 1):
            total = total + column_in[j, i]
        column[i] = total
    chip_copies = [
        copies.start(column.at[i], chip_in.at[i], (z, 2 * k + c)) for i, k in enumerate(chips[:3])
    ]

    rot_copy.wait_recv()
    first = rotated[group_of, 0] + rotated_in[0]
    second = rotated[group_of, 1] + rotated_in[1]
    for h in range(pieces):
        at = slice(h * fine, (h + 1) * fine)
        if h == 0:
            proj = block[z]
            for j, copy in enumerate(block_copies):
                copy.wait_recv()
                proj = proj + block_in[j]
        else:
            proj = column[3]
            for i, copy in enumerate(chip_copies):
                copy.wait_recv()
                proj = proj + chip_in[i]
        mean = beta_mean * first[at] + (1.0 - beta_mean) * proj
        square = beta_square * second[at] + (1.0 - beta_square) * proj * proj
        moments_new[z, 0, at] = mean
        moments_new[z, 1, at] = square
        direction[d, z, at] = (
            mean / bias_mean / (jnp.sqrt(square / bias_square) + adam_epsilon)
        ).astype(BF16)

    settled = len(copies.started)
    spread = []
    spread = [[], [], [], []]
    for to in [planes[0], planes[2], planes[1], z]:
        for i, k in enumerate(chips):
            if i < 3 or to is not z:
                spread[i].append(copies.start(direction.at[d, z], direction.at[d, z], (to, 2 * k + c)))
    moment_spread = [copies.start(moments_new.at[z], moments_new.at[z], (to, d)) for to in planes]
    for copy in copies.started[:settled]:
        copy.wait_send()

    @pl.when(c == group_of)
    def _():
        for i in range(2):
            for j in range(2):
                moment_copy(i, j).wait_send()
            moment_relay(i).wait_send()
        moment_forward.wait_send()

    forwards = []
    for i in (3, 1, 2, 0):
        for copy in spread[i]:
            copy.wait_recv()
        mine = direction.at[2 * chips[i] + c]
        forwards.append(copies.start(mine, mine, (z, partner)))
    load_weight.wait()
    for copy in sum(spread, moment_spread):
        copy.wait_send()
    for copy in forwards:
        copy.wait_recv()
    directions = direction[...].reshape(rank, cols)
    tall = min(rows, 256)
    for s in range(0, rows, tall):
        update = jnp.dot(basis[s : s + tall, :], directions, preferred_element_type=F32)
        new_weight[s : s + tall, :] = weights[s : s + tall, :] - step_scale * update
    for copy in moment_spread:
        copy.wait_recv()
    m_new[...] = moments_new[:, 0].reshape(blk, cols)
    v_new[...] = moments_new[:, 1].reshape(blk, cols)

    for copy in forwards:
        copy.wait_send()


def shared_rows(rows):
    top, bottom = shared_part
    return rows * top // bottom // 32 * 32


def square_scratch(n_outer, n_dev, rows, cols, rank):
    blk = rank // n_dev
    sub = blk // n_outer
    fine = sub // pieces
    span = 4 * blk
    dma = pltpu.SemaphoreType.DMA
    few = shared_rows(rows)
    kept = rows - few
    count = 50 + 15 * pieces + 6 * n_outer
    return [
        pltpu.VMEM((4, kept, cols), BF16),
        pltpu.VMEM((4, kept, cols), BF16),
        pltpu.VMEM((4, few, cols), BF16),
        pltpu.VMEM((4, few, cols), BF16),
        pltpu.VMEM((kept, cols), BF16),
        pltpu.VMEM((kept, cols), BF16),
        pltpu.VMEM((kept, cols), BF16),
        pltpu.VMEM((kept, cols), BF16),
        pltpu.VMEM((kept, cols), F32),
        pltpu.VMEM((kept, cols), F32),
        pltpu.VMEM((kept, 2 * cols), BF16),
        pltpu.VMEM((rows, rank), BF16),
        pltpu.VMEM((rows, span), BF16),
        pltpu.VMEM((rows, cols), F32),
        pltpu.VMEM((2, 4, blk, cols), F32),
        pltpu.VMEM((2, 4, n_outer // 2, 2, sub, span), F32),
        pltpu.VMEM((4, 2, sub, span), F32),
        pltpu.VMEM((4, 2, sub, span), F32),
        pltpu.VMEM((2, 2, sub, span), F32),
        pltpu.VMEM((2, sub, span), F32),
        pltpu.VMEM((2, 2, sub, cols), F32),
        pltpu.VMEM((2, sub, cols), F32),
        pltpu.VMEM((pieces, 2, 4, n_outer, fine, cols), F32),
        pltpu.VMEM((pieces, 4, n_outer, fine, cols), F32),
        pltpu.VMEM((pieces, 4, n_outer, fine, cols), F32),
        pltpu.VMEM((3, n_outer, fine, cols), F32),
        pltpu.VMEM((n_outer, fine, cols), F32),
        pltpu.VMEM((n_outer - 1, fine, cols), F32),
        pltpu.VMEM((4, fine, cols), F32),
        pltpu.VMEM((n_outer - 1, 4, fine, cols), F32),
        pltpu.VMEM((3, fine, cols), F32),
        pltpu.VMEM((n_dev, n_outer, sub, cols), BF16),
        pltpu.VMEM((n_outer, 2, sub, cols), F32),
        dma((4,)),
        dma((4,)),
        dma((4,)),
        dma((2, 3)),
        dma((2, 3)),
        dma,
        dma,
        dma((count,)),
        dma((count,)),
        dma((4,)),
        dma((4,)),
        pltpu.SemaphoreType.REGULAR((max(n_outer - 2, 1),)),
    ]


def plain_scratch(n_outer, n_dev, rows, cols, rank):
    blk = rank // n_dev
    per = n_dev // n_outer
    span = per * blk
    n_chip = n_dev // 2
    dma = pltpu.SemaphoreType.DMA
    return (
        [
            pltpu.VMEM((n_dev, rows, cols), BF16),
            pltpu.VMEM((rows, rank), BF16),
            pltpu.VMEM((rows, span), BF16),
            pltpu.VMEM((rows, cols), F32),
            pltpu.VMEM((2, per, blk, cols), F32),
            pltpu.VMEM((n_dev, blk, span), F32),
            pltpu.VMEM((n_chip, blk, span), F32),
            pltpu.VMEM((n_chip, blk, span), F32),
            pltpu.VMEM((n_chip, blk, span), F32),
            pltpu.VMEM((2, blk, cols), F32),
            pltpu.VMEM((n_outer, 2, blk, cols), F32),
            pltpu.VMEM((n_dev, blk, cols), F32),
            pltpu.VMEM((n_chip, blk, cols), F32),
            pltpu.VMEM((n_chip, blk, cols), F32),
            pltpu.VMEM((n_chip, blk, cols), F32),
            pltpu.VMEM((blk, cols), F32),
            pltpu.VMEM((n_outer, blk, cols), F32),
            pltpu.VMEM((n_dev, blk, cols), BF16),
            dma((6,)),
            dma((per,)),
            dma((chunks, n_dev)),
            dma((chunks, n_dev)),
            dma((2, per, n_chip)),
            dma((2, per)),
            dma((2, per)),
            dma((2, per)),
        ]
        + [dma((n_chip,))] * 4
        + [dma((n_outer,))] * 2
        + [dma((parts, n_chip))] * 4
        + [dma((parts, n_outer))] * 2
        + [dma((parts, n_dev))] * 2
    )


def hand_over(weight_in, m_in, v_in, weight_out, m_out, v_out):
    weight_out[...] = weight_in[...]
    m_out[...] = m_in[...]
    v_out[...] = v_in[...]


def on_device(n_outer, n_dev, partials, p_old, p_new, weight, m_old, v_old):
    rows, cols = weight.shape
    rank = p_new.shape[1]
    blk = rank // n_dev
    per = n_dev // n_outer
    span = per * blk
    n_chip = n_dev // 2
    squared = n_chip == 4 and n_dev % n_outer == 0 and n_outer % 2 == 0 and rows % 64 == 0 and blk % 128 == 0 and pieces == 2 and blk % (16 * pieces * n_outer) == 0
    if blk % 128 and not squared:
        z = lax.axis_index("outer")
        p_old = jnp.concatenate(
            [
                lax.dynamic_slice_in_dim(p_old, (k * n_outer + z) * blk, blk, axis=1)
                for k in range(per)
            ],
            axis=1,
        )
    anywhere = pl.BlockSpec(memory_space=pltpu.HBM)
    vmem = pl.BlockSpec(memory_space=pltpu.VMEM)
    if squared:
        body, scratch = square_kernel, square_scratch(n_outer, n_dev, rows, cols, rank)
    else:
        body, scratch = kernel, plain_scratch(n_outer, n_dev, rows, cols, rank)
    operands = (partials[0], p_old, p_new, weight, m_old, v_old)
    results = pl.pallas_call(
        functools.partial(body, n_outer, n_dev),
        out_shape=(
            jax.ShapeDtypeStruct((rows, cols), F32),
            jax.ShapeDtypeStruct((blk, cols), F32),
            jax.ShapeDtypeStruct((blk, cols), F32),
        ),
        in_specs=[anywhere] * 6,
        out_specs=(vmem, vmem, vmem),
        scratch_shapes=scratch,
        compiler_params=pltpu.CompilerParams(
            collective_id=0, has_side_effects=True, vmem_limit_bytes=vmem_limit
        ),
    )(*[pltpu.with_memory_space_constraint(a, pltpu.HBM) for a in operands])
    return pl.pallas_call(
        hand_over,
        out_shape=tuple(jax.ShapeDtypeStruct(r.shape, r.dtype) for r in results),
        in_specs=[vmem] * 3,
        out_specs=(vmem,) * 3,
        compiler_params=pltpu.CompilerParams(vmem_limit_bytes=finish_limit),
    )(*results)


def solution(mesh):
    in_specs = (
        P(("outer", "dev"), None, None),
        P("dev", None),
        P("dev", None),
        P("dev", None),
        P("dev", None),
        P("dev", None),
    )
    out_specs = (P("dev", None), P("dev", None), P("dev", None))
    return jax.shard_map(
        functools.partial(on_device, mesh.shape["outer"], mesh.shape["dev"]),
        mesh=mesh,
        in_specs=in_specs,
        out_specs=out_specs,
        check_vma=False,
    )
```
